512 devices in a mesh: pipe: 8 (over z), expert: 64 (over x, y, core).
Axes of the slice: x: 4, y: 8, z: 8, core: 2. Of those that a mesh axis runs over, the one named last changes fastest.
Arguments:
- tokens: bfloat16 [2, 2048, 3584], P(None, ('pipe', 'expert')), may hold values from -6 to 6
- cotangent: bfloat16 [2, 2048, 3584], P(None, ('pipe', 'expert')), may hold values from -6 to 6
- expert_ids: int32 [2, 2048, 2], P(None, ('pipe', 'expert')), may hold values from 0 to 3, all different within a row; in each aligned block of 4 rows (0 to 3, 4 to 7, ..., all dimensions but the last counted through in order) at most 3 rows name the same one
- gate_values: bfloat16 [2, 2048, 2], P(None, ('pipe', 'expert')), may hold values from 0.19921875 to 1.5
- w_gate: bfloat16 [3584, 8192], P('pipe', 'expert'), may hold values from -0.09375 to 0.09375
- w_up: bfloat16 [3584, 8192], P('pipe', 'expert'), may hold values from -0.09375 to 0.09375
- w_down_t: bfloat16 [3584, 8192], P('pipe', 'expert'), may hold values from -0.125 to 0.125
Outputs:
- d_tokens: bfloat16 [2, 2048, 3584], P(None, ('pipe', 'expert'))
- gate_weight_gradient: float32 [2, 2048, 2], P(None, ('pipe', 'expert'))
- dw_gate: bfloat16 [3584, 8192], P('pipe', 'expert')
- dw_up: bfloat16 [3584, 8192], P('pipe', 'expert')
- dw_down_t: bfloat16 [3584, 8192], P('pipe', 'expert')
The draws below stay inside these ranges and needn't reach their ends.
Inputs may be any that keep to these rules, and one draw needn't show every extreme that they name: `expert_ids`: within each micro-batch, the 4 tokens of one device route to one expert at most 3 times; a token's 2 experts differ.
All inputs are finite; a program needn't handle non-finite values.
Results may differ from the reference program's by a relative error of at most 0.014.
Values may be sent and summed in bfloat16 or wider, within the bound.
A program may use at most 64 MiB of HBM per device.

```python
import math
import jax
import jax.numpy as jnp
import numpy as np
from jax import lax

D = 3584
F = 2048
EXPERTS = 4
TOP = 2
MB = 2
TOK_MB = 4
CAP = 3
TOKENS = 2048
N_PIPE = 8
N_EXPERT = 64


def shard_levels(key, extent, pieces, low, top_value):
    level, own = 1.0, jax.random.fold_in(key, 6)
    for axis_at, shards_of in pieces:
        draws = jnp.exp(jax.random.uniform(jax.random.fold_in(own, axis_at), (shards_of,), jnp.float32, low / len(pieces), top_value / len(pieces)))
        level = level * jnp.repeat(draws, extent[axis_at] // shards_of).reshape([-1 if axis == axis_at else 1 for axis in range(len(extent))])
    return level


def assign_block(key, own, number, rows, count, top, reach, lean):
    ranking = jax.random.permutation(key, count)
    heavy_load, ordinary = shares(count, rows * top, reach, lean, True), shares(count, rows * top, reach, lean, False)
    places = jnp.arange(count)

    def named(sizes, turn):
        used = int((sizes > 0).sum())
        fixed = max(1, used // 4)
        passed = fixed + (places - fixed + turn * (used - fixed)) % max(1, count - fixed)
        return jnp.zeros((count,), jnp.int32).at[ranking[jnp.where(places < fixed, places, passed)]].set(jnp.asarray(sizes, jnp.int32))

    sizes = jnp.where(number % 4 == 0, named(heavy_load, number // 4), named(ordinary, number - number // 4 - 1))
    mixed = jax.random.permutation(jax.random.fold_in(own, 3), count)
    donor, sink = mixed[0:count // 2 * 2:2], mixed[1:count // 2 * 2:2]
    room = jnp.minimum(sizes[donor] - 1, reach - sizes[sink]) // 2
    room = jnp.where((donor == ranking[0]) | (sink == ranking[0]) | (sizes[sink] == 0), 0, jnp.maximum(room, 0))
    passed = jax.random.randint(jax.random.fold_in(own, 4), (count // 2,), 0, 1 << 20) % (room + 1)
    sizes = sizes.at[donor].add(-passed).at[sink].add(passed)
    items = jnp.searchsorted(jnp.cumsum(sizes), jnp.arange(rows * top), side="right").astype(jnp.int32)
    listing = items.reshape(top, rows).T
    listing = listing[jax.random.permutation(jax.random.fold_in(own, 1), rows)]
    turn = jax.random.randint(jax.random.fold_in(own, 2), (rows, 1), 0, top)
    return jnp.take_along_axis(listing, (jnp.arange(top)[None, :] + turn) % top, axis=1)


def shares(number_of, total, reach, lean, full):
    loads = [(1 << 20) // math.isqrt(rank ** lean) + 1 for rank in range(1, number_of + 1)]
    largest = reach if full else min(reach, max(-(-total // number_of), total * loads[0] // sum(loads)))
    least = 1 if total - largest >= number_of - 1 else 0
    holding, rest = [largest] + [least] * (number_of - 1), total - largest - least * (number_of - 1)
    while rest > 0:
        candidates = [i for i in range(1, number_of) if holding[i] < largest] or [i for i in range(1, number_of) if holding[i] < reach]
        pool, left = sum([loads[i] for i in candidates]), rest
        for i in candidates:
            addition = min(reach - holding[i], max(1, left * loads[i] // pool), rest)
            holding[i] = holding[i] + addition
            rest = rest - addition
    return np.array(holding)


def gaussian(key, dims, width, most, cuts=(), kind=jnp.bfloat16):
    drawn = width * jax.random.normal(key, dims, jnp.float32)
    if cuts:
        drawn = drawn * shard_levels(key, dims, cuts, -0.22, 0.18)
    return jnp.clip(drawn, -most, most).astype(kind)


def setup_inputs(seed: int = 0) -> dict:
    keys = jax.random.split(jax.random.key(seed), 8)
    tokens = gaussian(keys[0], (MB, TOKENS, D), 1.0, 6.0, ((1, 512),))
    cotangent = gaussian(keys[1], (MB, TOKENS, D), 1.0, 6.0, ((1, 512),))
    expert_ids_keys = jax.random.split(jax.random.fold_in(keys[2], 1), MB * TOKENS // TOK_MB)
    expert_ids_turns = jax.random.permutation(jax.random.fold_in(keys[2], 3), MB * TOKENS // TOK_MB)
    expert_ids = jax.vmap(lambda own, number: assign_block(jax.random.fold_in(keys[2], 2), own, number, TOK_MB, EXPERTS, TOP, CAP, 2))(expert_ids_keys, expert_ids_turns).reshape((MB, TOKENS, TOP))
    gate_values = jnp.clip(0.19921875 + 1.3007812 * jax.random.uniform(keys[3], (MB, TOKENS, TOP), jnp.float32) ** shard_levels(keys[3], (MB, TOKENS, TOP), ((1, 512),), -0.2, 0.2), 0.19921875, 1.5).astype(jnp.bfloat16)
    w_gate = gaussian(keys[4], (D, EXPERTS * F), D ** -0.5, 0.09375, ((0, 8), (1, 64)))
    w_up = gaussian(keys[5], (D, EXPERTS * F), D ** -0.5, 0.09375, ((0, 8), (1, 64)))
    w_down_t = gaussian(keys[6], (D, EXPERTS * F), F ** -0.5, 0.125, ((0, 8), (1, 64)))
    return {"tokens": tokens, "cotangent": cotangent, "expert_ids": expert_ids, "gate_values": gate_values, "w_gate": w_gate, "w_up": w_up, "w_down_t": w_down_t}


def reference(tokens, cotangent, expert_ids, gate_values, w_gate, w_up, w_down_t):
    devices = N_PIPE * N_EXPERT
    routes = TOK_MB * TOP
    ids = expert_ids.reshape(MB, devices, routes).astype(jnp.int32)
    onehot = (ids[..., None] == jnp.arange(EXPERTS, dtype=jnp.int32)).astype(jnp.int32)
    earlier = jnp.cumsum(onehot, axis=2) - onehot
    position = lax.optimization_barrier(jnp.sum(earlier * onehot, axis=3)).astype(jnp.int32)
    micro_index = jnp.broadcast_to(jnp.arange(MB, dtype=jnp.int32)[:, None, None], ids.shape)
    device_index = jnp.broadcast_to(jnp.arange(devices, dtype=jnp.int32)[None, :, None], ids.shape)
    route_index = jnp.broadcast_to(jnp.arange(routes, dtype=jnp.int32)[None, None, :], ids.shape)
    token_flat = micro_index * TOKENS + device_index * TOK_MB + route_index // TOP
    route_flat = token_flat * TOP + route_index % TOP
    empty_slots = jnp.full((MB, devices, EXPERTS, CAP), -1, jnp.int32)
    token_slot = empty_slots.at[micro_index, device_index, ids, position].set(token_flat)
    route_slot = empty_slots.at[micro_index, device_index, ids, position].set(route_flat)
    tok_flat = tokens.reshape(MB * TOKENS, D)
    cot_flat = cotangent.reshape(MB * TOKENS, D)
    flattened_gate = gate_values.reshape(MB * TOKENS * TOP)
    scale = 1.0 / math.sqrt(MB * TOKENS * TOP / EXPERTS)
    highest_precision = lax.Precision.HIGHEST

    def pipe_sum(left_rows, right_rows):
        left_part = left_rows.reshape(MB, N_PIPE, N_EXPERT * CAP, D).astype(jnp.float32)
        right_part = right_rows.reshape(MB, N_PIPE, N_EXPERT * CAP, F).astype(jnp.float32)
        term = jnp.einsum('mprd,mprf->pdf', left_part, right_part, precision=highest_precision) * scale
        return lax.optimization_barrier(jnp.sum(term.astype(jnp.bfloat16).astype(jnp.float32), axis=0)).astype(jnp.bfloat16)

    def one_expert(carry, expert):
        dx_acc, gate_acc = carry
        tok_slot_e = jnp.take(token_slot, expert, axis=2).reshape(-1)
        route_slot_e = jnp.take(route_slot, expert, axis=2).reshape(-1)
        live = tok_slot_e >= 0
        safe_tok = jnp.where(live, tok_slot_e, 0).astype(jnp.int32)
        safe_route = jnp.where(live, route_slot_e, 0).astype(jnp.int32)
        live_bf = live.astype(jnp.bfloat16)[:, None]
        tok_rows = tok_flat[safe_tok] * live_bf
        cot_rows = cot_flat[safe_tok] * live_bf
        gate_rows = (flattened_gate[safe_route] * live_bf[:, 0]).astype(jnp.float32)[:, None]
        start = (expert * F).astype(jnp.int32)
        gate_cols = lax.dynamic_slice_in_dim(w_gate, start, F, 1)
        up_cols = lax.dynamic_slice_in_dim(w_up, start, F, 1)
        down_cols = lax.dynamic_slice_in_dim(w_down_t, start, F, 1)
        pre_gate = jnp.dot(tok_rows, gate_cols, preferred_element_type=jnp.float32)
        pre_up = jnp.dot(tok_rows, up_cols, preferred_element_type=jnp.float32)
        back_proj = jnp.dot(cot_rows, down_cols, preferred_element_type=jnp.float32)
        sigmoid_gate = jax.nn.sigmoid(pre_gate)
        activated = pre_gate * sigmoid_gate
        hidden = activated * pre_up
        gate_part = lax.optimization_barrier(jnp.sum(back_proj * hidden, axis=1))
        scaled_hidden = (gate_rows * hidden).astype(jnp.bfloat16)
        d_hidden = gate_rows * back_proj
        d_pre_gate = (d_hidden * pre_up * sigmoid_gate * (1.0 + pre_gate * (1.0 - sigmoid_gate))).astype(jnp.bfloat16)
        d_pre_up = (d_hidden * activated).astype(jnp.bfloat16)
        input_grad = jnp.dot(d_pre_gate, gate_cols.T, preferred_element_type=jnp.float32)
        input_grad = input_grad + jnp.dot(d_pre_up, up_cols.T, preferred_element_type=jnp.float32)
        dx_acc = dx_acc.at[safe_tok].add(input_grad)
        gate_acc = gate_acc.at[safe_route].add(gate_part)
        grad_gate = pipe_sum(tok_rows, d_pre_gate)
        grad_up = pipe_sum(tok_rows, d_pre_up)
        grad_down = pipe_sum(cot_rows, scaled_hidden)
        return ((dx_acc, gate_acc), (grad_gate, grad_up, grad_down))
    init = (jnp.zeros((MB * TOKENS, D), jnp.float32), jnp.zeros((MB * TOKENS * TOP,), jnp.float32))
    (dx_acc, gate_acc), grads = lax.scan(one_expert, init, jnp.arange(EXPERTS, dtype=jnp.int32))

    def columns(stacked):
        return jnp.transpose(stacked, (1, 0, 2)).reshape(D, EXPERTS * F)
    d_tokens = dx_acc.reshape(MB, TOKENS, D).astype(jnp.bfloat16)
    gate_weight_gradient = gate_acc.reshape(MB, TOKENS, TOP)
    return (d_tokens, gate_weight_gradient, columns(grads[0]), columns(grads[1]), columns(grads[2]))
```

```python
import math

import jax
import jax.numpy as jnp
from jax import lax
from jax.sharding import PartitionSpec as P

EXPERTS = 4
CAP = 3


def route_table(expert_ids, expert_total, capacity):
    micro_count, tok_count, top_count = expert_ids.shape
    flat_ids = expert_ids.reshape(micro_count, tok_count * top_count)
    onehot = (
        flat_ids[:, :, None] == jnp.arange(expert_total, dtype=jnp.int32)[None, None, :]
    ).astype(jnp.int32)
    earlier = jnp.cumsum(onehot, axis=1) - onehot
    position = jnp.sum(earlier * onehot, axis=2)
    slot_index = flat_ids * capacity + position
    slot_ids = jnp.arange(expert_total * capacity, dtype=jnp.int32)
    return (slot_index[:, None, :] == slot_ids[None, :, None]).astype(jnp.float32)


def on_device(tokens, cotangent, expert_ids, gate_values, w_gate, w_up, w_down_t):
    micro_count, tok_count, d_model = tokens.shape
    top_count = expert_ids.shape[2]
    pipe_size = lax.axis_size("pipe")
    expert_size = lax.axis_size("expert")
    group_size = expert_size // EXPERTS
    capacity = CAP
    slot_total = EXPERTS * capacity
    highest_precision = lax.Precision.HIGHEST
    cols = w_gate.shape[1]
    w_full = lax.all_gather(
        jnp.concatenate([w_gate, w_up, w_down_t], axis=1), "pipe", axis=0, tiled=True
    )
    gate_full = w_full[:, :cols]
    up_full = w_full[:, cols : 2 * cols]
    down_full = w_full[:, 2 * cols :]
    routing_table = route_table(expert_ids, EXPERTS, capacity)
    routing_table_bfloat16 = routing_table.astype(jnp.bfloat16)
    token_replica = jnp.repeat(tokens, top_count, axis=1)
    cotangent_replica = jnp.repeat(cotangent, top_count, axis=1)
    flattened_gate = gate_values.reshape(micro_count, tok_count * top_count)
    send_tok = jnp.einsum(
        "egf,efh->egh", routing_table_bfloat16, token_replica, preferred_element_type=jnp.float32
    ).astype(jnp.bfloat16)
    send_cot = jnp.einsum(
        "egf,efh->egh",
        routing_table_bfloat16,
        cotangent_replica,
        preferred_element_type=jnp.float32,
    ).astype(jnp.bfloat16)
    send_gate = jnp.einsum(
        "wkx,wx->wk", routing_table_bfloat16, flattened_gate, preferred_element_type=jnp.float32
    ).astype(jnp.bfloat16)
    send_tok = send_tok.reshape(micro_count, EXPERTS, capacity, d_model)
    send_cot = send_cot.reshape(micro_count, EXPERTS, capacity, d_model)
    gate_blocks = jnp.broadcast_to(
        send_gate.reshape(micro_count, EXPERTS, 1, capacity),
        (micro_count, EXPERTS, group_size, capacity),
    ).reshape(micro_count, expert_size, capacity)
    tok_blocks = jnp.broadcast_to(
        send_tok[:, :, None], (micro_count, EXPERTS, group_size, capacity, d_model)
    ).reshape(micro_count, expert_size, capacity, d_model)
    cot_blocks = jnp.broadcast_to(
        send_cot[:, :, None], (micro_count, EXPERTS, group_size, capacity, d_model)
    ).reshape(micro_count, expert_size, capacity, d_model)
    recv_tok, recv_cot, recv_gate = (
        lax.all_to_all(tok_blocks, "expert", split_axis=1, concat_axis=1, tiled=True),
        lax.all_to_all(cot_blocks, "expert", split_axis=1, concat_axis=1, tiled=True),
        lax.all_to_all(gate_blocks, "expert", split_axis=1, concat_axis=1, tiled=True),
    )
    row_count = micro_count * expert_size * capacity
    tok_rows = recv_tok.reshape(row_count, d_model)
    cot_rows = recv_cot.reshape(row_count, d_model)
    gate_rows = recv_gate.reshape(row_count, 1).astype(jnp.float32)
    pre_gate = jnp.dot(tok_rows, gate_full, preferred_element_type=jnp.float32)
    pre_up = jnp.dot(tok_rows, up_full, preferred_element_type=jnp.float32)
    back_proj = jnp.dot(cot_rows, down_full, preferred_element_type=jnp.float32)
    sigmoid_gate = jax.nn.sigmoid(pre_gate)
    activated = pre_gate * sigmoid_gate
    hidden = activated * pre_up
    gate_part = jnp.sum(back_proj * hidden, axis=1)
    scaled_hidden = (gate_rows * hidden).astype(jnp.bfloat16)
    d_hidden = gate_rows * back_proj
    d_pre_gate = (
        d_hidden * pre_up * sigmoid_gate * (1.0 + pre_gate * (1.0 - sigmoid_gate))
    ).astype(jnp.bfloat16)
    d_pre_up = (d_hidden * activated).astype(jnp.bfloat16)
    input_part = jnp.dot(d_pre_gate, gate_full.T, preferred_element_type=jnp.float32)
    input_part = input_part + jnp.dot(d_pre_up, up_full.T, preferred_element_type=jnp.float32)
    tokens_total = tok_count * pipe_size * expert_size
    grad_scale = 1.0 / math.sqrt(micro_count * tokens_total * top_count / EXPERTS)
    contract = (((0,), (0,)), ((), ()))
    part_gate = lax.dot_general(tok_rows, d_pre_gate, contract, preferred_element_type=jnp.float32)
    part_up = lax.dot_general(tok_rows, d_pre_up, contract, preferred_element_type=jnp.float32)
    part_down = lax.dot_general(
        cot_rows, scaled_hidden, contract, preferred_element_type=jnp.float32
    )
    summed = lax.psum_scatter(
        (jnp.concatenate([part_gate, part_up, part_down], 1) * grad_scale).astype(jnp.bfloat16),
        "pipe",
        scatter_dimension=0,
        tiled=True,
    ).astype(jnp.float32)
    hidden_width = gate_full.shape[1]
    dw_gate = summed[:, :hidden_width].astype(jnp.bfloat16)
    dw_up = summed[:, hidden_width : 2 * hidden_width].astype(jnp.bfloat16)
    dw_down_t = summed[:, 2 * hidden_width :].astype(jnp.bfloat16)
    input_blocks = input_part.reshape(micro_count, expert_size, capacity, d_model)
    gate_sums = gate_part.reshape(micro_count, expert_size, capacity)
    back_rows, back_gate = (
        lax.all_to_all(
            input_blocks.astype(jnp.bfloat16), "expert", split_axis=1, concat_axis=1, tiled=True
        ).astype(input_blocks.dtype),
        lax.all_to_all(
            gate_sums.astype(jnp.bfloat16), "expert", split_axis=1, concat_axis=1, tiled=True
        ).astype(gate_sums.dtype),
    )
    slot_input = jnp.sum(
        back_rows.reshape(micro_count, EXPERTS, group_size, capacity, d_model), axis=2
    )
    gate_per_slot = jnp.sum(back_gate.reshape(micro_count, EXPERTS, group_size, capacity), axis=2)
    slot_input = slot_input.reshape(micro_count, slot_total, d_model)
    gate_per_slot = gate_per_slot.reshape(micro_count, slot_total)
    token_table = jnp.sum(
        routing_table.reshape(micro_count, slot_total, tok_count, top_count), axis=3
    )
    d_tokens = jnp.einsum(
        "msc,msd->mcd", token_table, slot_input, precision=highest_precision
    ).astype(jnp.bfloat16)
    gate_weight_gradient = jnp.einsum(
        "kxw,kx->kw", routing_table, gate_per_slot, precision=highest_precision
    ).reshape(micro_count, tok_count, top_count)
    return (d_tokens, gate_weight_gradient, dw_gate, dw_up, dw_down_t)


def solution(mesh):
    return jax.shard_map(
        on_device,
        mesh=mesh,
        in_specs=(
            P(None, ("pipe", "expert"), None),
            P(None, ("pipe", "expert"), None),
            P(None, ("pipe", "expert"), None),
            P(None, ("pipe", "expert"), None),
            P("pipe", "expert"),
            P("pipe", "expert"),
            P("pipe", "expert"),
        ),
        out_specs=(
            P(None, ("pipe", "expert"), None),
            P(None, ("pipe", "expert"), None),
            P("pipe", "expert"),
            P("pipe", "expert"),
            P("pipe", "expert"),
        ),
        check_vma=False,
    )
```

```python
import math

import jax
import jax.numpy as jnp
import numpy as np
from jax import lax
from jax.sharding import Mesh
from jax.sharding import PartitionSpec as P

EXPERTS = 4
CAP = 3
SHARE = ("ey", "core")
TOKEN_AXES = ("pipe", "ex", "ey", "core")


def route_table(expert_ids, expert_total, capacity):
    micro_count, tok_count, top_count = expert_ids.shape
    flat_ids = expert_ids.reshape(micro_count, tok_count * top_count)
    onehot = (
        flat_ids[:, :, None] == jnp.arange(expert_total, dtype=jnp.int32)[None, None, :]
    ).astype(jnp.int32)
    earlier = jnp.cumsum(onehot, axis=1) - onehot
    position = jnp.sum(earlier * onehot, axis=2)
    slot_index = flat_ids * capacity + position
    slot_ids = jnp.arange(expert_total * capacity, dtype=jnp.int32)
    return (slot_index[:, None, :] == slot_ids[None, :, None]).astype(jnp.float32)


def on_device(tokens, cotangent, expert_ids, gate_values, w_gate, w_up, w_down_t):
    micro_count, tok_count, d_model = tokens.shape
    top_count = expert_ids.shape[2]
    pipe_size = lax.axis_size("pipe")
    expert_size = lax.axis_size("ex") * lax.axis_size("ey") * lax.axis_size("core")
    capacity = CAP
    slot_total = EXPERTS * capacity
    highest_precision = lax.Precision.HIGHEST
    cols = w_gate.shape[1]
    w_full = lax.all_gather(
        jnp.concatenate([w_gate, w_up, w_down_t], axis=1), "pipe", axis=0, tiled=True
    )
    gate_full = w_full[:, :cols]
    up_full = w_full[:, cols : 2 * cols]
    down_full = w_full[:, 2 * cols :]
    routing_table = route_table(expert_ids, EXPERTS, capacity)
    routing_table_bfloat16 = routing_table.astype(jnp.bfloat16)
    lanes = 128
    flattened_gate = gate_values.reshape(micro_count, tok_count * top_count)
    payload = jnp.concatenate(
        [
            jnp.repeat(tokens, top_count, axis=1),
            jnp.repeat(cotangent, top_count, axis=1),
            jnp.broadcast_to(flattened_gate[:, :, None], flattened_gate.shape + (lanes,)),
        ],
        axis=2,
    )
    send = jnp.einsum(
        "egf,efh->egh", routing_table_bfloat16, payload, preferred_element_type=jnp.float32
    ).astype(jnp.bfloat16)
    send = send.reshape(micro_count, EXPERTS, capacity, payload.shape[2])
    arrived = lax.all_to_all(send, "ex", split_axis=1, concat_axis=1, tiled=True)
    rows_all = lax.all_gather(arrived, SHARE, axis=0, tiled=False)
    share_count = rows_all.shape[0]
    row_count = share_count * micro_count * EXPERTS * capacity
    rows_all = rows_all.reshape(row_count, payload.shape[2])
    tok_rows = rows_all[:, :d_model]
    cot_rows = rows_all[:, d_model : 2 * d_model]
    gate_rows = rows_all[:, 2 * d_model : 2 * d_model + 1].astype(jnp.float32)
    pre_gate = jnp.dot(tok_rows, gate_full, preferred_element_type=jnp.float32)
    pre_up = jnp.dot(tok_rows, up_full, preferred_element_type=jnp.float32)
    back_proj = jnp.dot(cot_rows, down_full, preferred_element_type=jnp.float32)
    sigmoid_gate = jax.nn.sigmoid(pre_gate)
    activated = pre_gate * sigmoid_gate
    hidden = activated * pre_up
    gate_part = jnp.sum(back_proj * hidden, axis=1)
    scaled_hidden = (gate_rows * hidden).astype(jnp.bfloat16)
    d_hidden = gate_rows * back_proj
    d_pre_gate = (
        d_hidden * pre_up * sigmoid_gate * (1.0 + pre_gate * (1.0 - sigmoid_gate))
    ).astype(jnp.bfloat16)
    d_pre_up = (d_hidden * activated).astype(jnp.bfloat16)
    input_part = jnp.dot(d_pre_gate, gate_full.T, preferred_element_type=jnp.float32)
    input_part = input_part + jnp.dot(d_pre_up, up_full.T, preferred_element_type=jnp.float32)
    tokens_total = tok_count * pipe_size * expert_size
    grad_scale = 1.0 / math.sqrt(micro_count * tokens_total * top_count / EXPERTS)
    contract = (((0,), (0,)), ((), ()))
    part_gate = lax.dot_general(tok_rows, d_pre_gate, contract, preferred_element_type=jnp.float32)
    part_up = lax.dot_general(tok_rows, d_pre_up, contract, preferred_element_type=jnp.float32)
    part_down = lax.dot_general(
        cot_rows, scaled_hidden, contract, preferred_element_type=jnp.float32
    )
    summed = lax.psum_scatter(
        (jnp.concatenate([part_gate, part_up, part_down], 1) * grad_scale).astype(jnp.bfloat16),
        "pipe",
        scatter_dimension=0,
        tiled=True,
    ).astype(jnp.float32)
    hidden_width = gate_full.shape[1]
    dw_gate = summed[:, :hidden_width].astype(jnp.bfloat16)
    dw_up = summed[:, hidden_width : 2 * hidden_width].astype(jnp.bfloat16)
    dw_down_t = summed[:, 2 * hidden_width :].astype(jnp.bfloat16)
    input_blocks = input_part.reshape(share_count, micro_count, EXPERTS, capacity, d_model)
    gate_sums = gate_part.reshape(share_count, micro_count, EXPERTS, capacity)
    input_mine = lax.psum_scatter(
        input_part.astype(jnp.bfloat16), SHARE, scatter_dimension=0, tiled=True
    ).reshape(input_blocks.shape[1:])
    gate_mine = lax.psum_scatter(
        gate_part, SHARE, scatter_dimension=0, tiled=True
    ).reshape(gate_sums.shape[1:])
    slot_input = lax.all_to_all(input_mine, "ex", split_axis=1, concat_axis=1, tiled=True)
    gate_per_slot = lax.all_to_all(gate_mine, "ex", split_axis=1, concat_axis=1, tiled=True)
    slot_input = slot_input.astype(jnp.float32).reshape(micro_count, slot_total, d_model)
    gate_per_slot = gate_per_slot.reshape(micro_count, slot_total)
    token_table = jnp.sum(
        routing_table.reshape(micro_count, slot_total, tok_count, top_count), axis=3
    )
    d_tokens = jnp.einsum(
        "msc,msd->mcd", token_table, slot_input, precision=highest_precision
    ).astype(jnp.bfloat16)
    gate_weight_gradient = jnp.einsum(
        "kxw,kx->kw", routing_table, gate_per_slot, precision=highest_precision
    ).reshape(micro_count, tok_count, top_count)
    return (d_tokens, gate_weight_gradient, dw_gate, dw_up, dw_down_t)


def solution(mesh):
    pipe_size, expert_size = mesh.devices.shape
    split = Mesh(
        np.asarray(mesh.devices).reshape(pipe_size, EXPERTS, expert_size // EXPERTS // 2, 2),
        TOKEN_AXES,
    )
    token_spec = P(None, TOKEN_AXES, None)
    weight_spec = P("pipe", ("ex", "ey", "core"))
    return jax.shard_map(
        on_device,
        mesh=split,
        in_specs=(token_spec,) * 4 + (weight_spec,) * 3,
        out_specs=(token_spec, token_spec) + (weight_spec,) * 3,
        check_vma=False,
    )
```

```python
import math

import jax
import jax.numpy as jnp
import numpy as np
from jax import lax
from jax.sharding import Mesh
from jax.sharding import PartitionSpec as P

EXPERTS = 4
CAP = 3
SHARE = ("ey", "core")
TOKEN_AXES = ("pipe", "ex", "ey", "core")


def route_table(expert_ids, expert_total, capacity):
    micro_count, tok_count, top_count = expert_ids.shape
    flat_ids = expert_ids.reshape(micro_count, tok_count * top_count)
    onehot = (
        flat_ids[:, :, None] == jnp.arange(expert_total, dtype=jnp.int32)[None, None, :]
    ).astype(jnp.int32)
    earlier = jnp.cumsum(onehot, axis=1) - onehot
    position = jnp.sum(earlier * onehot, axis=2)
    slot_index = flat_ids * capacity + position
    slot_ids = jnp.arange(expert_total * capacity, dtype=jnp.int32)
    return (slot_index[:, None, :] == slot_ids[None, :, None]).astype(jnp.float32)


def on_device(tokens, cotangent, expert_ids, gate_values, w_gate, w_up, w_down_t):
    micro_count, tok_count, d_model = tokens.shape
    top_count = expert_ids.shape[2]
    pipe_size = lax.axis_size("pipe")
    expert_size = lax.axis_size("ex") * lax.axis_size("ey") * lax.axis_size("core")
    capacity = CAP
    slot_total = EXPERTS * capacity
    highest_precision = lax.Precision.HIGHEST
    cols = w_gate.shape[1]
    w_full = lax.all_gather(
        jnp.concatenate([w_gate, w_up, w_down_t], axis=1), "pipe", axis=0, tiled=True
    )
    gate_full = w_full[:, :cols]
    up_full = w_full[:, cols : 2 * cols]
    down_full = w_full[:, 2 * cols :]
    routing_table = route_table(expert_ids, EXPERTS, capacity)
    routing_table_bfloat16 = routing_table.astype(jnp.bfloat16)
    lanes = 128
    flattened_gate = gate_values.reshape(micro_count, tok_count * top_count)
    payload = jnp.concatenate(
        [
            jnp.repeat(tokens, top_count, axis=1),
            jnp.repeat(cotangent, top_count, axis=1),
            jnp.broadcast_to(flattened_gate[:, :, None], flattened_gate.shape + (lanes,)),
        ],
        axis=2,
    )
    send = jnp.einsum(
        "egf,efh->egh", routing_table_bfloat16, payload, preferred_element_type=jnp.float32
    ).astype(jnp.bfloat16)
    width = payload.shape[2]
    block_rows = micro_count * capacity
    send = jnp.transpose(send.reshape(micro_count, EXPERTS, capacity, width), (1, 0, 2, 3))
    send = send.reshape(EXPERTS * block_rows, width)
    arrived = lax.all_to_all(send, "ex", split_axis=0, concat_axis=0, tiled=True)
    rows_all = lax.all_gather(arrived, SHARE, axis=0, tiled=True)
    row_count = rows_all.shape[0]
    share_count = row_count // arrived.shape[0]
    tok_rows = rows_all[:, :d_model]
    cot_rows = rows_all[:, d_model : 2 * d_model]
    gate_rows = rows_all[:, 2 * d_model : 2 * d_model + 1].astype(jnp.float32)
    pre_gate = jnp.dot(tok_rows, gate_full, preferred_element_type=jnp.float32)
    pre_up = jnp.dot(tok_rows, up_full, preferred_element_type=jnp.float32)
    back_proj = jnp.dot(cot_rows, down_full, preferred_element_type=jnp.float32)
    sigmoid_gate = jax.nn.sigmoid(pre_gate)
    activated = pre_gate * sigmoid_gate
    hidden = activated * pre_up
    gate_part = jnp.sum(back_proj * hidden, axis=1)
    scaled_hidden = (gate_rows * hidden).astype(jnp.bfloat16)
    d_hidden = gate_rows * back_proj
    d_pre_gate = (
        d_hidden * pre_up * sigmoid_gate * (1.0 + pre_gate * (1.0 - sigmoid_gate))
    ).astype(jnp.bfloat16)
    d_pre_up = (d_hidden * activated).astype(jnp.bfloat16)
    input_part = jnp.dot(d_pre_gate, gate_full.T, preferred_element_type=jnp.float32)
    input_part = input_part + jnp.dot(d_pre_up, up_full.T, preferred_element_type=jnp.float32)
    tokens_total = tok_count * pipe_size * expert_size
    grad_scale = 1.0 / math.sqrt(micro_count * tokens_total * top_count / EXPERTS)
    contract = (((0,), (0,)), ((), ()))
    part_gate = lax.dot_general(tok_rows, d_pre_gate, contract, preferred_element_type=jnp.float32)
    part_up = lax.dot_general(tok_rows, d_pre_up, contract, preferred_element_type=jnp.float32)
    part_down = lax.dot_general(
        cot_rows, scaled_hidden, contract, preferred_element_type=jnp.float32
    )
    summed = lax.psum_scatter(
        (jnp.concatenate([part_gate, part_up, part_down], 1) * grad_scale).astype(jnp.bfloat16),
        "pipe",
        scatter_dimension=0,
        tiled=True,
    ).astype(jnp.float32)
    hidden_width = gate_full.shape[1]
    dw_gate = summed[:, :hidden_width].astype(jnp.bfloat16)
    dw_up = summed[:, hidden_width : 2 * hidden_width].astype(jnp.bfloat16)
    dw_down_t = summed[:, 2 * hidden_width :].astype(jnp.bfloat16)
    input_mine = lax.psum_scatter(
        input_part.astype(jnp.bfloat16), SHARE, scatter_dimension=0, tiled=True
    )
    gate_pieces = lax.all_to_all(
        gate_part.reshape(share_count, EXPERTS * block_rows), SHARE, 0, 0, tiled=True
    )
    gate_mine = jnp.sum(gate_pieces, axis=0)
    gate_high = gate_mine.astype(jnp.bfloat16)
    gate_low = (gate_mine - gate_high.astype(jnp.float32)).astype(jnp.bfloat16)
    gate_columns = jnp.zeros((gate_mine.shape[0], lanes), jnp.bfloat16)
    gate_columns = gate_columns.at[:, 0].set(gate_high).at[:, 1].set(gate_low)
    back = lax.all_to_all(
        jnp.concatenate([input_mine, gate_columns], axis=1), "ex", 0, 0, tiled=True
    )
    back = jnp.transpose(back.reshape(EXPERTS, micro_count, capacity, back.shape[1]), (1, 0, 2, 3))
    back = back.reshape(micro_count, slot_total, back.shape[3])
    slot_input = back[:, :, :d_model].astype(jnp.float32)
    gate_per_slot = back[:, :, d_model].astype(jnp.float32) + back[:, :, d_model + 1].astype(
        jnp.float32
    )
    token_table = jnp.sum(
        routing_table.reshape(micro_count, slot_total, tok_count, top_count), axis=3
    )
    d_tokens = jnp.einsum(
        "msc,msd->mcd", token_table, slot_input, precision=highest_precision
    ).astype(jnp.bfloat16)
    gate_weight_gradient = jnp.einsum(
        "kxw,kx->kw", routing_table, gate_per_slot, precision=highest_precision
    ).reshape(micro_count, tok_count, top_count)
    return (d_tokens, gate_weight_gradient, dw_gate, dw_up, dw_down_t)


def solution(mesh):
    pipe_size, expert_size = mesh.devices.shape
    split = Mesh(
        np.asarray(mesh.devices).reshape(pipe_size, EXPERTS, expert_size // EXPERTS // 2, 2),
        TOKEN_AXES,
    )
    token_spec = P(None, TOKEN_AXES, None)
    weight_spec = P("pipe", ("ex", "ey", "core"))
    return jax.shard_map(
        on_device,
        mesh=split,
        in_specs=(token_spec,) * 4 + (weight_spec,) * 3,
        out_specs=(token_spec, token_spec) + (weight_spec,) * 3,
        check_vma=False,
    )
```

```python
import math

import jax
import jax.numpy as jnp
import numpy as np
from jax import lax
from jax.experimental import pallas as pl
from jax.experimental.pallas import tpu as pltpu
from jax.sharding import Mesh
from jax.sharding import PartitionSpec as P

EXPERTS = 4
CAP = 3
SHARE = ("ey", "core")
TOKEN_AXES = ("pipe", "ex", "ey", "core")


def route_table(expert_ids, expert_total, capacity):
    micro_count, tok_count, top_count = expert_ids.shape
    flat_ids = expert_ids.reshape(micro_count, tok_count * top_count)
    onehot = (
        flat_ids[:, :, None] == jnp.arange(expert_total, dtype=jnp.int32)[None, None, :]
    ).astype(jnp.int32)
    earlier = jnp.cumsum(onehot, axis=1) - onehot
    position = jnp.sum(earlier * onehot, axis=2)
    slot_index = flat_ids * capacity + position
    slot_ids = jnp.arange(expert_total * capacity, dtype=jnp.int32)
    return (slot_index[:, None, :] == slot_ids[None, :, None]).astype(jnp.float32)


def ring_gather_kernel(x_ref, after_ref, out_ref, send_sems, recv_sems, local_sem):
    del after_ref
    count = lax.axis_size("pipe")
    me = lax.axis_index("pipe")
    rest = tuple(lax.axis_index(name) for name in TOKEN_AXES[1:])
    right = lax.rem(me + 1, count)
    left = lax.rem(me + count - 1, count)
    barrier = pltpu.get_barrier_semaphore()
    for peer in (left, right):
        pl.semaphore_signal(
            barrier, inc=1, device_id=(peer,) + rest, device_id_type=pl.DeviceIdType.MESH
        )
    pl.semaphore_wait(barrier, 2)
    own = pltpu.make_async_copy(x_ref, out_ref.at[me], local_sem)
    own.start()
    plans = ((right, count // 2, lambda s: lax.rem(me - s + count, count)),
             (left, (count - 1) // 2, lambda s: lax.rem(me + s, count)))
    started = []

    def transfer(direction, step):
        peer, _, slab_of = plans[direction]
        slab = slab_of(step)
        return pltpu.make_async_remote_copy(
            src_ref=x_ref if step == 0 else out_ref.at[slab],
            dst_ref=out_ref.at[slab],
            send_sem=send_sems.at[direction, step],
            recv_sem=recv_sems.at[direction, step],
            device_id=(peer,) + rest,
            device_id_type=pl.DeviceIdType.MESH,
        )

    def arrival(direction, step):
        peer, _, slab_of = plans[direction]
        source = left if peer is right else right
        slab = lax.rem(slab_of(step + 1), count)
        return pltpu.make_async_remote_copy(
            src_ref=out_ref.at[slab],
            dst_ref=out_ref.at[slab],
            send_sem=send_sems.at[direction, step],
            recv_sem=recv_sems.at[direction, step],
            device_id=(source,) + rest,
            device_id_type=pl.DeviceIdType.MESH,
        )

    for step in range(count // 2):
        for direction in (0, 1):
            if step >= plans[direction][1]:
                continue
            if step > 0:
                arrival(direction, step - 1).wait_recv()
            copy = transfer(direction, step)
            copy.start()
            started.append(copy)
    for direction in (0, 1):
        arrival(direction, plans[direction][1] - 1).wait_recv()
    for copy in started:
        copy.wait_send()
    own.wait()


def ring_gather(x, after):
    count = lax.axis_size("pipe")
    steps = count // 2
    return pl.pallas_call(
        ring_gather_kernel,
        out_shape=jax.ShapeDtypeStruct((count,) + x.shape, x.dtype),
        in_specs=[pl.BlockSpec(memory_space=pl.ANY)] * 2,
        out_specs=pl.BlockSpec(memory_space=pl.ANY),
        scratch_shapes=[
            pltpu.SemaphoreType.DMA((2, steps)),
            pltpu.SemaphoreType.DMA((2, steps)),
            pltpu.SemaphoreType.DMA,
        ],
        compiler_params=pltpu.CompilerParams(collective_id=0, has_side_effects=True),
    )(x, after)


def on_device(tokens, cotangent, expert_ids, gate_values, w_gate, w_up, w_down_t):
    micro_count, tok_count, d_model = tokens.shape
    top_count = expert_ids.shape[2]
    pipe_size = lax.axis_size("pipe")
    expert_size = lax.axis_size("ex") * lax.axis_size("ey") * lax.axis_size("core")
    capacity = CAP
    slot_total = EXPERTS * capacity
    highest_precision = lax.Precision.HIGHEST
    cols = w_gate.shape[1]
    routing_table = route_table(expert_ids, EXPERTS, capacity)
    routing_table_bfloat16 = routing_table.astype(jnp.bfloat16)
    lanes = 128
    flattened_gate = gate_values.reshape(micro_count, tok_count * top_count)
    payload = jnp.concatenate(
        [
            jnp.repeat(tokens, top_count, axis=1),
            jnp.repeat(cotangent, top_count, axis=1),
            jnp.broadcast_to(flattened_gate[:, :, None], flattened_gate.shape + (lanes,)),
        ],
        axis=2,
    )
    send = jnp.einsum(
        "egf,efh->egh", routing_table_bfloat16, payload, preferred_element_type=jnp.float32
    ).astype(jnp.bfloat16)
    width = payload.shape[2]
    block_rows = micro_count * capacity
    send = jnp.transpose(send.reshape(micro_count, EXPERTS, capacity, width), (1, 0, 2, 3))
    send = send.reshape(EXPERTS * block_rows, width)
    arrived = lax.all_to_all(send, "ex", split_axis=0, concat_axis=0, tiled=True)
    rows_all = lax.all_gather(arrived, SHARE, axis=0, tiled=True)
    w_local = jnp.concatenate([w_gate, w_up, w_down_t], axis=1)
    w_full = ring_gather(w_local, arrived).reshape(-1, w_local.shape[1])
    gate_full = w_full[:, :cols]
    up_full = w_full[:, cols : 2 * cols]
    down_full = w_full[:, 2 * cols :]
    row_count = rows_all.shape[0]
    share_count = row_count // arrived.shape[0]
    tok_rows = rows_all[:, :d_model]
    cot_rows = rows_all[:, d_model : 2 * d_model]
    gate_rows = rows_all[:, 2 * d_model : 2 * d_model + 1].astype(jnp.float32)
    pre_gate = jnp.dot(tok_rows, gate_full, preferred_element_type=jnp.float32)
    pre_up = jnp.dot(tok_rows, up_full, preferred_element_type=jnp.float32)
    back_proj = jnp.dot(cot_rows, down_full, preferred_element_type=jnp.float32)
    sigmoid_gate = jax.nn.sigmoid(pre_gate)
    activated = pre_gate * sigmoid_gate
    hidden = activated * pre_up
    gate_part = jnp.sum(back_proj * hidden, axis=1)
    scaled_hidden = (gate_rows * hidden).astype(jnp.bfloat16)
    d_hidden = gate_rows * back_proj
    d_pre_gate = (
        d_hidden * pre_up * sigmoid_gate * (1.0 + pre_gate * (1.0 - sigmoid_gate))
    ).astype(jnp.bfloat16)
    d_pre_up = (d_hidden * activated).astype(jnp.bfloat16)
    input_part = jnp.dot(d_pre_gate, gate_full.T, preferred_element_type=jnp.float32)
    input_part = input_part + jnp.dot(d_pre_up, up_full.T, preferred_element_type=jnp.float32)
    tokens_total = tok_count * pipe_size * expert_size
    grad_scale = 1.0 / math.sqrt(micro_count * tokens_total * top_count / EXPERTS)
    contract = (((0,), (0,)), ((), ()))
    part_gate = lax.dot_general(tok_rows, d_pre_gate, contract, preferred_element_type=jnp.float32)
    part_up = lax.dot_general(tok_rows, d_pre_up, contract, preferred_element_type=jnp.float32)
    part_down = lax.dot_general(
        cot_rows, scaled_hidden, contract, preferred_element_type=jnp.float32
    )
    summed = lax.psum_scatter(
        (jnp.concatenate([part_gate, part_up, part_down], 1) * grad_scale).astype(jnp.bfloat16),
        "pipe",
        scatter_dimension=0,
        tiled=True,
    ).astype(jnp.float32)
    hidden_width = gate_full.shape[1]
    dw_gate = summed[:, :hidden_width].astype(jnp.bfloat16)
    dw_up = summed[:, hidden_width : 2 * hidden_width].astype(jnp.bfloat16)
    dw_down_t = summed[:, 2 * hidden_width :].astype(jnp.bfloat16)
    input_mine = lax.psum_scatter(
        input_part.astype(jnp.bfloat16), SHARE, scatter_dimension=0, tiled=True
    )
    gate_pieces = lax.all_to_all(
        gate_part.reshape(share_count, EXPERTS * block_rows), SHARE, 0, 0, tiled=True
    )
    gate_mine = jnp.sum(gate_pieces, axis=0)
    gate_high = gate_mine.astype(jnp.bfloat16)
    gate_low = (gate_mine - gate_high.astype(jnp.float32)).astype(jnp.bfloat16)
    gate_columns = jnp.zeros((gate_mine.shape[0], lanes), jnp.bfloat16)
    gate_columns = gate_columns.at[:, 0].set(gate_high).at[:, 1].set(gate_low)
    back = lax.all_to_all(
        jnp.concatenate([input_mine, gate_columns], axis=1), "ex", 0, 0, tiled=True
    )
    back = jnp.transpose(back.reshape(EXPERTS, micro_count, capacity, back.shape[1]), (1, 0, 2, 3))
    back = back.reshape(micro_count, slot_total, back.shape[3])
    slot_input = back[:, :, :d_model].astype(jnp.float32)
    gate_per_slot = back[:, :, d_model].astype(jnp.float32) + back[:, :, d_model + 1].astype(
        jnp.float32
    )
    token_table = jnp.sum(
        routing_table.reshape(micro_count, slot_total, tok_count, top_count), axis=3
    )
    d_tokens = jnp.einsum(
        "msc,msd->mcd", token_table, slot_input, precision=highest_precision
    ).astype(jnp.bfloat16)
    gate_weight_gradient = jnp.einsum(
        "kxw,kx->kw", routing_table, gate_per_slot, precision=highest_precision
    ).reshape(micro_count, tok_count, top_count)
    return (d_tokens, gate_weight_gradient, dw_gate, dw_up, dw_down_t)


def solution(mesh):
    pipe_size, expert_size = mesh.devices.shape
    split = Mesh(
        np.asarray(mesh.devices).reshape(pipe_size, EXPERTS, expert_size // EXPERTS // 2, 2),
        TOKEN_AXES,
    )
    token_spec = P(None, TOKEN_AXES, None)
    weight_spec = P("pipe", ("ex", "ey", "core"))
    return jax.shard_map(
        on_device,
        mesh=split,
        in_specs=(token_spec,) * 4 + (weight_spec,) * 3,
        out_specs=(token_spec, token_spec) + (weight_spec,) * 3,
        check_vma=False,
    )
```

```python
import math

import jax
import jax.numpy as jnp
import numpy as np
from jax import lax
from jax.experimental import pallas as pl
from jax.experimental.pallas import tpu as pltpu
from jax.sharding import Mesh
from jax.sharding import PartitionSpec as P

EXPERTS = 4
CAP = 3
SHARE = ("ey", "core")
TOKEN_AXES = ("pipe", "ex", "ey", "core")


def route_table(expert_ids, expert_total, capacity):
    micro_count, tok_count, top_count = expert_ids.shape
    flat_ids = expert_ids.reshape(micro_count, tok_count * top_count)
    onehot = (
        flat_ids[:, :, None] == jnp.arange(expert_total, dtype=jnp.int32)[None, None, :]
    ).astype(jnp.int32)
    earlier = jnp.cumsum(onehot, axis=1) - onehot
    position = jnp.sum(earlier * onehot, axis=2)
    slot_index = flat_ids * capacity + position
    slot_ids = jnp.arange(expert_total * capacity, dtype=jnp.int32)
    return (slot_index[:, None, :] == slot_ids[None, :, None]).astype(jnp.float32)


def ring_gather_kernel(x_ref, after_ref, out_ref, send_sems, recv_sems, local_sem):
    del after_ref
    count = lax.axis_size("pipe")
    me = lax.axis_index("pipe")
    rest = tuple(lax.axis_index(name) for name in TOKEN_AXES[1:])
    right = lax.rem(me + 1, count)
    left = lax.rem(me + count - 1, count)
    barrier = pltpu.get_barrier_semaphore()
    for peer in (left, right):
        pl.semaphore_signal(
            barrier, inc=1, device_id=(peer,) + rest, device_id_type=pl.DeviceIdType.MESH
        )
    pl.semaphore_wait(barrier, 2)
    own = pltpu.make_async_copy(x_ref, out_ref.at[me], local_sem)
    own.start()
    plans = ((right, count // 2, lambda s: lax.rem(me - s + count, count)),
             (left, (count - 1) // 2, lambda s: lax.rem(me + s, count)))
    started = []

    def transfer(direction, step):
        peer, _, slab_of = plans[direction]
        slab = slab_of(step)
        return pltpu.make_async_remote_copy(
            src_ref=x_ref if step == 0 else out_ref.at[slab],
            dst_ref=out_ref.at[slab],
            send_sem=send_sems.at[direction, step],
            recv_sem=recv_sems.at[direction, step],
            device_id=(peer,) + rest,
            device_id_type=pl.DeviceIdType.MESH,
        )

    def arrival(direction, step):
        peer, _, slab_of = plans[direction]
        source = left if peer is right else right
        slab = lax.rem(slab_of(step + 1), count)
        return pltpu.make_async_remote_copy(
            src_ref=out_ref.at[slab],
            dst_ref=out_ref.at[slab],
            send_sem=send_sems.at[direction, step],
            recv_sem=recv_sems.at[direction, step],
            device_id=(source,) + rest,
            device_id_type=pl.DeviceIdType.MESH,
        )

    for step in range(count // 2):
        for direction in (0, 1):
            if step >= plans[direction][1]:
                continue
            if step > 0:
                arrival(direction, step - 1).wait_recv()
            copy = transfer(direction, step)
            copy.start()
            started.append(copy)
    for direction in (0, 1):
        arrival(direction, plans[direction][1] - 1).wait_recv()
    for copy in started:
        copy.wait_send()
    own.wait()


def ring_gather(x, after):
    count = lax.axis_size("pipe")
    steps = count // 2
    return pl.pallas_call(
        ring_gather_kernel,
        out_shape=jax.ShapeDtypeStruct((count,) + x.shape, x.dtype),
        in_specs=[pl.BlockSpec(memory_space=pl.ANY)] * 2,
        out_specs=pl.BlockSpec(memory_space=pl.ANY),
        scratch_shapes=[
            pltpu.SemaphoreType.DMA((2, steps)),
            pltpu.SemaphoreType.DMA((2, steps)),
            pltpu.SemaphoreType.DMA,
        ],
        compiler_params=pltpu.CompilerParams(collective_id=0, has_side_effects=True),
    )(x, after)


def ring_sum_kernel(part_ref, after_ref, out_ref, landing, outgoing, send_sems, recv_sems):
    del after_ref
    count = lax.axis_size("pipe")
    me = lax.axis_index("pipe")
    rest = tuple(lax.axis_index(name) for name in TOKEN_AXES[1:])
    right = lax.rem(me + 1, count)
    left = lax.rem(me + count - 1, count)
    half = part_ref.shape[1] // 2
    barrier = pltpu.get_barrier_semaphore()
    for peer in (left, right):
        pl.semaphore_signal(
            barrier, inc=1, device_id=(peer,) + rest, device_id_type=pl.DeviceIdType.MESH
        )
    pl.semaphore_wait(barrier, 2)
    peers = (right, left)
    rows = (pl.ds(0, half), pl.ds(half, half))

    def chunk_at(direction, step):
        if direction == 0:
            return lax.rem(me - step - 1 + 2 * count, count)
        return lax.rem(me + step + 1, count)

    def copy(direction, step, peer):
        return pltpu.make_async_remote_copy(
            src_ref=outgoing.at[direction, step],
            dst_ref=landing.at[direction, step],
            send_sem=send_sems.at[direction, step],
            recv_sem=recv_sems.at[direction, step],
            device_id=(peer,) + rest,
            device_id_type=pl.DeviceIdType.MESH,
        )

    started = []
    for step in range(count - 1):
        for direction in (0, 1):
            own = part_ref[chunk_at(direction, step), rows[direction], :].astype(jnp.float32)
            if step > 0:
                copy(direction, step - 1, peers[1 - direction]).wait_recv()
                own = own + landing[direction, step - 1].astype(jnp.float32)
            outgoing[direction, step] = own.astype(outgoing.dtype)
            sending = copy(direction, step, peers[direction])
            sending.start()
            started.append(sending)
    for direction in (0, 1):
        copy(direction, count - 2, peers[1 - direction]).wait_recv()
        total = part_ref[me, rows[direction], :].astype(jnp.float32)
        total = total + landing[direction, count - 2].astype(jnp.float32)
        out_ref[rows[direction], :] = total.astype(out_ref.dtype)
    for sending in started:
        sending.wait_send()


def ring_sum(parts, after):
    count = lax.axis_size("pipe")
    rows = parts.shape[0] // count
    parts = parts.reshape(count, rows, parts.shape[1])
    slot = (2, count - 1, rows // 2, parts.shape[2])
    return pl.pallas_call(
        ring_sum_kernel,
        out_shape=jax.ShapeDtypeStruct((rows, parts.shape[2]), parts.dtype),
        in_specs=[
            pl.BlockSpec(memory_space=pltpu.VMEM),
            pl.BlockSpec(memory_space=pl.ANY),
        ],
        out_specs=pl.BlockSpec(memory_space=pltpu.VMEM),
        scratch_shapes=[
            pltpu.VMEM(slot, parts.dtype),
            pltpu.VMEM(slot, parts.dtype),
            pltpu.SemaphoreType.DMA(slot[:2]),
            pltpu.SemaphoreType.DMA(slot[:2]),
        ],
        compiler_params=pltpu.CompilerParams(collective_id=1, has_side_effects=True),
    )(parts, after)


def on_device(tokens, cotangent, expert_ids, gate_values, w_gate, w_up, w_down_t):
    micro_count, tok_count, d_model = tokens.shape
    top_count = expert_ids.shape[2]
    pipe_size = lax.axis_size("pipe")
    expert_size = lax.axis_size("ex") * lax.axis_size("ey") * lax.axis_size("core")
    capacity = CAP
    slot_total = EXPERTS * capacity
    highest_precision = lax.Precision.HIGHEST
    cols = w_gate.shape[1]
    routing_table = route_table(expert_ids, EXPERTS, capacity)
    routing_table_bfloat16 = routing_table.astype(jnp.bfloat16)
    lanes = 128
    flattened_gate = gate_values.reshape(micro_count, tok_count * top_count)
    payload = jnp.concatenate(
        [
            jnp.repeat(tokens, top_count, axis=1),
            jnp.repeat(cotangent, top_count, axis=1),
            jnp.broadcast_to(flattened_gate[:, :, None], flattened_gate.shape + (lanes,)),
        ],
        axis=2,
    )
    send = jnp.einsum(
        "egf,efh->egh", routing_table_bfloat16, payload, preferred_element_type=jnp.float32
    ).astype(jnp.bfloat16)
    width = payload.shape[2]
    block_rows = micro_count * capacity
    send = jnp.transpose(send.reshape(micro_count, EXPERTS, capacity, width), (1, 0, 2, 3))
    send = send.reshape(EXPERTS * block_rows, width)
    arrived = lax.all_to_all(send, "ex", split_axis=0, concat_axis=0, tiled=True)
    rows_all = lax.all_gather(arrived, SHARE, axis=0, tiled=True)
    w_local = jnp.concatenate([w_gate, w_up, w_down_t], axis=1)
    w_full = ring_gather(w_local, arrived).reshape(-1, w_local.shape[1])
    gate_full = w_full[:, :cols]
    up_full = w_full[:, cols : 2 * cols]
    down_full = w_full[:, 2 * cols :]
    row_count = rows_all.shape[0]
    share_count = row_count // arrived.shape[0]
    tok_rows = rows_all[:, :d_model]
    cot_rows = rows_all[:, d_model : 2 * d_model]
    gate_rows = rows_all[:, 2 * d_model : 2 * d_model + 1].astype(jnp.float32)
    pre_gate = jnp.dot(tok_rows, gate_full, preferred_element_type=jnp.float32)
    pre_up = jnp.dot(tok_rows, up_full, preferred_element_type=jnp.float32)
    back_proj = jnp.dot(cot_rows, down_full, preferred_element_type=jnp.float32)
    sigmoid_gate = jax.nn.sigmoid(pre_gate)
    activated = pre_gate * sigmoid_gate
    hidden = activated * pre_up
    gate_part = jnp.sum(back_proj * hidden, axis=1)
    scaled_hidden = (gate_rows * hidden).astype(jnp.bfloat16)
    d_hidden = gate_rows * back_proj
    d_pre_gate = (
        d_hidden * pre_up * sigmoid_gate * (1.0 + pre_gate * (1.0 - sigmoid_gate))
    ).astype(jnp.bfloat16)
    d_pre_up = (d_hidden * activated).astype(jnp.bfloat16)
    input_part = jnp.dot(d_pre_gate, gate_full.T, preferred_element_type=jnp.float32)
    input_part = input_part + jnp.dot(d_pre_up, up_full.T, preferred_element_type=jnp.float32)
    tokens_total = tok_count * pipe_size * expert_size
    grad_scale = 1.0 / math.sqrt(micro_count * tokens_total * top_count / EXPERTS)
    contract = (((0,), (0,)), ((), ()))
    part_gate = lax.dot_general(tok_rows, d_pre_gate, contract, preferred_element_type=jnp.float32)
    part_up = lax.dot_general(tok_rows, d_pre_up, contract, preferred_element_type=jnp.float32)
    part_down = lax.dot_general(
        cot_rows, scaled_hidden, contract, preferred_element_type=jnp.float32
    )
    input_shares = input_part.astype(jnp.bfloat16)
    input_mine = lax.psum_scatter(input_shares, SHARE, scatter_dimension=0, tiled=True)
    summed = ring_sum(
        (jnp.concatenate([part_gate, part_up, part_down], 1) * grad_scale).astype(jnp.bfloat16),
        input_shares,
    ).astype(jnp.float32)
    hidden_width = gate_full.shape[1]
    dw_gate = summed[:, :hidden_width].astype(jnp.bfloat16)
    dw_up = summed[:, hidden_width : 2 * hidden_width].astype(jnp.bfloat16)
    dw_down_t = summed[:, 2 * hidden_width :].astype(jnp.bfloat16)
    gate_pieces = lax.all_to_all(
        gate_part.reshape(share_count, EXPERTS * block_rows), SHARE, 0, 0, tiled=True
    )
    gate_mine = jnp.sum(gate_pieces, axis=0)
    gate_high = gate_mine.astype(jnp.bfloat16)
    gate_low = (gate_mine - gate_high.astype(jnp.float32)).astype(jnp.bfloat16)
    gate_columns = jnp.zeros((gate_mine.shape[0], lanes), jnp.bfloat16)
    gate_columns = gate_columns.at[:, 0].set(gate_high).at[:, 1].set(gate_low)
    back = lax.all_to_all(
        jnp.concatenate([input_mine, gate_columns], axis=1), "ex", 0, 0, tiled=True
    )
    back = jnp.transpose(back.reshape(EXPERTS, micro_count, capacity, back.shape[1]), (1, 0, 2, 3))
    back = back.reshape(micro_count, slot_total, back.shape[3])
    slot_input = back[:, :, :d_model].astype(jnp.float32)
    gate_per_slot = back[:, :, d_model].astype(jnp.float32) + back[:, :, d_model + 1].astype(
        jnp.float32
    )
    token_table = jnp.sum(
        routing_table.reshape(micro_count, slot_total, tok_count, top_count), axis=3
    )
    d_tokens = jnp.einsum(
        "msc,msd->mcd", token_table, slot_input, precision=highest_precision
    ).astype(jnp.bfloat16)
    gate_weight_gradient = jnp.einsum(
        "kxw,kx->kw", routing_table, gate_per_slot, precision=highest_precision
    ).reshape(micro_count, tok_count, top_count)
    return (d_tokens, gate_weight_gradient, dw_gate, dw_up, dw_down_t)


def solution(mesh):
    pipe_size, expert_size = mesh.devices.shape
    split = Mesh(
        np.asarray(mesh.devices).reshape(pipe_size, EXPERTS, expert_size // EXPERTS // 2, 2),
        TOKEN_AXES,
    )
    token_spec = P(None, TOKEN_AXES, None)
    weight_spec = P("pipe", ("ex", "ey", "core"))
    return jax.shard_map(
        on_device,
        mesh=split,
        in_specs=(token_spec,) * 4 + (weight_spec,) * 3,
        out_specs=(token_spec, token_spec) + (weight_spec,) * 3,
        check_vma=False,
    )
```

```python
import math

import jax
import jax.numpy as jnp
import numpy as np
from jax import lax
from jax.experimental import pallas as pl
from jax.experimental.pallas import tpu as pltpu
from jax.sharding import Mesh
from jax.sharding import PartitionSpec as P

EXPERTS = 4
CAP = 3
SHARE = ("ey", "core")
TOKEN_AXES = ("pipe", "ex", "ey", "core")


def route_table(expert_ids, expert_total, capacity):
    micro_count, tok_count, top_count = expert_ids.shape
    flat_ids = expert_ids.reshape(micro_count, tok_count * top_count)
    onehot = (
        flat_ids[:, :, None] == jnp.arange(expert_total, dtype=jnp.int32)[None, None, :]
    ).astype(jnp.int32)
    earlier = jnp.cumsum(onehot, axis=1) - onehot
    position = jnp.sum(earlier * onehot, axis=2)
    slot_index = flat_ids * capacity + position
    slot_ids = jnp.arange(expert_total * capacity, dtype=jnp.int32)
    return (slot_index[:, None, :] == slot_ids[None, :, None]).astype(jnp.float32)


def ring_gather_kernel(x_ref, after_ref, out_ref, send_sems, recv_sems, local_sem):
    del after_ref
    count = lax.axis_size("pipe")
    me = lax.axis_index("pipe")
    rest = tuple(lax.axis_index(name) for name in TOKEN_AXES[1:])
    right = lax.rem(me + 1, count)
    left = lax.rem(me + count - 1, count)
    barrier = pltpu.get_barrier_semaphore()
    for peer in (left, right):
        pl.semaphore_signal(
            barrier, inc=1, device_id=(peer,) + rest, device_id_type=pl.DeviceIdType.MESH
        )
    pl.semaphore_wait(barrier, 2)
    own = pltpu.make_async_copy(x_ref, out_ref.at[me], local_sem)
    own.start()
    plans = ((right, count // 2, lambda s: lax.rem(me - s + count, count)),
             (left, (count - 1) // 2, lambda s: lax.rem(me + s, count)))
    started = []

    def transfer(direction, step):
        peer, _, slab_of = plans[direction]
        slab = slab_of(step)
        return pltpu.make_async_remote_copy(
            src_ref=x_ref if step == 0 else out_ref.at[slab],
            dst_ref=out_ref.at[slab],
            send_sem=send_sems.at[direction, step],
            recv_sem=recv_sems.at[direction, step],
            device_id=(peer,) + rest,
            device_id_type=pl.DeviceIdType.MESH,
        )

    def arrival(direction, step):
        peer, _, slab_of = plans[direction]
        source = left if peer is right else right
        slab = lax.rem(slab_of(step + 1), count)
        return pltpu.make_async_remote_copy(
            src_ref=out_ref.at[slab],
            dst_ref=out_ref.at[slab],
            send_sem=send_sems.at[direction, step],
            recv_sem=recv_sems.at[direction, step],
            device_id=(source,) + rest,
            device_id_type=pl.DeviceIdType.MESH,
        )

    for step in range(count // 2):
        for direction in (0, 1):
            if step >= plans[direction][1]:
                continue
            if step > 0:
                arrival(direction, step - 1).wait_recv()
            copy = transfer(direction, step)
            copy.start()
            started.append(copy)
    for direction in (0, 1):
        arrival(direction, plans[direction][1] - 1).wait_recv()
    for copy in started:
        copy.wait_send()
    own.wait()


def ring_gather(x, after):
    count = lax.axis_size("pipe")
    steps = count // 2
    return pl.pallas_call(
        ring_gather_kernel,
        out_shape=jax.ShapeDtypeStruct((count,) + x.shape, x.dtype),
        in_specs=[pl.BlockSpec(memory_space=pl.ANY)] * 2,
        out_specs=pl.BlockSpec(memory_space=pl.ANY),
        scratch_shapes=[
            pltpu.SemaphoreType.DMA((2, steps)),
            pltpu.SemaphoreType.DMA((2, steps)),
            pltpu.SemaphoreType.DMA,
        ],
        compiler_params=pltpu.CompilerParams(collective_id=0, has_side_effects=True),
    )(x, after)


def ring_sum_kernel(part_ref, after_ref, out_ref, landing, outgoing, send_sems, recv_sems):
    del after_ref
    count = lax.axis_size("pipe")
    me = lax.axis_index("pipe")
    rest = tuple(lax.axis_index(name) for name in TOKEN_AXES[1:])
    right = lax.rem(me + 1, count)
    left = lax.rem(me + count - 1, count)
    half = part_ref.shape[1] // 2
    barrier = pltpu.get_barrier_semaphore()
    for peer in (left, right):
        pl.semaphore_signal(
            barrier, inc=1, device_id=(peer,) + rest, device_id_type=pl.DeviceIdType.MESH
        )
    pl.semaphore_wait(barrier, 2)
    peers = (right, left)
    rows = (pl.ds(0, half), pl.ds(half, half))

    def chunk_at(direction, step):
        if direction == 0:
            return lax.rem(me - step - 1 + 2 * count, count)
        return lax.rem(me + step + 1, count)

    def copy(direction, step, peer):
        return pltpu.make_async_remote_copy(
            src_ref=outgoing.at[direction, step],
            dst_ref=landing.at[direction, step],
            send_sem=send_sems.at[direction, step],
            recv_sem=recv_sems.at[direction, step],
            device_id=(peer,) + rest,
            device_id_type=pl.DeviceIdType.MESH,
        )

    started = []
    for step in range(count - 1):
        for direction in (0, 1):
            own = part_ref[chunk_at(direction, step), rows[direction], :].astype(jnp.float32)
            if step > 0:
                copy(direction, step - 1, peers[1 - direction]).wait_recv()
                own = own + landing[direction, step - 1].astype(jnp.float32)
            outgoing[direction, step] = own.astype(outgoing.dtype)
            sending = copy(direction, step, peers[direction])
            sending.start()
            started.append(sending)
    for direction in (0, 1):
        copy(direction, count - 2, peers[1 - direction]).wait_recv()
        total = part_ref[me, rows[direction], :].astype(jnp.float32)
        total = total + landing[direction, count - 2].astype(jnp.float32)
        out_ref[rows[direction], :] = total.astype(out_ref.dtype)
    for sending in started:
        sending.wait_send()


def ring_sum(parts, after):
    count = lax.axis_size("pipe")
    rows = parts.shape[0] // count
    parts = parts.reshape(count, rows, parts.shape[1])
    slot = (2, count - 1, rows // 2, parts.shape[2])
    return pl.pallas_call(
        ring_sum_kernel,
        out_shape=jax.ShapeDtypeStruct((rows, parts.shape[2]), parts.dtype),
        in_specs=[
            pl.BlockSpec(memory_space=pltpu.VMEM),
            pl.BlockSpec(memory_space=pl.ANY),
        ],
        out_specs=pl.BlockSpec(memory_space=pltpu.VMEM),
        scratch_shapes=[
            pltpu.VMEM(slot, parts.dtype),
            pltpu.VMEM(slot, parts.dtype),
            pltpu.SemaphoreType.DMA(slot[:2]),
            pltpu.SemaphoreType.DMA(slot[:2]),
        ],
        compiler_params=pltpu.CompilerParams(collective_id=1, has_side_effects=True),
    )(parts, after)


def on_device(tokens, cotangent, expert_ids, gate_values, w_gate, w_up, w_down_t):
    micro_count, tok_count, d_model = tokens.shape
    top_count = expert_ids.shape[2]
    pipe_size = lax.axis_size("pipe")
    expert_size = lax.axis_size("ex") * lax.axis_size("ey") * lax.axis_size("core")
    capacity = CAP
    slot_total = EXPERTS * capacity
    highest_precision = lax.Precision.HIGHEST
    cols = w_gate.shape[1]
    routing_table = route_table(expert_ids, EXPERTS, capacity)
    routing_table_bfloat16 = routing_table.astype(jnp.bfloat16)
    lanes = 128
    flattened_gate = gate_values.reshape(micro_count, tok_count * top_count)
    payload = jnp.concatenate(
        [
            jnp.repeat(tokens, top_count, axis=1),
            jnp.repeat(cotangent, top_count, axis=1),
            jnp.broadcast_to(flattened_gate[:, :, None], flattened_gate.shape + (lanes,)),
        ],
        axis=2,
    )
    send = jnp.einsum(
        "egf,efh->egh", routing_table_bfloat16, payload, preferred_element_type=jnp.float32
    ).astype(jnp.bfloat16)
    width = payload.shape[2]
    block_rows = micro_count * capacity
    send = jnp.transpose(send.reshape(micro_count, EXPERTS, capacity, width), (1, 0, 2, 3))
    send = send.reshape(EXPERTS * block_rows, width)
    arrived = lax.all_to_all(send, "ex", split_axis=0, concat_axis=0, tiled=True)
    rows_all = lax.all_gather(
        lax.all_gather(arrived, "core", axis=0, tiled=True), "ey", axis=0, tiled=True
    )
    w_local = jnp.concatenate([w_gate, w_up, w_down_t], axis=1)
    w_full = ring_gather(w_local, arrived).reshape(-1, w_local.shape[1])
    gate_full = w_full[:, :cols]
    up_full = w_full[:, cols : 2 * cols]
    down_full = w_full[:, 2 * cols :]
    row_count = rows_all.shape[0]
    share_count = row_count // arrived.shape[0]
    tok_rows = rows_all[:, :d_model]
    cot_rows = rows_all[:, d_model : 2 * d_model]
    gate_rows = rows_all[:, 2 * d_model : 2 * d_model + 1].astype(jnp.float32)
    pre_gate = jnp.dot(tok_rows, gate_full, preferred_element_type=jnp.float32)
    pre_up = jnp.dot(tok_rows, up_full, preferred_element_type=jnp.float32)
    back_proj = jnp.dot(cot_rows, down_full, preferred_element_type=jnp.float32)
    sigmoid_gate = jax.nn.sigmoid(pre_gate)
    activated = pre_gate * sigmoid_gate
    hidden = activated * pre_up
    gate_part = jnp.sum(back_proj * hidden, axis=1)
    scaled_hidden = (gate_rows * hidden).astype(jnp.bfloat16)
    d_hidden = gate_rows * back_proj
    d_pre_gate = (
        d_hidden * pre_up * sigmoid_gate * (1.0 + pre_gate * (1.0 - sigmoid_gate))
    ).astype(jnp.bfloat16)
    d_pre_up = (d_hidden * activated).astype(jnp.bfloat16)
    core_count = lax.axis_size("core")

    def core_major(rows):
        blocks = rows.reshape(row_count // (core_count * arrived.shape[0]), core_count, -1)
        return jnp.swapaxes(blocks, 0, 1).reshape(rows.shape)

    input_part = jnp.dot(core_major(d_pre_gate), gate_full.T, preferred_element_type=jnp.float32)
    input_part = input_part + jnp.dot(
        core_major(d_pre_up), up_full.T, preferred_element_type=jnp.float32
    )
    tokens_total = tok_count * pipe_size * expert_size
    grad_scale = 1.0 / math.sqrt(micro_count * tokens_total * top_count / EXPERTS)
    contract = (((0,), (0,)), ((), ()))
    part_gate = lax.dot_general(tok_rows, d_pre_gate, contract, preferred_element_type=jnp.float32)
    part_up = lax.dot_general(tok_rows, d_pre_up, contract, preferred_element_type=jnp.float32)
    part_down = lax.dot_general(
        cot_rows, scaled_hidden, contract, preferred_element_type=jnp.float32
    )
    input_shares = input_part.astype(jnp.bfloat16)
    input_mine = lax.psum_scatter(
        lax.psum_scatter(input_shares, "core", scatter_dimension=0, tiled=True),
        "ey",
        scatter_dimension=0,
        tiled=True,
    )
    summed = ring_sum(
        (jnp.concatenate([part_gate, part_up, part_down], 1) * grad_scale).astype(jnp.bfloat16),
        input_shares,
    ).astype(jnp.float32)
    hidden_width = gate_full.shape[1]
    dw_gate = summed[:, :hidden_width].astype(jnp.bfloat16)
    dw_up = summed[:, hidden_width : 2 * hidden_width].astype(jnp.bfloat16)
    dw_down_t = summed[:, 2 * hidden_width :].astype(jnp.bfloat16)
    gate_pieces = lax.all_to_all(
        gate_part.reshape(share_count, EXPERTS * block_rows), SHARE, 0, 0, tiled=True
    )
    gate_mine = jnp.sum(gate_pieces, axis=0)
    gate_high = gate_mine.astype(jnp.bfloat16)
    gate_low = (gate_mine - gate_high.astype(jnp.float32)).astype(jnp.bfloat16)
    gate_columns = jnp.zeros((gate_mine.shape[0], lanes), jnp.bfloat16)
    gate_columns = gate_columns.at[:, 0].set(gate_high).at[:, 1].set(gate_low)
    back = lax.all_to_all(
        jnp.concatenate([input_mine, gate_columns], axis=1), "ex", 0, 0, tiled=True
    )
    back = jnp.transpose(back.reshape(EXPERTS, micro_count, capacity, back.shape[1]), (1, 0, 2, 3))
    back = back.reshape(micro_count, slot_total, back.shape[3])
    slot_input = back[:, :, :d_model].astype(jnp.float32)
    gate_per_slot = back[:, :, d_model].astype(jnp.float32) + back[:, :, d_model + 1].astype(
        jnp.float32
    )
    token_table = jnp.sum(
        routing_table.reshape(micro_count, slot_total, tok_count, top_count), axis=3
    )
    d_tokens = jnp.einsum(
        "msc,msd->mcd", token_table, slot_input, precision=highest_precision
    ).astype(jnp.bfloat16)
    gate_weight_gradient = jnp.einsum(
        "kxw,kx->kw", routing_table, gate_per_slot, precision=highest_precision
    ).reshape(micro_count, tok_count, top_count)
    return (d_tokens, gate_weight_gradient, dw_gate, dw_up, dw_down_t)


def solution(mesh):
    pipe_size, expert_size = mesh.devices.shape
    split = Mesh(
        np.asarray(mesh.devices).reshape(pipe_size, EXPERTS, expert_size // EXPERTS // 2, 2),
        TOKEN_AXES,
    )
    token_spec = P(None, TOKEN_AXES, None)
    weight_spec = P("pipe", ("ex", "ey", "core"))
    return jax.shard_map(
        on_device,
        mesh=split,
        in_specs=(token_spec,) * 4 + (weight_spec,) * 3,
        out_specs=(token_spec, token_spec) + (weight_spec,) * 3,
        check_vma=False,
    )
```

```python
import math

import jax
import jax.numpy as jnp
import numpy as np
from jax import lax
from jax.experimental import pallas as pl
from jax.experimental.pallas import tpu as pltpu
from jax.sharding import Mesh
from jax.sharding import PartitionSpec as P

EXPERTS = 4
CAP = 3
SHARE = ("ey", "core")
TOKEN_AXES = ("pipe", "ex", "ey", "core")


def route_table(expert_ids, expert_total, capacity):
    micro_count, tok_count, top_count = expert_ids.shape
    flat_ids = expert_ids.reshape(micro_count, tok_count * top_count)
    onehot = (
        flat_ids[:, :, None] == jnp.arange(expert_total, dtype=jnp.int32)[None, None, :]
    ).astype(jnp.int32)
    earlier = jnp.cumsum(onehot, axis=1) - onehot
    position = jnp.sum(earlier * onehot, axis=2)
    slot_index = flat_ids * capacity + position
    slot_ids = jnp.arange(expert_total * capacity, dtype=jnp.int32)
    return (slot_index[:, None, :] == slot_ids[None, :, None]).astype(jnp.float32)


def ring_gather_kernel(x_ref, after_ref, out_ref, send_sems, recv_sems, local_sem):
    del after_ref
    count = lax.axis_size("pipe")
    me = lax.axis_index("pipe")
    rest = tuple(lax.axis_index(name) for name in TOKEN_AXES[1:])
    right = lax.rem(me + 1, count)
    left = lax.rem(me + count - 1, count)
    barrier = pltpu.get_barrier_semaphore()
    for peer in (left, right):
        pl.semaphore_signal(
            barrier, inc=1, device_id=(peer,) + rest, device_id_type=pl.DeviceIdType.MESH
        )
    pl.semaphore_wait(barrier, 2)
    own = pltpu.make_async_copy(x_ref, out_ref.at[me], local_sem)
    own.start()
    plans = ((right, count // 2, lambda s: lax.rem(me - s + count, count)),
             (left, (count - 1) // 2, lambda s: lax.rem(me + s, count)))
    started = []

    def transfer(direction, step):
        peer, _, slab_of = plans[direction]
        slab = slab_of(step)
        return pltpu.make_async_remote_copy(
            src_ref=x_ref if step == 0 else out_ref.at[slab],
            dst_ref=out_ref.at[slab],
            send_sem=send_sems.at[direction, step],
            recv_sem=recv_sems.at[direction, step],
            device_id=(peer,) + rest,
            device_id_type=pl.DeviceIdType.MESH,
        )

    def arrival(direction, step):
        peer, _, slab_of = plans[direction]
        source = left if peer is right else right
        slab = lax.rem(slab_of(step + 1), count)
        return pltpu.make_async_remote_copy(
            src_ref=out_ref.at[slab],
            dst_ref=out_ref.at[slab],
            send_sem=send_sems.at[direction, step],
            recv_sem=recv_sems.at[direction, step],
            device_id=(source,) + rest,
            device_id_type=pl.DeviceIdType.MESH,
        )

    for step in range(count // 2):
        for direction in (0, 1):
            if step >= plans[direction][1]:
                continue
            if step > 0:
                arrival(direction, step - 1).wait_recv()
            copy = transfer(direction, step)
            copy.start()
            started.append(copy)
    for direction in (0, 1):
        arrival(direction, plans[direction][1] - 1).wait_recv()
    for copy in started:
        copy.wait_send()
    own.wait()


def ring_gather(x, after):
    count = lax.axis_size("pipe")
    steps = count // 2
    return pl.pallas_call(
        ring_gather_kernel,
        out_shape=jax.ShapeDtypeStruct((count,) + x.shape, x.dtype),
        in_specs=[pl.BlockSpec(memory_space=pl.ANY)] * 2,
        out_specs=pl.BlockSpec(memory_space=pl.ANY),
        scratch_shapes=[
            pltpu.SemaphoreType.DMA((2, steps)),
            pltpu.SemaphoreType.DMA((2, steps)),
            pltpu.SemaphoreType.DMA,
        ],
        compiler_params=pltpu.CompilerParams(collective_id=0, has_side_effects=True),
    )(x, after)


def ring_sum_kernel(part_ref, after_ref, out_ref, landing, outgoing, send_sems, recv_sems):
    del after_ref
    count = lax.axis_size("pipe")
    me = lax.axis_index("pipe")
    rest = tuple(lax.axis_index(name) for name in TOKEN_AXES[1:])
    right = lax.rem(me + 1, count)
    left = lax.rem(me + count - 1, count)
    half = part_ref.shape[1] // 2
    barrier = pltpu.get_barrier_semaphore()
    for peer in (left, right):
        pl.semaphore_signal(
            barrier, inc=1, device_id=(peer,) + rest, device_id_type=pl.DeviceIdType.MESH
        )
    pl.semaphore_wait(barrier, 2)
    peers = (right, left)
    rows = (pl.ds(0, half), pl.ds(half, half))

    def chunk_at(direction, step):
        if direction == 0:
            return lax.rem(me - step - 1 + 2 * count, count)
        return lax.rem(me + step + 1, count)

    def copy(direction, step, peer):
        return pltpu.make_async_remote_copy(
            src_ref=outgoing.at[direction, step],
            dst_ref=landing.at[direction, step],
            send_sem=send_sems.at[direction, step],
            recv_sem=recv_sems.at[direction, step],
            device_id=(peer,) + rest,
            device_id_type=pl.DeviceIdType.MESH,
        )

    started = []
    for step in range(count - 1):
        for direction in (0, 1):
            own = part_ref[chunk_at(direction, step), rows[direction], :].astype(jnp.float32)
            if step > 0:
                copy(direction, step - 1, peers[1 - direction]).wait_recv()
                own = own + landing[direction, step - 1].astype(jnp.float32)
            outgoing[direction, step] = own.astype(outgoing.dtype)
            sending = copy(direction, step, peers[direction])
            sending.start()
            started.append(sending)
    for direction in (0, 1):
        copy(direction, count - 2, peers[1 - direction]).wait_recv()
        total = part_ref[me, rows[direction], :].astype(jnp.float32)
        total = total + landing[direction, count - 2].astype(jnp.float32)
        out_ref[rows[direction], :] = total.astype(out_ref.dtype)
    for sending in started:
        sending.wait_send()


def ring_sum(parts, after):
    count = lax.axis_size("pipe")
    rows = parts.shape[0] // count
    parts = parts.reshape(count, rows, parts.shape[1])
    slot = (2, count - 1, rows // 2, parts.shape[2])
    return pl.pallas_call(
        ring_sum_kernel,
        out_shape=jax.ShapeDtypeStruct((rows, parts.shape[2]), parts.dtype),
        in_specs=[
            pl.BlockSpec(memory_space=pltpu.VMEM),
            pl.BlockSpec(memory_space=pl.ANY),
        ],
        out_specs=pl.BlockSpec(memory_space=pltpu.VMEM),
        scratch_shapes=[
            pltpu.VMEM(slot, parts.dtype),
            pltpu.VMEM(slot, parts.dtype),
            pltpu.SemaphoreType.DMA(slot[:2]),
            pltpu.SemaphoreType.DMA(slot[:2]),
        ],
        compiler_params=pltpu.CompilerParams(collective_id=1, has_side_effects=True),
    )(parts, after)


def exchange_kernel(x_ref, out_ref, send_sems, recv_sems, local_sem):
    count = lax.axis_size("ex")
    me = lax.axis_index("ex")
    pipe = lax.axis_index("pipe")
    rest = tuple(lax.axis_index(name) for name in TOKEN_AXES[2:])

    def device(peer):
        return (pipe, peer) + rest

    barrier = pltpu.get_barrier_semaphore()
    for shift in range(1, count):
        pl.semaphore_signal(
            barrier,
            inc=1,
            device_id=device(lax.rem(me + shift, count)),
            device_id_type=pl.DeviceIdType.MESH,
        )
    pl.semaphore_wait(barrier, count - 1)
    own = pltpu.make_async_copy(x_ref.at[me], out_ref.at[me], local_sem)
    own.start()
    started = []
    for shift in range(1, count):
        peer = lax.rem(me + shift, count)
        sending = pltpu.make_async_remote_copy(
            src_ref=x_ref.at[peer],
            dst_ref=out_ref.at[me],
            send_sem=send_sems.at[peer],
            recv_sem=recv_sems.at[me],
            device_id=device(peer),
            device_id_type=pl.DeviceIdType.MESH,
        )
        sending.start()
        started.append(sending)
    for shift in range(1, count):
        source = lax.rem(me + count - shift, count)
        pltpu.make_async_remote_copy(
            src_ref=x_ref.at[source],
            dst_ref=out_ref.at[source],
            send_sem=send_sems.at[source],
            recv_sem=recv_sems.at[source],
            device_id=device(source),
            device_id_type=pl.DeviceIdType.MESH,
        ).wait_recv()
    for sending in started:
        sending.wait_send()
    own.wait()


def exchange(x, collective):
    count = lax.axis_size("ex")
    return pl.pallas_call(
        exchange_kernel,
        out_shape=jax.ShapeDtypeStruct(x.shape, x.dtype),
        in_specs=[pl.BlockSpec(memory_space=pl.ANY)],
        out_specs=pl.BlockSpec(memory_space=pl.ANY),
        scratch_shapes=[
            pltpu.SemaphoreType.DMA((count,)),
            pltpu.SemaphoreType.DMA((count,)),
            pltpu.SemaphoreType.DMA,
        ],
        compiler_params=pltpu.CompilerParams(collective_id=collective, has_side_effects=True),
    )(x)


def on_device(tokens, cotangent, expert_ids, gate_values, w_gate, w_up, w_down_t):
    micro_count, tok_count, d_model = tokens.shape
    top_count = expert_ids.shape[2]
    pipe_size = lax.axis_size("pipe")
    expert_size = lax.axis_size("ex") * lax.axis_size("ey") * lax.axis_size("core")
    capacity = CAP
    slot_total = EXPERTS * capacity
    highest_precision = lax.Precision.HIGHEST
    cols = w_gate.shape[1]
    routing_table = route_table(expert_ids, EXPERTS, capacity)
    routing_table_bfloat16 = routing_table.astype(jnp.bfloat16)
    lanes = 128
    flattened_gate = gate_values.reshape(micro_count, tok_count * top_count)
    payload = jnp.concatenate(
        [
            jnp.repeat(tokens, top_count, axis=1),
            jnp.repeat(cotangent, top_count, axis=1),
            jnp.broadcast_to(flattened_gate[:, :, None], flattened_gate.shape + (lanes,)),
        ],
        axis=2,
    )
    send = jnp.einsum(
        "egf,efh->egh", routing_table_bfloat16, payload, preferred_element_type=jnp.float32
    ).astype(jnp.bfloat16)
    width = payload.shape[2]
    block_rows = micro_count * capacity
    send = jnp.transpose(send.reshape(micro_count, EXPERTS, capacity, width), (1, 0, 2, 3))
    send = send.reshape(EXPERTS, block_rows, width)
    arrived = exchange(send, 2).reshape(EXPERTS * block_rows, width)
    rows_all = lax.all_gather(arrived, SHARE, axis=0, tiled=True)
    w_local = jnp.concatenate([w_gate, w_up, w_down_t], axis=1)
    w_full = ring_gather(w_local, arrived).reshape(-1, w_local.shape[1])
    gate_full = w_full[:, :cols]
    up_full = w_full[:, cols : 2 * cols]
    down_full = w_full[:, 2 * cols :]
    row_count = rows_all.shape[0]
    share_count = row_count // arrived.shape[0]
    tok_rows = rows_all[:, :d_model]
    cot_rows = rows_all[:, d_model : 2 * d_model]
    gate_rows = rows_all[:, 2 * d_model : 2 * d_model + 1].astype(jnp.float32)
    pre_gate = jnp.dot(tok_rows, gate_full, preferred_element_type=jnp.float32)
    pre_up = jnp.dot(tok_rows, up_full, preferred_element_type=jnp.float32)
    back_proj = jnp.dot(cot_rows, down_full, preferred_element_type=jnp.float32)
    sigmoid_gate = jax.nn.sigmoid(pre_gate)
    activated = pre_gate * sigmoid_gate
    hidden = activated * pre_up
    gate_part = jnp.sum(back_proj * hidden, axis=1)
    scaled_hidden = (gate_rows * hidden).astype(jnp.bfloat16)
    d_hidden = gate_rows * back_proj
    d_pre_gate = (
        d_hidden * pre_up * sigmoid_gate * (1.0 + pre_gate * (1.0 - sigmoid_gate))
    ).astype(jnp.bfloat16)
    d_pre_up = (d_hidden * activated).astype(jnp.bfloat16)
    input_part = jnp.dot(d_pre_gate, gate_full.T, preferred_element_type=jnp.float32)
    input_part = input_part + jnp.dot(d_pre_up, up_full.T, preferred_element_type=jnp.float32)
    tokens_total = tok_count * pipe_size * expert_size
    grad_scale = 1.0 / math.sqrt(micro_count * tokens_total * top_count / EXPERTS)
    contract = (((0,), (0,)), ((), ()))
    part_gate = lax.dot_general(tok_rows, d_pre_gate, contract, preferred_element_type=jnp.float32)
    part_up = lax.dot_general(tok_rows, d_pre_up, contract, preferred_element_type=jnp.float32)
    part_down = lax.dot_general(
        cot_rows, scaled_hidden, contract, preferred_element_type=jnp.float32
    )
    input_shares = input_part.astype(jnp.bfloat16)
    input_mine = lax.psum_scatter(input_shares, SHARE, scatter_dimension=0, tiled=True)
    summed = ring_sum(
        (jnp.concatenate([part_gate, part_up, part_down], 1) * grad_scale).astype(jnp.bfloat16),
        input_shares,
    ).astype(jnp.float32)
    hidden_width = gate_full.shape[1]
    dw_gate = summed[:, :hidden_width].astype(jnp.bfloat16)
    dw_up = summed[:, hidden_width : 2 * hidden_width].astype(jnp.bfloat16)
    dw_down_t = summed[:, 2 * hidden_width :].astype(jnp.bfloat16)
    gate_pieces = lax.all_to_all(
        gate_part.reshape(share_count, EXPERTS * block_rows), SHARE, 0, 0, tiled=True
    )
    gate_mine = jnp.sum(gate_pieces, axis=0)
    gate_high = gate_mine.astype(jnp.bfloat16)
    gate_low = (gate_mine - gate_high.astype(jnp.float32)).astype(jnp.bfloat16)
    gate_columns = jnp.zeros((gate_mine.shape[0], lanes), jnp.bfloat16)
    gate_columns = gate_columns.at[:, 0].set(gate_high).at[:, 1].set(gate_low)
    back = jnp.concatenate([input_mine, gate_columns], axis=1)
    back = exchange(back.reshape(EXPERTS, block_rows, back.shape[1]), 3)
    back = jnp.transpose(back.reshape(EXPERTS, micro_count, capacity, back.shape[2]), (1, 0, 2, 3))
    back = back.reshape(micro_count, slot_total, back.shape[3])
    slot_input = back[:, :, :d_model].astype(jnp.float32)
    gate_per_slot = back[:, :, d_model].astype(jnp.float32) + back[:, :, d_model + 1].astype(
        jnp.float32
    )
    token_table = jnp.sum(
        routing_table.reshape(micro_count, slot_total, tok_count, top_count), axis=3
    )
    d_tokens = jnp.einsum(
        "msc,msd->mcd", token_table, slot_input, precision=highest_precision
    ).astype(jnp.bfloat16)
    gate_weight_gradient = jnp.einsum(
        "kxw,kx->kw", routing_table, gate_per_slot, precision=highest_precision
    ).reshape(micro_count, tok_count, top_count)
    return (d_tokens, gate_weight_gradient, dw_gate, dw_up, dw_down_t)


def solution(mesh):
    pipe_size, expert_size = mesh.devices.shape
    split = Mesh(
        np.asarray(mesh.devices).reshape(pipe_size, EXPERTS, expert_size // EXPERTS // 2, 2),
        TOKEN_AXES,
    )
    token_spec = P(None, TOKEN_AXES, None)
    weight_spec = P("pipe", ("ex", "ey", "core"))
    return jax.shard_map(
        on_device,
        mesh=split,
        in_specs=(token_spec,) * 4 + (weight_spec,) * 3,
        out_specs=(token_spec, token_spec) + (weight_spec,) * 3,
        check_vma=False,
    )
```

```python
import math

import jax
import jax.numpy as jnp
import numpy as np
from jax import lax
from jax.experimental import pallas as pl
from jax.experimental.pallas import tpu as pltpu
from jax.sharding import Mesh
from jax.sharding import PartitionSpec as P

EXPERTS = 4
CAP = 3
SHARE = ("ey", "core")
TOKEN_AXES = ("pipe", "ex", "ey", "core")


def route_table(expert_ids, expert_total, capacity):
    micro_count, tok_count, top_count = expert_ids.shape
    flat_ids = expert_ids.reshape(micro_count, tok_count * top_count)
    onehot = (
        flat_ids[:, :, None] == jnp.arange(expert_total, dtype=jnp.int32)[None, None, :]
    ).astype(jnp.int32)
    earlier = jnp.cumsum(onehot, axis=1) - onehot
    position = jnp.sum(earlier * onehot, axis=2)
    slot_index = flat_ids * capacity + position
    slot_ids = jnp.arange(expert_total * capacity, dtype=jnp.int32)
    return (slot_index[:, None, :] == slot_ids[None, :, None]).astype(jnp.float32)


def ring_gather_kernel(x_ref, after_ref, out_ref, send_sems, recv_sems, local_sem):
    del after_ref
    count = lax.axis_size("pipe")
    me = lax.axis_index("pipe")
    rest = tuple(lax.axis_index(name) for name in TOKEN_AXES[1:])
    right = lax.rem(me + 1, count)
    left = lax.rem(me + count - 1, count)
    barrier = pltpu.get_barrier_semaphore()
    for peer in (left, right):
        pl.semaphore_signal(
            barrier, inc=1, device_id=(peer,) + rest, device_id_type=pl.DeviceIdType.MESH
        )
    pl.semaphore_wait(barrier, 2)
    own = pltpu.make_async_copy(x_ref, out_ref.at[me], local_sem)
    own.start()
    plans = ((right, count // 2, lambda s: lax.rem(me - s + count, count)),
             (left, (count - 1) // 2, lambda s: lax.rem(me + s, count)))
    started = []

    def transfer(direction, step):
        peer, _, slab_of = plans[direction]
        slab = slab_of(step)
        return pltpu.make_async_remote_copy(
            src_ref=x_ref if step == 0 else out_ref.at[slab],
            dst_ref=out_ref.at[slab],
            send_sem=send_sems.at[direction, step],
            recv_sem=recv_sems.at[direction, step],
            device_id=(peer,) + rest,
            device_id_type=pl.DeviceIdType.MESH,
        )

    def arrival(direction, step):
        peer, _, slab_of = plans[direction]
        source = left if peer is right else right
        slab = lax.rem(slab_of(step + 1), count)
        return pltpu.make_async_remote_copy(
            src_ref=out_ref.at[slab],
            dst_ref=out_ref.at[slab],
            send_sem=send_sems.at[direction, step],
            recv_sem=recv_sems.at[direction, step],
            device_id=(source,) + rest,
            device_id_type=pl.DeviceIdType.MESH,
        )

    for step in range(count // 2):
        for direction in (0, 1):
            if step >= plans[direction][1]:
                continue
            if step > 0:
                arrival(direction, step - 1).wait_recv()
            copy = transfer(direction, step)
            copy.start()
            started.append(copy)
    for direction in (0, 1):
        arrival(direction, plans[direction][1] - 1).wait_recv()
    for copy in started:
        copy.wait_send()
    own.wait()


def ring_gather(x, after):
    count = lax.axis_size("pipe")
    steps = count // 2
    return pl.pallas_call(
        ring_gather_kernel,
        out_shape=jax.ShapeDtypeStruct((count,) + x.shape, x.dtype),
        in_specs=[pl.BlockSpec(memory_space=pl.ANY)] * 2,
        out_specs=pl.BlockSpec(memory_space=pl.ANY),
        scratch_shapes=[
            pltpu.SemaphoreType.DMA((2, steps)),
            pltpu.SemaphoreType.DMA((2, steps)),
            pltpu.SemaphoreType.DMA,
        ],
        compiler_params=pltpu.CompilerParams(collective_id=0, has_side_effects=True),
    )(x, after)


def ring_sum_kernel(part_ref, after_ref, out_ref, landing, outgoing, send_sems, recv_sems):
    del after_ref
    count = lax.axis_size("pipe")
    me = lax.axis_index("pipe")
    rest = tuple(lax.axis_index(name) for name in TOKEN_AXES[1:])
    right = lax.rem(me + 1, count)
    left = lax.rem(me + count - 1, count)
    half = part_ref.shape[1] // 2
    barrier = pltpu.get_barrier_semaphore()
    for peer in (left, right):
        pl.semaphore_signal(
            barrier, inc=1, device_id=(peer,) + rest, device_id_type=pl.DeviceIdType.MESH
        )
    pl.semaphore_wait(barrier, 2)
    peers = (right, left)
    rows = (pl.ds(0, half), pl.ds(half, half))

    def chunk_at(direction, step):
        if direction == 0:
            return lax.rem(me - step - 1 + 2 * count, count)
        return lax.rem(me + step + 1, count)

    def copy(direction, step, peer):
        return pltpu.make_async_remote_copy(
            src_ref=outgoing.at[direction, step],
            dst_ref=landing.at[direction, step],
            send_sem=send_sems.at[direction, step],
            recv_sem=recv_sems.at[direction, step],
            device_id=(peer,) + rest,
            device_id_type=pl.DeviceIdType.MESH,
        )

    started = []
    for step in range(count - 1):
        for direction in (0, 1):
            own = part_ref[chunk_at(direction, step), rows[direction], :].astype(jnp.float32)
            if step > 0:
                copy(direction, step - 1, peers[1 - direction]).wait_recv()
                own = own + landing[direction, step - 1].astype(jnp.float32)
            outgoing[direction, step] = own.astype(outgoing.dtype)
            sending = copy(direction, step, peers[direction])
            sending.start()
            started.append(sending)
    for direction in (0, 1):
        copy(direction, count - 2, peers[1 - direction]).wait_recv()
        total = part_ref[me, rows[direction], :].astype(jnp.float32)
        total = total + landing[direction, count - 2].astype(jnp.float32)
        out_ref[rows[direction], :] = total.astype(out_ref.dtype)
    for sending in started:
        sending.wait_send()


def ring_sum(parts, after):
    count = lax.axis_size("pipe")
    rows = parts.shape[0] // count
    parts = parts.reshape(count, rows, parts.shape[1])
    slot = (2, count - 1, rows // 2, parts.shape[2])
    return pl.pallas_call(
        ring_sum_kernel,
        out_shape=jax.ShapeDtypeStruct((rows, parts.shape[2]), parts.dtype),
        in_specs=[
            pl.BlockSpec(memory_space=pltpu.VMEM),
            pl.BlockSpec(memory_space=pl.ANY),
        ],
        out_specs=pl.BlockSpec(memory_space=pltpu.VMEM),
        scratch_shapes=[
            pltpu.VMEM(slot, parts.dtype),
            pltpu.VMEM(slot, parts.dtype),
            pltpu.SemaphoreType.DMA(slot[:2]),
            pltpu.SemaphoreType.DMA(slot[:2]),
        ],
        compiler_params=pltpu.CompilerParams(collective_id=1, has_side_effects=True),
    )(parts, after)


def on_device(tokens, cotangent, expert_ids, gate_values, w_gate, w_up, w_down_t):
    micro_count, tok_count, d_model = tokens.shape
    top_count = expert_ids.shape[2]
    pipe_size = lax.axis_size("pipe")
    expert_size = lax.axis_size("ex") * lax.axis_size("ey") * lax.axis_size("core")
    capacity = CAP
    slot_total = EXPERTS * capacity
    highest_precision = lax.Precision.HIGHEST
    cols = w_gate.shape[1]
    routing_table = route_table(expert_ids, EXPERTS, capacity)
    routing_table_bfloat16 = routing_table.astype(jnp.bfloat16)
    lanes = 128
    flattened_gate = gate_values.reshape(micro_count, tok_count * top_count)
    payload = jnp.concatenate(
        [
            jnp.repeat(tokens, top_count, axis=1),
            jnp.repeat(cotangent, top_count, axis=1),
            jnp.broadcast_to(flattened_gate[:, :, None], flattened_gate.shape + (lanes,)),
        ],
        axis=2,
    )
    send = jnp.einsum(
        "egf,efh->egh", routing_table_bfloat16, payload, preferred_element_type=jnp.float32
    ).astype(jnp.bfloat16)
    width = payload.shape[2]
    block_rows = micro_count * capacity
    send = jnp.transpose(send.reshape(micro_count, EXPERTS, capacity, width), (1, 0, 2, 3))
    send = send.reshape(EXPERTS * block_rows, width)
    arrived = lax.all_to_all(send, "ex", split_axis=0, concat_axis=0, tiled=True)
    rows_all = lax.all_gather(arrived, SHARE, axis=0, tiled=True)
    w_local = jnp.concatenate([w_gate, w_up, w_down_t], axis=1)
    w_full = ring_gather(w_local, arrived).reshape(-1, w_local.shape[1])
    gate_full = w_full[:, :cols]
    up_full = w_full[:, cols : 2 * cols]
    down_full = w_full[:, 2 * cols :]
    row_count = rows_all.shape[0]
    share_count = row_count // arrived.shape[0]
    tok_rows = rows_all[:, :d_model]
    cot_rows = rows_all[:, d_model : 2 * d_model]
    gate_rows = rows_all[:, 2 * d_model : 2 * d_model + 1].astype(jnp.float32)
    pre_gate = jnp.dot(tok_rows, gate_full, preferred_element_type=jnp.float32)
    pre_up = jnp.dot(tok_rows, up_full, preferred_element_type=jnp.float32)
    back_proj = jnp.dot(cot_rows, down_full, preferred_element_type=jnp.float32)
    sigmoid_gate = jax.nn.sigmoid(pre_gate)
    activated = pre_gate * sigmoid_gate
    hidden = activated * pre_up
    gate_part = jnp.sum(back_proj * hidden, axis=1)
    scaled_hidden = (gate_rows * hidden).astype(jnp.bfloat16)
    d_hidden = gate_rows * back_proj
    d_pre_gate = (
        d_hidden * pre_up * sigmoid_gate * (1.0 + pre_gate * (1.0 - sigmoid_gate))
    ).astype(jnp.bfloat16)
    d_pre_up = (d_hidden * activated).astype(jnp.bfloat16)
    input_part = jnp.dot(d_pre_gate, gate_full.T, preferred_element_type=jnp.float32)
    input_part = input_part + jnp.dot(d_pre_up, up_full.T, preferred_element_type=jnp.float32)
    tokens_total = tok_count * pipe_size * expert_size
    grad_scale = 1.0 / math.sqrt(micro_count * tokens_total * top_count / EXPERTS)
    contract = (((0,), (0,)), ((), ()))
    part_gate = lax.dot_general(tok_rows, d_pre_gate, contract, preferred_element_type=jnp.float32)
    part_up = lax.dot_general(tok_rows, d_pre_up, contract, preferred_element_type=jnp.float32)
    part_down = lax.dot_general(
        cot_rows, scaled_hidden, contract, preferred_element_type=jnp.float32
    )
    me_share = lax.axis_index("ey") * lax.axis_size("core") + lax.axis_index("core")
    gate_high = gate_part.astype(jnp.bfloat16)
    gate_low = (gate_part - gate_high.astype(jnp.float32)).astype(jnp.bfloat16)
    lane = lax.broadcasted_iota(jnp.int32, (1, lanes), 1)
    gate_columns = jnp.where(lane == 2 * me_share, gate_high[:, None], 0).astype(jnp.bfloat16)
    gate_columns = jnp.where(lane == 2 * me_share + 1, gate_low[:, None], gate_columns)
    input_shares = jnp.concatenate([input_part.astype(jnp.bfloat16), gate_columns], axis=1)
    input_mine = lax.psum_scatter(input_shares, SHARE, scatter_dimension=0, tiled=True)
    summed = ring_sum(
        (jnp.concatenate([part_gate, part_up, part_down], 1) * grad_scale).astype(jnp.bfloat16),
        input_shares,
    ).astype(jnp.float32)
    hidden_width = gate_full.shape[1]
    dw_gate = summed[:, :hidden_width].astype(jnp.bfloat16)
    dw_up = summed[:, hidden_width : 2 * hidden_width].astype(jnp.bfloat16)
    dw_down_t = summed[:, 2 * hidden_width :].astype(jnp.bfloat16)
    back = lax.all_to_all(input_mine, "ex", 0, 0, tiled=True)
    back = jnp.transpose(back.reshape(EXPERTS, micro_count, capacity, back.shape[1]), (1, 0, 2, 3))
    back = back.reshape(micro_count, slot_total, back.shape[3])
    slot_input = back[:, :, :d_model].astype(jnp.float32)
    gate_split = back[:, :, d_model : d_model + 2 * share_count].astype(jnp.float32)
    gate_per_slot = jnp.sum(gate_split, axis=2)
    token_table = jnp.sum(
        routing_table.reshape(micro_count, slot_total, tok_count, top_count), axis=3
    )
    d_tokens = jnp.einsum(
        "msc,msd->mcd", token_table, slot_input, precision=highest_precision
    ).astype(jnp.bfloat16)
    gate_weight_gradient = jnp.einsum(
        "kxw,kx->kw", routing_table, gate_per_slot, precision=highest_precision
    ).reshape(micro_count, tok_count, top_count)
    return (d_tokens, gate_weight_gradient, dw_gate, dw_up, dw_down_t)


def solution(mesh):
    pipe_size, expert_size = mesh.devices.shape
    split = Mesh(
        np.asarray(mesh.devices).reshape(pipe_size, EXPERTS, expert_size // EXPERTS // 2, 2),
        TOKEN_AXES,
    )
    token_spec = P(None, TOKEN_AXES, None)
    weight_spec = P("pipe", ("ex", "ey", "core"))
    return jax.shard_map(
        on_device,
        mesh=split,
        in_specs=(token_spec,) * 4 + (weight_spec,) * 3,
        out_specs=(token_spec, token_spec) + (weight_spec,) * 3,
        check_vma=False,
    )
```

```python
import math

import jax
import jax.numpy as jnp
import numpy as np
from jax import lax
from jax.experimental import pallas as pl
from jax.experimental.pallas import tpu as pltpu
from jax.sharding import Mesh
from jax.sharding import PartitionSpec as P

EXPERTS = 4
CAP = 3
SHARE = ("ey", "core")
TOKEN_AXES = ("pipe", "ex", "ey", "core")


def route_table(expert_ids, expert_total, capacity):
    micro_count, tok_count, top_count = expert_ids.shape
    flat_ids = expert_ids.reshape(micro_count, tok_count * top_count)
    onehot = (
        flat_ids[:, :, None] == jnp.arange(expert_total, dtype=jnp.int32)[None, None, :]
    ).astype(jnp.int32)
    earlier = jnp.cumsum(onehot, axis=1) - onehot
    position = jnp.sum(earlier * onehot, axis=2)
    slot_index = flat_ids * capacity + position
    slot_ids = jnp.arange(expert_total * capacity, dtype=jnp.int32)
    return (slot_index[:, None, :] == slot_ids[None, :, None]).astype(jnp.float32)


def ring_gather_kernel(x_ref, after_ref, out_ref, send_sems, recv_sems, local_sem):
    del after_ref
    count = lax.axis_size("pipe")
    me = lax.axis_index("pipe")
    rest = tuple(lax.axis_index(name) for name in TOKEN_AXES[1:])
    right = lax.rem(me + 1, count)
    left = lax.rem(me + count - 1, count)
    barrier = pltpu.get_barrier_semaphore()
    for peer in (left, right):
        pl.semaphore_signal(
            barrier, inc=1, device_id=(peer,) + rest, device_id_type=pl.DeviceIdType.MESH
        )
    pl.semaphore_wait(barrier, 2)
    own = pltpu.make_async_copy(x_ref, out_ref.at[me], local_sem)
    own.start()
    plans = ((right, count // 2, lambda s: lax.rem(me - s + count, count)),
             (left, (count - 1) // 2, lambda s: lax.rem(me + s, count)))
    started = []

    def transfer(direction, step):
        peer, _, slab_of = plans[direction]
        slab = slab_of(step)
        return pltpu.make_async_remote_copy(
            src_ref=x_ref if step == 0 else out_ref.at[slab],
            dst_ref=out_ref.at[slab],
            send_sem=send_sems.at[direction, step],
            recv_sem=recv_sems.at[direction, step],
            device_id=(peer,) + rest,
            device_id_type=pl.DeviceIdType.MESH,
        )

    def arrival(direction, step):
        peer, _, slab_of = plans[direction]
        source = left if peer is right else right
        slab = lax.rem(slab_of(step + 1), count)
        return pltpu.make_async_remote_copy(
            src_ref=out_ref.at[slab],
            dst_ref=out_ref.at[slab],
            send_sem=send_sems.at[direction, step],
            recv_sem=recv_sems.at[direction, step],
            device_id=(source,) + rest,
            device_id_type=pl.DeviceIdType.MESH,
        )

    for step in range(count // 2):
        for direction in (0, 1):
            if step >= plans[direction][1]:
                continue
            if step > 0:
                arrival(direction, step - 1).wait_recv()
            copy = transfer(direction, step)
            copy.start()
            started.append(copy)
    for direction in (0, 1):
        arrival(direction, plans[direction][1] - 1).wait_recv()
    for copy in started:
        copy.wait_send()
    own.wait()


def ring_gather(x, after):
    count = lax.axis_size("pipe")
    steps = count // 2
    return pl.pallas_call(
        ring_gather_kernel,
        out_shape=jax.ShapeDtypeStruct((count,) + x.shape, x.dtype),
        in_specs=[pl.BlockSpec(memory_space=pl.ANY)] * 2,
        out_specs=pl.BlockSpec(memory_space=pl.ANY),
        scratch_shapes=[
            pltpu.SemaphoreType.DMA((2, steps)),
            pltpu.SemaphoreType.DMA((2, steps)),
            pltpu.SemaphoreType.DMA,
        ],
        compiler_params=pltpu.CompilerParams(collective_id=0, has_side_effects=True),
    )(x, after)


def ring_sum_kernel(part_ref, after_ref, out_ref, landing, outgoing, send_sems, recv_sems):
    del after_ref
    count = lax.axis_size("pipe")
    me = lax.axis_index("pipe")
    rest = tuple(lax.axis_index(name) for name in TOKEN_AXES[1:])
    right = lax.rem(me + 1, count)
    left = lax.rem(me + count - 1, count)
    half = part_ref.shape[1] // 2
    barrier = pltpu.get_barrier_semaphore()
    for peer in (left, right):
        pl.semaphore_signal(
            barrier, inc=1, device_id=(peer,) + rest, device_id_type=pl.DeviceIdType.MESH
        )
    pl.semaphore_wait(barrier, 2)
    peers = (right, left)
    rows = (pl.ds(0, half), pl.ds(half, half))

    def chunk_at(direction, step):
        if direction == 0:
            return lax.rem(me - step - 1 + 2 * count, count)
        return lax.rem(me + step + 1, count)

    def copy(direction, step, peer):
        return pltpu.make_async_remote_copy(
            src_ref=outgoing.at[direction, step],
            dst_ref=landing.at[direction, step],
            send_sem=send_sems.at[direction, step],
            recv_sem=recv_sems.at[direction, step],
            device_id=(peer,) + rest,
            device_id_type=pl.DeviceIdType.MESH,
        )

    started = []
    for step in range(count - 1):
        for direction in (0, 1):
            own = part_ref[chunk_at(direction, step), rows[direction], :].astype(jnp.float32)
            if step > 0:
                copy(direction, step - 1, peers[1 - direction]).wait_recv()
                own = own + landing[direction, step - 1].astype(jnp.float32)
            outgoing[direction, step] = own.astype(outgoing.dtype)
            sending = copy(direction, step, peers[direction])
            sending.start()
            started.append(sending)
    for direction in (0, 1):
        copy(direction, count - 2, peers[1 - direction]).wait_recv()
        total = part_ref[me, rows[direction], :].astype(jnp.float32)
        total = total + landing[direction, count - 2].astype(jnp.float32)
        out_ref[rows[direction], :] = total.astype(out_ref.dtype)
    for sending in started:
        sending.wait_send()


def ring_sum(parts, after):
    count = lax.axis_size("pipe")
    rows = parts.shape[0] // count
    parts = parts.reshape(count, rows, parts.shape[1])
    slot = (2, count - 1, rows // 2, parts.shape[2])
    return pl.pallas_call(
        ring_sum_kernel,
        out_shape=jax.ShapeDtypeStruct((rows, parts.shape[2]), parts.dtype),
        in_specs=[
            pl.BlockSpec(memory_space=pltpu.VMEM),
            pl.BlockSpec(memory_space=pl.ANY),
        ],
        out_specs=pl.BlockSpec(memory_space=pltpu.VMEM),
        scratch_shapes=[
            pltpu.VMEM(slot, parts.dtype),
            pltpu.VMEM(slot, parts.dtype),
            pltpu.SemaphoreType.DMA(slot[:2]),
            pltpu.SemaphoreType.DMA(slot[:2]),
        ],
        compiler_params=pltpu.CompilerParams(collective_id=1, has_side_effects=True),
    )(parts, after)


def pair_sum_kernel(x_ref, out_ref, landing, send_sem, recv_sem):
    me = lax.axis_index("core")
    other = 1 - me
    head = tuple(lax.axis_index(name) for name in TOKEN_AXES[:3])
    partner = head + (other,)
    barrier = pltpu.get_barrier_semaphore()
    pl.semaphore_signal(
        barrier, inc=1, device_id=partner, device_id_type=pl.DeviceIdType.MESH
    )
    pl.semaphore_wait(barrier, 1)
    sending = pltpu.make_async_remote_copy(
        src_ref=x_ref.at[other],
        dst_ref=landing,
        send_sem=send_sem,
        recv_sem=recv_sem,
        device_id=partner,
        device_id_type=pl.DeviceIdType.MESH,
    )
    sending.start()
    sending.wait_recv()
    total = x_ref[me].astype(jnp.float32) + landing[...].astype(jnp.float32)
    out_ref[...] = total.astype(out_ref.dtype)
    sending.wait_send()


def pair_sum(x):
    return pl.pallas_call(
        pair_sum_kernel,
        out_shape=jax.ShapeDtypeStruct(x.shape[1:], x.dtype),
        in_specs=[pl.BlockSpec(memory_space=pltpu.VMEM)],
        out_specs=pl.BlockSpec(memory_space=pltpu.VMEM),
        scratch_shapes=[
            pltpu.VMEM(x.shape[1:], x.dtype),
            pltpu.SemaphoreType.DMA,
            pltpu.SemaphoreType.DMA,
        ],
        compiler_params=pltpu.CompilerParams(collective_id=2, has_side_effects=True),
    )(x)


def on_device(tokens, cotangent, expert_ids, gate_values, w_gate, w_up, w_down_t):
    micro_count, tok_count, d_model = tokens.shape
    top_count = expert_ids.shape[2]
    pipe_size = lax.axis_size("pipe")
    expert_size = lax.axis_size("ex") * lax.axis_size("ey") * lax.axis_size("core")
    capacity = CAP
    slot_total = EXPERTS * capacity
    highest_precision = lax.Precision.HIGHEST
    cols = w_gate.shape[1]
    routing_table = route_table(expert_ids, EXPERTS, capacity)
    routing_table_bfloat16 = routing_table.astype(jnp.bfloat16)
    lanes = 128
    flattened_gate = gate_values.reshape(micro_count, tok_count * top_count)
    payload = jnp.concatenate(
        [
            jnp.repeat(tokens, top_count, axis=1),
            jnp.repeat(cotangent, top_count, axis=1),
            jnp.broadcast_to(flattened_gate[:, :, None], flattened_gate.shape + (lanes,)),
        ],
        axis=2,
    )
    send = jnp.einsum(
        "egf,efh->egh", routing_table_bfloat16, payload, preferred_element_type=jnp.float32
    ).astype(jnp.bfloat16)
    width = payload.shape[2]
    block_rows = micro_count * capacity
    send = jnp.transpose(send.reshape(micro_count, EXPERTS, capacity, width), (1, 0, 2, 3))
    send = send.reshape(EXPERTS * block_rows, width)
    arrived = lax.all_to_all(send, "ex", split_axis=0, concat_axis=0, tiled=True)
    rows_all = lax.all_gather(arrived, SHARE, axis=0, tiled=True)
    w_local = jnp.concatenate([w_gate, w_up, w_down_t], axis=1)
    w_full = ring_gather(w_local, arrived).reshape(-1, w_local.shape[1])
    gate_full = w_full[:, :cols]
    up_full = w_full[:, cols : 2 * cols]
    down_full = w_full[:, 2 * cols :]
    row_count = rows_all.shape[0]
    share_count = row_count // arrived.shape[0]
    tok_rows = rows_all[:, :d_model]
    cot_rows = rows_all[:, d_model : 2 * d_model]
    gate_rows = rows_all[:, 2 * d_model : 2 * d_model + 1].astype(jnp.float32)
    pre_gate = jnp.dot(tok_rows, gate_full, preferred_element_type=jnp.float32)
    pre_up = jnp.dot(tok_rows, up_full, preferred_element_type=jnp.float32)
    back_proj = jnp.dot(cot_rows, down_full, preferred_element_type=jnp.float32)
    sigmoid_gate = jax.nn.sigmoid(pre_gate)
    activated = pre_gate * sigmoid_gate
    hidden = activated * pre_up
    gate_part = jnp.sum(back_proj * hidden, axis=1)
    scaled_hidden = (gate_rows * hidden).astype(jnp.bfloat16)
    d_hidden = gate_rows * back_proj
    d_pre_gate = (
        d_hidden * pre_up * sigmoid_gate * (1.0 + pre_gate * (1.0 - sigmoid_gate))
    ).astype(jnp.bfloat16)
    d_pre_up = (d_hidden * activated).astype(jnp.bfloat16)
    core_count = lax.axis_size("core")

    def core_major(rows):
        blocks = rows.reshape(row_count // (core_count * arrived.shape[0]), core_count, -1)
        return jnp.swapaxes(blocks, 0, 1).reshape(rows.shape)

    input_part = jnp.dot(core_major(d_pre_gate), gate_full.T, preferred_element_type=jnp.float32)
    input_part = input_part + jnp.dot(
        core_major(d_pre_up), up_full.T, preferred_element_type=jnp.float32
    )
    tokens_total = tok_count * pipe_size * expert_size
    grad_scale = 1.0 / math.sqrt(micro_count * tokens_total * top_count / EXPERTS)
    contract = (((0,), (0,)), ((), ()))
    part_gate = lax.dot_general(tok_rows, d_pre_gate, contract, preferred_element_type=jnp.float32)
    part_up = lax.dot_general(tok_rows, d_pre_up, contract, preferred_element_type=jnp.float32)
    part_down = lax.dot_general(
        cot_rows, scaled_hidden, contract, preferred_element_type=jnp.float32
    )
    me_share = lax.axis_index("ey") * lax.axis_size("core") + lax.axis_index("core")
    gate_high = gate_part.astype(jnp.bfloat16)
    gate_low = (gate_part - gate_high.astype(jnp.float32)).astype(jnp.bfloat16)
    lane = lax.broadcasted_iota(jnp.int32, (1, lanes), 1)
    gate_columns = jnp.where(lane == 2 * me_share, gate_high[:, None], 0).astype(jnp.bfloat16)
    gate_columns = jnp.where(lane == 2 * me_share + 1, gate_low[:, None], gate_columns)
    input_shares = jnp.concatenate(
        [input_part.astype(jnp.bfloat16), core_major(gate_columns)], axis=1
    )
    input_pair = pair_sum(input_shares.reshape(core_count, row_count // core_count, -1))
    input_mine = lax.psum_scatter(input_pair, "ey", scatter_dimension=0, tiled=True)
    summed = ring_sum(
        (jnp.concatenate([part_gate, part_up, part_down], 1) * grad_scale).astype(jnp.bfloat16),
        input_pair,
    ).astype(jnp.float32)
    hidden_width = gate_full.shape[1]
    dw_gate = summed[:, :hidden_width].astype(jnp.bfloat16)
    dw_up = summed[:, hidden_width : 2 * hidden_width].astype(jnp.bfloat16)
    dw_down_t = summed[:, 2 * hidden_width :].astype(jnp.bfloat16)
    back = lax.all_to_all(input_mine, "ex", 0, 0, tiled=True)
    back = jnp.transpose(back.reshape(EXPERTS, micro_count, capacity, back.shape[1]), (1, 0, 2, 3))
    back = back.reshape(micro_count, slot_total, back.shape[3])
    slot_input = back[:, :, :d_model].astype(jnp.float32)
    gate_split = back[:, :, d_model : d_model + 2 * share_count].astype(jnp.float32)
    gate_per_slot = jnp.sum(gate_split, axis=2)
    token_table = jnp.sum(
        routing_table.reshape(micro_count, slot_total, tok_count, top_count), axis=3
    )
    d_tokens = jnp.einsum(
        "msc,msd->mcd", token_table, slot_input, precision=highest_precision
    ).astype(jnp.bfloat16)
    gate_weight_gradient = jnp.einsum(
        "kxw,kx->kw", routing_table, gate_per_slot, precision=highest_precision
    ).reshape(micro_count, tok_count, top_count)
    return (d_tokens, gate_weight_gradient, dw_gate, dw_up, dw_down_t)


def solution(mesh):
    pipe_size, expert_size = mesh.devices.shape
    split = Mesh(
        np.asarray(mesh.devices).reshape(pipe_size, EXPERTS, expert_size // EXPERTS // 2, 2),
        TOKEN_AXES,
    )
    token_spec = P(None, TOKEN_AXES, None)
    weight_spec = P("pipe", ("ex", "ey", "core"))
    return jax.shard_map(
        on_device,
        mesh=split,
        in_specs=(token_spec,) * 4 + (weight_spec,) * 3,
        out_specs=(token_spec, token_spec) + (weight_spec,) * 3,
        check_vma=False,
    )
```

```python
import math

import jax
import jax.numpy as jnp
import numpy as np
from jax import lax
from jax.experimental import pallas as pl
from jax.experimental.pallas import tpu as pltpu
from jax.sharding import Mesh
from jax.sharding import PartitionSpec as P

EXPERTS = 4
CAP = 3
SHARE = ("ey", "core")
TOKEN_AXES = ("pipe", "ex", "ey", "core")


def route_table(expert_ids, expert_total, capacity):
    micro_count, tok_count, top_count = expert_ids.shape
    flat_ids = expert_ids.reshape(micro_count, tok_count * top_count)
    onehot = (
        flat_ids[:, :, None] == jnp.arange(expert_total, dtype=jnp.int32)[None, None, :]
    ).astype(jnp.int32)
    earlier = jnp.cumsum(onehot, axis=1) - onehot
    position = jnp.sum(earlier * onehot, axis=2)
    slot_index = flat_ids * capacity + position
    slot_ids = jnp.arange(expert_total * capacity, dtype=jnp.int32)
    return (slot_index[:, None, :] == slot_ids[None, :, None]).astype(jnp.float32)


def ring_gather_kernel(x_ref, after_ref, out_ref, send_sems, recv_sems, local_sem):
    del after_ref
    count = lax.axis_size("pipe")
    me = lax.axis_index("pipe")
    rest = tuple(lax.axis_index(name) for name in TOKEN_AXES[1:])
    right = lax.rem(me + 1, count)
    left = lax.rem(me + count - 1, count)
    barrier = pltpu.get_barrier_semaphore()
    for peer in (left, right):
        pl.semaphore_signal(
            barrier, inc=1, device_id=(peer,) + rest, device_id_type=pl.DeviceIdType.MESH
        )
    pl.semaphore_wait(barrier, 2)
    own = pltpu.make_async_copy(x_ref, out_ref.at[me], local_sem)
    own.start()
    plans = ((right, count // 2, lambda s: lax.rem(me - s + count, count)),
             (left, (count - 1) // 2, lambda s: lax.rem(me + s, count)))
    started = []

    def transfer(direction, step):
        peer, _, slab_of = plans[direction]
        slab = slab_of(step)
        return pltpu.make_async_remote_copy(
            src_ref=x_ref if step == 0 else out_ref.at[slab],
            dst_ref=out_ref.at[slab],
            send_sem=send_sems.at[direction, step],
            recv_sem=recv_sems.at[direction, step],
            device_id=(peer,) + rest,
            device_id_type=pl.DeviceIdType.MESH,
        )

    def arrival(direction, step):
        peer, _, slab_of = plans[direction]
        source = left if peer is right else right
        slab = lax.rem(slab_of(step + 1), count)
        return pltpu.make_async_remote_copy(
            src_ref=out_ref.at[slab],
            dst_ref=out_ref.at[slab],
            send_sem=send_sems.at[direction, step],
            recv_sem=recv_sems.at[direction, step],
            device_id=(source,) + rest,
            device_id_type=pl.DeviceIdType.MESH,
        )

    for step in range(count // 2):
        for direction in (0, 1):
            if step >= plans[direction][1]:
                continue
            if step > 0:
                arrival(direction, step - 1).wait_recv()
            copy = transfer(direction, step)
            copy.start()
            started.append(copy)
    for direction in (0, 1):
        arrival(direction, plans[direction][1] - 1).wait_recv()
    for copy in started:
        copy.wait_send()
    own.wait()


def ring_gather(x, after):
    count = lax.axis_size("pipe")
    steps = count // 2
    return pl.pallas_call(
        ring_gather_kernel,
        out_shape=jax.ShapeDtypeStruct((count,) + x.shape, x.dtype),
        in_specs=[pl.BlockSpec(memory_space=pl.ANY)] * 2,
        out_specs=pl.BlockSpec(memory_space=pl.ANY),
        scratch_shapes=[
            pltpu.SemaphoreType.DMA((2, steps)),
            pltpu.SemaphoreType.DMA((2, steps)),
            pltpu.SemaphoreType.DMA,
        ],
        compiler_params=pltpu.CompilerParams(collective_id=0, has_side_effects=True),
    )(x, after)


def ring_sum_kernel(part_ref, after_ref, out_ref, landing, outgoing, send_sems, recv_sems):
    del after_ref
    count = lax.axis_size("pipe")
    me = lax.axis_index("pipe")
    rest = tuple(lax.axis_index(name) for name in TOKEN_AXES[1:])
    right = lax.rem(me + 1, count)
    left = lax.rem(me + count - 1, count)
    lanes_count = landing.shape[0]
    piece = part_ref.shape[1] // lanes_count
    barrier = pltpu.get_barrier_semaphore()
    for peer in (left, right):
        pl.semaphore_signal(
            barrier, inc=1, device_id=(peer,) + rest, device_id_type=pl.DeviceIdType.MESH
        )
    pl.semaphore_wait(barrier, 2)
    rows = [pl.ds(k * piece, piece) for k in range(lanes_count)]

    def goes_right(k):
        return k % 2 == 0

    def chunk_at(k, step):
        if goes_right(k):
            return lax.rem(me - step - 1 + 2 * count, count)
        return lax.rem(me + step + 1, count)

    def copy(k, step, peer):
        return pltpu.make_async_remote_copy(
            src_ref=outgoing.at[k, step],
            dst_ref=landing.at[k, step],
            send_sem=send_sems.at[k, step],
            recv_sem=recv_sems.at[k, step],
            device_id=(peer,) + rest,
            device_id_type=pl.DeviceIdType.MESH,
        )

    def sender(k):
        return right if goes_right(k) else left

    def source(k):
        return left if goes_right(k) else right

    started = []
    for step in range(count - 1):
        for k in range(lanes_count):
            own = part_ref[chunk_at(k, step), rows[k], :].astype(jnp.float32)
            if step > 0:
                copy(k, step - 1, source(k)).wait_recv()
                own = own + landing[k, step - 1].astype(jnp.float32)
            outgoing[k, step] = own.astype(outgoing.dtype)
            sending = copy(k, step, sender(k))
            sending.start()
            started.append(sending)
    for k in range(lanes_count):
        copy(k, count - 2, source(k)).wait_recv()
        total = part_ref[me, rows[k], :].astype(jnp.float32)
        total = total + landing[k, count - 2].astype(jnp.float32)
        out_ref[rows[k], :] = total.astype(out_ref.dtype)
    for sending in started:
        sending.wait_send()


def ring_sum(parts, after):
    count = lax.axis_size("pipe")
    rows = parts.shape[0] // count
    parts = parts.reshape(count, rows, parts.shape[1])
    pieces = 4
    slot = (pieces, count - 1, rows // pieces, parts.shape[2])
    return pl.pallas_call(
        ring_sum_kernel,
        out_shape=jax.ShapeDtypeStruct((rows, parts.shape[2]), parts.dtype),
        in_specs=[
            pl.BlockSpec(memory_space=pltpu.VMEM),
            pl.BlockSpec(memory_space=pl.ANY),
        ],
        out_specs=pl.BlockSpec(memory_space=pltpu.VMEM),
        scratch_shapes=[
            pltpu.VMEM(slot, parts.dtype),
            pltpu.VMEM(slot, parts.dtype),
            pltpu.SemaphoreType.DMA(slot[:2]),
            pltpu.SemaphoreType.DMA(slot[:2]),
        ],
        compiler_params=pltpu.CompilerParams(collective_id=1, has_side_effects=True),
    )(parts, after)


def pair_sum_kernel(x_ref, out_ref, landing, send_sem, recv_sem):
    me = lax.axis_index("core")
    other = 1 - me
    head = tuple(lax.axis_index(name) for name in TOKEN_AXES[:3])
    partner = head + (other,)
    barrier = pltpu.get_barrier_semaphore()
    pl.semaphore_signal(
        barrier, inc=1, device_id=partner, device_id_type=pl.DeviceIdType.MESH
    )
    pl.semaphore_wait(barrier, 1)
    sending = pltpu.make_async_remote_copy(
        src_ref=x_ref.at[other],
        dst_ref=landing,
        send_sem=send_sem,
        recv_sem=recv_sem,
        device_id=partner,
        device_id_type=pl.DeviceIdType.MESH,
    )
    sending.start()
    sending.wait_recv()
    total = x_ref[me].astype(jnp.float32) + landing[...].astype(jnp.float32)
    out_ref[...] = total.astype(out_ref.dtype)
    sending.wait_send()


def pair_sum(x):
    return pl.pallas_call(
        pair_sum_kernel,
        out_shape=jax.ShapeDtypeStruct(x.shape[1:], x.dtype),
        in_specs=[pl.BlockSpec(memory_space=pltpu.VMEM)],
        out_specs=pl.BlockSpec(memory_space=pltpu.VMEM),
        scratch_shapes=[
            pltpu.VMEM(x.shape[1:], x.dtype),
            pltpu.SemaphoreType.DMA,
            pltpu.SemaphoreType.DMA,
        ],
        compiler_params=pltpu.CompilerParams(collective_id=2, has_side_effects=True),
    )(x)


def on_device(tokens, cotangent, expert_ids, gate_values, w_gate, w_up, w_down_t):
    micro_count, tok_count, d_model = tokens.shape
    top_count = expert_ids.shape[2]
    pipe_size = lax.axis_size("pipe")
    expert_size = lax.axis_size("ex") * lax.axis_size("ey") * lax.axis_size("core")
    capacity = CAP
    slot_total = EXPERTS * capacity
    highest_precision = lax.Precision.HIGHEST
    cols = w_gate.shape[1]
    routing_table = route_table(expert_ids, EXPERTS, capacity)
    routing_table_bfloat16 = routing_table.astype(jnp.bfloat16)
    lanes = 128
    flattened_gate = gate_values.reshape(micro_count, tok_count * top_count)
    payload = jnp.concatenate(
        [
            jnp.repeat(tokens, top_count, axis=1),
            jnp.repeat(cotangent, top_count, axis=1),
            jnp.broadcast_to(flattened_gate[:, :, None], flattened_gate.shape + (lanes,)),
        ],
        axis=2,
    )
    send = jnp.einsum(
        "egf,efh->egh", routing_table_bfloat16, payload, preferred_element_type=jnp.float32
    ).astype(jnp.bfloat16)
    width = payload.shape[2]
    block_rows = micro_count * capacity
    send = jnp.transpose(send.reshape(micro_count, EXPERTS, capacity, width), (1, 0, 2, 3))
    send = send.reshape(EXPERTS * block_rows, width)
    arrived = lax.all_to_all(send, "ex", split_axis=0, concat_axis=0, tiled=True)
    rows_all = lax.all_gather(arrived, SHARE, axis=0, tiled=True)
    w_local = jnp.concatenate([w_gate, w_up, w_down_t], axis=1)
    w_full = ring_gather(w_local, arrived).reshape(-1, w_local.shape[1])
    gate_full = w_full[:, :cols]
    up_full = w_full[:, cols : 2 * cols]
    down_full = w_full[:, 2 * cols :]
    row_count = rows_all.shape[0]
    share_count = row_count // arrived.shape[0]
    tok_rows = rows_all[:, :d_model]
    cot_rows = rows_all[:, d_model : 2 * d_model]
    gate_rows = rows_all[:, 2 * d_model : 2 * d_model + 1].astype(jnp.float32)
    pre_gate = jnp.dot(tok_rows, gate_full, preferred_element_type=jnp.float32)
    pre_up = jnp.dot(tok_rows, up_full, preferred_element_type=jnp.float32)
    back_proj = jnp.dot(cot_rows, down_full, preferred_element_type=jnp.float32)
    sigmoid_gate = jax.nn.sigmoid(pre_gate)
    activated = pre_gate * sigmoid_gate
    hidden = activated * pre_up
    gate_part = jnp.sum(back_proj * hidden, axis=1)
    scaled_hidden = (gate_rows * hidden).astype(jnp.bfloat16)
    d_hidden = gate_rows * back_proj
    d_pre_gate = (
        d_hidden * pre_up * sigmoid_gate * (1.0 + pre_gate * (1.0 - sigmoid_gate))
    ).astype(jnp.bfloat16)
    d_pre_up = (d_hidden * activated).astype(jnp.bfloat16)
    core_count = lax.axis_size("core")

    def core_major(rows):
        blocks = rows.reshape(row_count // (core_count * arrived.shape[0]), core_count, -1)
        return jnp.swapaxes(blocks, 0, 1).reshape(rows.shape)

    input_part = jnp.dot(core_major(d_pre_gate), gate_full.T, preferred_element_type=jnp.float32)
    input_part = input_part + jnp.dot(
        core_major(d_pre_up), up_full.T, preferred_element_type=jnp.float32
    )
    tokens_total = tok_count * pipe_size * expert_size
    grad_scale = 1.0 / math.sqrt(micro_count * tokens_total * top_count / EXPERTS)
    contract = (((0,), (0,)), ((), ()))
    part_gate = lax.dot_general(tok_rows, d_pre_gate, contract, preferred_element_type=jnp.float32)
    part_up = lax.dot_general(tok_rows, d_pre_up, contract, preferred_element_type=jnp.float32)
    part_down = lax.dot_general(
        cot_rows, scaled_hidden, contract, preferred_element_type=jnp.float32
    )
    me_share = lax.axis_index("ey") * lax.axis_size("core") + lax.axis_index("core")
    gate_high = gate_part.astype(jnp.bfloat16)
    gate_low = (gate_part - gate_high.astype(jnp.float32)).astype(jnp.bfloat16)
    lane = lax.broadcasted_iota(jnp.int32, (1, lanes), 1)
    gate_columns = jnp.where(lane == 2 * me_share, gate_high[:, None], 0).astype(jnp.bfloat16)
    gate_columns = jnp.where(lane == 2 * me_share + 1, gate_low[:, None], gate_columns)
    input_shares = jnp.concatenate(
        [input_part.astype(jnp.bfloat16), core_major(gate_columns)], axis=1
    )
    input_pair = pair_sum(input_shares.reshape(core_count, row_count // core_count, -1))
    input_mine = lax.psum_scatter(input_pair, "ey", scatter_dimension=0, tiled=True)
    summed = ring_sum(
        (jnp.concatenate([part_gate, part_up, part_down], 1) * grad_scale).astype(jnp.bfloat16),
        input_pair,
    ).astype(jnp.float32)
    hidden_width = gate_full.shape[1]
    dw_gate = summed[:, :hidden_width].astype(jnp.bfloat16)
    dw_up = summed[:, hidden_width : 2 * hidden_width].astype(jnp.bfloat16)
    dw_down_t = summed[:, 2 * hidden_width :].astype(jnp.bfloat16)
    back = lax.all_to_all(input_mine, "ex", 0, 0, tiled=True)
    back = jnp.transpose(back.reshape(EXPERTS, micro_count, capacity, back.shape[1]), (1, 0, 2, 3))
    back = back.reshape(micro_count, slot_total, back.shape[3])
    slot_input = back[:, :, :d_model].astype(jnp.float32)
    gate_split = back[:, :, d_model : d_model + 2 * share_count].astype(jnp.float32)
    gate_per_slot = jnp.sum(gate_split, axis=2)
    token_table = jnp.sum(
        routing_table.reshape(micro_count, slot_total, tok_count, top_count), axis=3
    )
    d_tokens = jnp.einsum(
        "msc,msd->mcd", token_table, slot_input, precision=highest_precision
    ).astype(jnp.bfloat16)
    gate_weight_gradient = jnp.einsum(
        "kxw,kx->kw", routing_table, gate_per_slot, precision=highest_precision
    ).reshape(micro_count, tok_count, top_count)
    return (d_tokens, gate_weight_gradient, dw_gate, dw_up, dw_down_t)


def solution(mesh):
    pipe_size, expert_size = mesh.devices.shape
    split = Mesh(
        np.asarray(mesh.devices).reshape(pipe_size, EXPERTS, expert_size // EXPERTS // 2, 2),
        TOKEN_AXES,
    )
    token_spec = P(None, TOKEN_AXES, None)
    weight_spec = P("pipe", ("ex", "ey", "core"))
    return jax.shard_map(
        on_device,
        mesh=split,
        in_specs=(token_spec,) * 4 + (weight_spec,) * 3,
        out_specs=(token_spec, token_spec) + (weight_spec,) * 3,
        check_vma=False,
    )
```

```python
import math

import jax
import jax.numpy as jnp
import numpy as np
from jax import lax
from jax.experimental import pallas as pl
from jax.experimental.pallas import tpu as pltpu
from jax.sharding import Mesh
from jax.sharding import PartitionSpec as P

EXPERTS = 4
CAP = 3
SHARE = ("ey", "core")
TOKEN_AXES = ("pipe", "ex", "ey", "core")


def route_table(expert_ids, expert_total, capacity):
    micro_count, tok_count, top_count = expert_ids.shape
    flat_ids = expert_ids.reshape(micro_count, tok_count * top_count)
    onehot = (
        flat_ids[:, :, None] == jnp.arange(expert_total, dtype=jnp.int32)[None, None, :]
    ).astype(jnp.int32)
    earlier = jnp.cumsum(onehot, axis=1) - onehot
    position = jnp.sum(earlier * onehot, axis=2)
    slot_index = flat_ids * capacity + position
    slot_ids = jnp.arange(expert_total * capacity, dtype=jnp.int32)
    return (slot_index[:, None, :] == slot_ids[None, :, None]).astype(jnp.float32)


def ring_gather_kernel(x_ref, after_ref, out_ref, send_sems, recv_sems, local_sem):
    del after_ref
    count = lax.axis_size("pipe")
    me = lax.axis_index("pipe")
    rest = tuple(lax.axis_index(name) for name in TOKEN_AXES[1:])
    right = lax.rem(me + 1, count)
    left = lax.rem(me + count - 1, count)
    barrier = pltpu.get_barrier_semaphore()
    for peer in (left, right):
        pl.semaphore_signal(
            barrier, inc=1, device_id=(peer,) + rest, device_id_type=pl.DeviceIdType.MESH
        )
    pl.semaphore_wait(barrier, 2)
    own = pltpu.make_async_copy(x_ref, out_ref.at[me], local_sem)
    own.start()
    plans = ((right, count // 2, lambda s: lax.rem(me - s + count, count)),
             (left, (count - 1) // 2, lambda s: lax.rem(me + s, count)))
    started = []

    def transfer(direction, step):
        peer, _, slab_of = plans[direction]
        slab = slab_of(step)
        return pltpu.make_async_remote_copy(
            src_ref=x_ref if step == 0 else out_ref.at[slab],
            dst_ref=out_ref.at[slab],
            send_sem=send_sems.at[direction, step],
            recv_sem=recv_sems.at[direction, step],
            device_id=(peer,) + rest,
            device_id_type=pl.DeviceIdType.MESH,
        )

    def arrival(direction, step):
        peer, _, slab_of = plans[direction]
        source = left if peer is right else right
        slab = lax.rem(slab_of(step + 1), count)
        return pltpu.make_async_remote_copy(
            src_ref=out_ref.at[slab],
            dst_ref=out_ref.at[slab],
            send_sem=send_sems.at[direction, step],
            recv_sem=recv_sems.at[direction, step],
            device_id=(source,) + rest,
            device_id_type=pl.DeviceIdType.MESH,
        )

    for step in range(count // 2):
        for direction in (0, 1):
            if step >= plans[direction][1]:
                continue
            if step > 0:
                arrival(direction, step - 1).wait_recv()
            copy = transfer(direction, step)
            copy.start()
            started.append(copy)
    for direction in (0, 1):
        arrival(direction, plans[direction][1] - 1).wait_recv()
    for copy in started:
        copy.wait_send()
    own.wait()


def ring_gather(x, after):
    count = lax.axis_size("pipe")
    steps = count // 2
    return pl.pallas_call(
        ring_gather_kernel,
        out_shape=jax.ShapeDtypeStruct((count,) + x.shape, x.dtype),
        in_specs=[pl.BlockSpec(memory_space=pl.ANY)] * 2,
        out_specs=pl.BlockSpec(memory_space=pl.ANY),
        scratch_shapes=[
            pltpu.SemaphoreType.DMA((2, steps)),
            pltpu.SemaphoreType.DMA((2, steps)),
            pltpu.SemaphoreType.DMA,
        ],
        compiler_params=pltpu.CompilerParams(collective_id=0, has_side_effects=True),
    )(x, after)


def ring_sum_kernel(part_ref, after_ref, out_ref, landing, outgoing, send_sems, recv_sems):
    del after_ref
    count = lax.axis_size("pipe")
    me = lax.axis_index("pipe")
    rest = tuple(lax.axis_index(name) for name in TOKEN_AXES[1:])
    right = lax.rem(me + 1, count)
    left = lax.rem(me + count - 1, count)
    lanes_count = landing.shape[0]
    piece = part_ref.shape[1] // lanes_count
    barrier = pltpu.get_barrier_semaphore()
    for peer in (left, right):
        pl.semaphore_signal(
            barrier, inc=1, device_id=(peer,) + rest, device_id_type=pl.DeviceIdType.MESH
        )
    pl.semaphore_wait(barrier, 2)
    rows = [pl.ds(k * piece, piece) for k in range(lanes_count)]

    def goes_right(k):
        return k % 2 == 0

    def chunk_at(k, step):
        if goes_right(k):
            return lax.rem(me - step - 1 + 2 * count, count)
        return lax.rem(me + step + 1, count)

    def copy(k, step, peer):
        return pltpu.make_async_remote_copy(
            src_ref=outgoing.at[k, step],
            dst_ref=landing.at[k, step],
            send_sem=send_sems.at[k, step],
            recv_sem=recv_sems.at[k, step],
            device_id=(peer,) + rest,
            device_id_type=pl.DeviceIdType.MESH,
        )

    def sender(k):
        return right if goes_right(k) else left

    def source(k):
        return left if goes_right(k) else right

    started = []
    for step in range(count - 1):
        for k in range(lanes_count):
            own = part_ref[chunk_at(k, step), rows[k], :].astype(jnp.float32)
            if step > 0:
                copy(k, step - 1, source(k)).wait_recv()
                own = own + landing[k, step - 1].astype(jnp.float32)
            outgoing[k, step] = own.astype(outgoing.dtype)
            sending = copy(k, step, sender(k))
            sending.start()
            started.append(sending)
    for k in range(lanes_count):
        copy(k, count - 2, source(k)).wait_recv()
        total = part_ref[me, rows[k], :].astype(jnp.float32)
        total = total + landing[k, count - 2].astype(jnp.float32)
        out_ref[rows[k], :] = total.astype(out_ref.dtype)
    for sending in started:
        sending.wait_send()


def ring_sum(parts, after):
    count = lax.axis_size("pipe")
    rows = parts.shape[0] // count
    parts = parts.reshape(count, rows, parts.shape[1])
    pieces = 14
    slot = (pieces, count - 1, rows // pieces, parts.shape[2])
    return pl.pallas_call(
        ring_sum_kernel,
        out_shape=jax.ShapeDtypeStruct((rows, parts.shape[2]), parts.dtype),
        in_specs=[
            pl.BlockSpec(memory_space=pltpu.VMEM),
            pl.BlockSpec(memory_space=pl.ANY),
        ],
        out_specs=pl.BlockSpec(memory_space=pltpu.VMEM),
        scratch_shapes=[
            pltpu.VMEM(slot, parts.dtype),
            pltpu.VMEM(slot, parts.dtype),
            pltpu.SemaphoreType.DMA(slot[:2]),
            pltpu.SemaphoreType.DMA(slot[:2]),
        ],
        compiler_params=pltpu.CompilerParams(collective_id=1, has_side_effects=True),
    )(parts, after)


def pair_sum_kernel(x_ref, out_ref, landing, send_sem, recv_sem):
    me = lax.axis_index("core")
    other = 1 - me
    head = tuple(lax.axis_index(name) for name in TOKEN_AXES[:3])
    partner = head + (other,)
    barrier = pltpu.get_barrier_semaphore()
    pl.semaphore_signal(
        barrier, inc=1, device_id=partner, device_id_type=pl.DeviceIdType.MESH
    )
    pl.semaphore_wait(barrier, 1)
    sending = pltpu.make_async_remote_copy(
        src_ref=x_ref.at[other],
        dst_ref=landing,
        send_sem=send_sem,
        recv_sem=recv_sem,
        device_id=partner,
        device_id_type=pl.DeviceIdType.MESH,
    )
    sending.start()
    sending.wait_recv()
    total = x_ref[me].astype(jnp.float32) + landing[...].astype(jnp.float32)
    out_ref[...] = total.astype(out_ref.dtype)
    sending.wait_send()


def pair_sum(x):
    return pl.pallas_call(
        pair_sum_kernel,
        out_shape=jax.ShapeDtypeStruct(x.shape[1:], x.dtype),
        in_specs=[pl.BlockSpec(memory_space=pltpu.VMEM)],
        out_specs=pl.BlockSpec(memory_space=pltpu.VMEM),
        scratch_shapes=[
            pltpu.VMEM(x.shape[1:], x.dtype),
            pltpu.SemaphoreType.DMA,
            pltpu.SemaphoreType.DMA,
        ],
        compiler_params=pltpu.CompilerParams(collective_id=2, has_side_effects=True),
    )(x)


def on_device(tokens, cotangent, expert_ids, gate_values, w_gate, w_up, w_down_t):
    micro_count, tok_count, d_model = tokens.shape
    top_count = expert_ids.shape[2]
    pipe_size = lax.axis_size("pipe")
    expert_size = lax.axis_size("ex") * lax.axis_size("ey") * lax.axis_size("core")
    capacity = CAP
    slot_total = EXPERTS * capacity
    highest_precision = lax.Precision.HIGHEST
    cols = w_gate.shape[1]
    routing_table = route_table(expert_ids, EXPERTS, capacity)
    routing_table_bfloat16 = routing_table.astype(jnp.bfloat16)
    lanes = 128
    flattened_gate = gate_values.reshape(micro_count, tok_count * top_count)
    payload = jnp.concatenate(
        [
            jnp.repeat(tokens, top_count, axis=1),
            jnp.repeat(cotangent, top_count, axis=1),
            jnp.broadcast_to(flattened_gate[:, :, None], flattened_gate.shape + (lanes,)),
        ],
        axis=2,
    )
    send = jnp.einsum(
        "egf,efh->egh", routing_table_bfloat16, payload, preferred_element_type=jnp.float32
    ).astype(jnp.bfloat16)
    width = payload.shape[2]
    block_rows = micro_count * capacity
    send = jnp.transpose(send.reshape(micro_count, EXPERTS, capacity, width), (1, 0, 2, 3))
    send = send.reshape(EXPERTS * block_rows, width)
    arrived = lax.all_to_all(send, "ex", split_axis=0, concat_axis=0, tiled=True)
    rows_all = lax.all_gather(arrived, SHARE, axis=0, tiled=True)
    w_local = jnp.concatenate([w_gate, w_up, w_down_t], axis=1)
    w_full = ring_gather(w_local, arrived).reshape(-1, w_local.shape[1])
    gate_full = w_full[:, :cols]
    up_full = w_full[:, cols : 2 * cols]
    down_full = w_full[:, 2 * cols :]
    row_count = rows_all.shape[0]
    share_count = row_count // arrived.shape[0]
    tok_rows = rows_all[:, :d_model]
    cot_rows = rows_all[:, d_model : 2 * d_model]
    gate_rows = rows_all[:, 2 * d_model : 2 * d_model + 1].astype(jnp.float32)
    pre_gate = jnp.dot(tok_rows, gate_full, preferred_element_type=jnp.float32)
    pre_up = jnp.dot(tok_rows, up_full, preferred_element_type=jnp.float32)
    back_proj = jnp.dot(cot_rows, down_full, preferred_element_type=jnp.float32)
    sigmoid_gate = jax.nn.sigmoid(pre_gate)
    activated = pre_gate * sigmoid_gate
    hidden = activated * pre_up
    gate_part = jnp.sum(back_proj * hidden, axis=1)
    scaled_hidden = (gate_rows * hidden).astype(jnp.bfloat16)
    d_hidden = gate_rows * back_proj
    d_pre_gate = (
        d_hidden * pre_up * sigmoid_gate * (1.0 + pre_gate * (1.0 - sigmoid_gate))
    ).astype(jnp.bfloat16)
    d_pre_up = (d_hidden * activated).astype(jnp.bfloat16)
    core_count = lax.axis_size("core")

    def core_major(rows):
        blocks = rows.reshape(row_count // (core_count * arrived.shape[0]), core_count, -1)
        return jnp.swapaxes(blocks, 0, 1).reshape(rows.shape)

    input_part = jnp.dot(core_major(d_pre_gate), gate_full.T, preferred_element_type=jnp.float32)
    input_part = input_part + jnp.dot(
        core_major(d_pre_up), up_full.T, preferred_element_type=jnp.float32
    )
    tokens_total = tok_count * pipe_size * expert_size
    grad_scale = 1.0 / math.sqrt(micro_count * tokens_total * top_count / EXPERTS)
    contract = (((0,), (0,)), ((), ()))
    part_gate = lax.dot_general(tok_rows, d_pre_gate, contract, preferred_element_type=jnp.float32)
    part_up = lax.dot_general(tok_rows, d_pre_up, contract, preferred_element_type=jnp.float32)
    part_down = lax.dot_general(
        cot_rows, scaled_hidden, contract, preferred_element_type=jnp.float32
    )
    me_share = lax.axis_index("ey") * lax.axis_size("core") + lax.axis_index("core")
    gate_high = gate_part.astype(jnp.bfloat16)
    gate_low = (gate_part - gate_high.astype(jnp.float32)).astype(jnp.bfloat16)
    lane = lax.broadcasted_iota(jnp.int32, (1, lanes), 1)
    gate_columns = jnp.where(lane == 2 * me_share, gate_high[:, None], 0).astype(jnp.bfloat16)
    gate_columns = jnp.where(lane == 2 * me_share + 1, gate_low[:, None], gate_columns)
    input_shares = jnp.concatenate(
        [input_part.astype(jnp.bfloat16), core_major(gate_columns)], axis=1
    )
    input_pair = pair_sum(input_shares.reshape(core_count, row_count // core_count, -1))
    input_mine = lax.psum_scatter(input_pair, "ey", scatter_dimension=0, tiled=True)
    summed = ring_sum(
        (jnp.concatenate([part_gate, part_up, part_down], 1) * grad_scale).astype(jnp.bfloat16),
        input_pair,
    ).astype(jnp.float32)
    hidden_width = gate_full.shape[1]
    dw_gate = summed[:, :hidden_width].astype(jnp.bfloat16)
    dw_up = summed[:, hidden_width : 2 * hidden_width].astype(jnp.bfloat16)
    dw_down_t = summed[:, 2 * hidden_width :].astype(jnp.bfloat16)
    back = lax.all_to_all(input_mine, "ex", 0, 0, tiled=True)
    back = jnp.transpose(back.reshape(EXPERTS, micro_count, capacity, back.shape[1]), (1, 0, 2, 3))
    back = back.reshape(micro_count, slot_total, back.shape[3])
    slot_input = back[:, :, :d_model].astype(jnp.float32)
    gate_split = back[:, :, d_model : d_model + 2 * share_count].astype(jnp.float32)
    gate_per_slot = jnp.sum(gate_split, axis=2)
    token_table = jnp.sum(
        routing_table.reshape(micro_count, slot_total, tok_count, top_count), axis=3
    )
    d_tokens = jnp.einsum(
        "msc,msd->mcd", token_table, slot_input, precision=highest_precision
    ).astype(jnp.bfloat16)
    gate_weight_gradient = jnp.einsum(
        "kxw,kx->kw", routing_table, gate_per_slot, precision=highest_precision
    ).reshape(micro_count, tok_count, top_count)
    return (d_tokens, gate_weight_gradient, dw_gate, dw_up, dw_down_t)


def solution(mesh):
    pipe_size, expert_size = mesh.devices.shape
    split = Mesh(
        np.asarray(mesh.devices).reshape(pipe_size, EXPERTS, expert_size // EXPERTS // 2, 2),
        TOKEN_AXES,
    )
    token_spec = P(None, TOKEN_AXES, None)
    weight_spec = P("pipe", ("ex", "ey", "core"))
    return jax.shard_map(
        on_device,
        mesh=split,
        in_specs=(token_spec,) * 4 + (weight_spec,) * 3,
        out_specs=(token_spec, token_spec) + (weight_spec,) * 3,
        check_vma=False,
    )
```

```python
import math

import jax
import jax.numpy as jnp
import numpy as np
from jax import lax
from jax.experimental import pallas as pl
from jax.experimental.pallas import tpu as pltpu
from jax.sharding import Mesh
from jax.sharding import PartitionSpec as P

EXPERTS = 4
CAP = 3
SHARE = ("ey", "core")
TOKEN_AXES = ("pipe", "ex", "ey", "core")


def route_table(expert_ids, expert_total, capacity):
    micro_count, tok_count, top_count = expert_ids.shape
    flat_ids = expert_ids.reshape(micro_count, tok_count * top_count)
    onehot = (
        flat_ids[:, :, None] == jnp.arange(expert_total, dtype=jnp.int32)[None, None, :]
    ).astype(jnp.int32)
    earlier = jnp.cumsum(onehot, axis=1) - onehot
    position = jnp.sum(earlier * onehot, axis=2)
    slot_index = flat_ids * capacity + position
    slot_ids = jnp.arange(expert_total * capacity, dtype=jnp.int32)
    return (slot_index[:, None, :] == slot_ids[None, :, None]).astype(jnp.float32)


def ring_gather_kernel(x_ref, after_ref, out_ref, send_sems, recv_sems, local_sem):
    del after_ref
    count = lax.axis_size("pipe")
    me = lax.axis_index("pipe")
    rest = tuple(lax.axis_index(name) for name in TOKEN_AXES[1:])
    right = lax.rem(me + 1, count)
    left = lax.rem(me + count - 1, count)
    barrier = pltpu.get_barrier_semaphore()
    for peer in (left, right):
        pl.semaphore_signal(
            barrier, inc=1, device_id=(peer,) + rest, device_id_type=pl.DeviceIdType.MESH
        )
    pl.semaphore_wait(barrier, 2)
    own = pltpu.make_async_copy(x_ref, out_ref.at[me], local_sem)
    own.start()
    plans = ((right, count // 2, lambda s: lax.rem(me - s + count, count)),
             (left, (count - 1) // 2, lambda s: lax.rem(me + s, count)))
    started = []

    def transfer(direction, step):
        peer, _, slab_of = plans[direction]
        slab = slab_of(step)
        return pltpu.make_async_remote_copy(
            src_ref=x_ref if step == 0 else out_ref.at[slab],
            dst_ref=out_ref.at[slab],
            send_sem=send_sems.at[direction, step],
            recv_sem=recv_sems.at[direction, step],
            device_id=(peer,) + rest,
            device_id_type=pl.DeviceIdType.MESH,
        )

    def arrival(direction, step):
        peer, _, slab_of = plans[direction]
        source = left if peer is right else right
        slab = lax.rem(slab_of(step + 1), count)
        return pltpu.make_async_remote_copy(
            src_ref=out_ref.at[slab],
            dst_ref=out_ref.at[slab],
            send_sem=send_sems.at[direction, step],
            recv_sem=recv_sems.at[direction, step],
            device_id=(source,) + rest,
            device_id_type=pl.DeviceIdType.MESH,
        )

    for step in range(count // 2):
        for direction in (0, 1):
            if step >= plans[direction][1]:
                continue
            if step > 0:
                arrival(direction, step - 1).wait_recv()
            copy = transfer(direction, step)
            copy.start()
            started.append(copy)
    for direction in (0, 1):
        arrival(direction, plans[direction][1] - 1).wait_recv()
    for copy in started:
        copy.wait_send()
    own.wait()


def ring_gather(x, after):
    count = lax.axis_size("pipe")
    steps = count // 2
    return pl.pallas_call(
        ring_gather_kernel,
        out_shape=jax.ShapeDtypeStruct((count,) + x.shape, x.dtype),
        in_specs=[pl.BlockSpec(memory_space=pl.ANY)] * 2,
        out_specs=pl.BlockSpec(memory_space=pl.ANY),
        scratch_shapes=[
            pltpu.SemaphoreType.DMA((2, steps)),
            pltpu.SemaphoreType.DMA((2, steps)),
            pltpu.SemaphoreType.DMA,
        ],
        compiler_params=pltpu.CompilerParams(collective_id=0, has_side_effects=True),
    )(x, after)


def ring_sum_kernel(part_ref, after_ref, out_ref, landing, outgoing, send_sems, recv_sems):
    del after_ref
    count = lax.axis_size("pipe")
    me = lax.axis_index("pipe")
    rest = tuple(lax.axis_index(name) for name in TOKEN_AXES[1:])
    right = lax.rem(me + 1, count)
    left = lax.rem(me + count - 1, count)
    lanes_count = landing.shape[0]
    piece = part_ref.shape[1] // lanes_count
    barrier = pltpu.get_barrier_semaphore()
    for peer in (left, right):
        pl.semaphore_signal(
            barrier, inc=1, device_id=(peer,) + rest, device_id_type=pl.DeviceIdType.MESH
        )
    pl.semaphore_wait(barrier, 2)
    rows = [pl.ds(k * piece, piece) for k in range(lanes_count)]

    def goes_right(k):
        return k % 2 == 0

    def chunk_at(k, step):
        if goes_right(k):
            return lax.rem(me - step - 1 + 2 * count, count)
        return lax.rem(me + step + 1, count)

    def copy(k, step, peer):
        return pltpu.make_async_remote_copy(
            src_ref=outgoing.at[k, step],
            dst_ref=landing.at[k, step],
            send_sem=send_sems.at[k, step],
            recv_sem=recv_sems.at[k, step],
            device_id=(peer,) + rest,
            device_id_type=pl.DeviceIdType.MESH,
        )

    def sender(k):
        return right if goes_right(k) else left

    def source(k):
        return left if goes_right(k) else right

    started = []
    for step in range(count - 1):
        for k in range(lanes_count):
            own = part_ref[chunk_at(k, step), rows[k], :].astype(jnp.float32)
            if step > 0:
                copy(k, step - 1, source(k)).wait_recv()
                own = own + landing[k, step - 1].astype(jnp.float32)
            outgoing[k, step] = own.astype(outgoing.dtype)
            sending = copy(k, step, sender(k))
            sending.start()
            started.append(sending)
    for k in range(lanes_count):
        copy(k, count - 2, source(k)).wait_recv()
        total = part_ref[me, rows[k], :].astype(jnp.float32)
        total = total + landing[k, count - 2].astype(jnp.float32)
        out_ref[rows[k], :] = total.astype(out_ref.dtype)
    for sending in started:
        sending.wait_send()


def ring_sum(parts, after):
    count = lax.axis_size("pipe")
    rows = parts.shape[0] // count
    parts = parts.reshape(count, rows, parts.shape[1])
    pieces = 14
    slot = (pieces, count - 1, rows // pieces, parts.shape[2])
    return pl.pallas_call(
        ring_sum_kernel,
        out_shape=jax.ShapeDtypeStruct((rows, parts.shape[2]), parts.dtype),
        in_specs=[
            pl.BlockSpec(memory_space=pltpu.VMEM),
            pl.BlockSpec(memory_space=pl.ANY),
        ],
        out_specs=pl.BlockSpec(memory_space=pltpu.VMEM),
        scratch_shapes=[
            pltpu.VMEM(slot, parts.dtype),
            pltpu.VMEM(slot, parts.dtype),
            pltpu.SemaphoreType.DMA(slot[:2]),
            pltpu.SemaphoreType.DMA(slot[:2]),
        ],
        compiler_params=pltpu.CompilerParams(collective_id=1, has_side_effects=True),
    )(parts, after)


def pair_sum_kernel(x_ref, out_ref, landing, mine, send_sem, recv_sem, local_sem):
    me = lax.axis_index("core")
    other = 1 - me
    head = tuple(lax.axis_index(name) for name in TOKEN_AXES[:3])
    partner = head + (other,)
    barrier = pltpu.get_barrier_semaphore()
    pl.semaphore_signal(
        barrier, inc=1, device_id=partner, device_id_type=pl.DeviceIdType.MESH
    )
    pl.semaphore_wait(barrier, 1)
    sending = pltpu.make_async_remote_copy(
        src_ref=x_ref.at[other],
        dst_ref=landing,
        send_sem=send_sem,
        recv_sem=recv_sem,
        device_id=partner,
        device_id_type=pl.DeviceIdType.MESH,
    )
    sending.start()
    own = pltpu.make_async_copy(x_ref.at[me], mine, local_sem)
    own.start()
    own.wait()
    sending.wait_recv()
    total = mine[...].astype(jnp.float32) + landing[...].astype(jnp.float32)
    out_ref[...] = total.astype(out_ref.dtype)
    sending.wait_send()


def pair_sum(x):
    return pl.pallas_call(
        pair_sum_kernel,
        out_shape=jax.ShapeDtypeStruct(x.shape[1:], x.dtype),
        in_specs=[pl.BlockSpec(memory_space=pl.ANY)],
        out_specs=pl.BlockSpec(memory_space=pltpu.VMEM),
        scratch_shapes=[
            pltpu.VMEM(x.shape[1:], x.dtype),
            pltpu.VMEM(x.shape[1:], x.dtype),
            pltpu.SemaphoreType.DMA,
            pltpu.SemaphoreType.DMA,
            pltpu.SemaphoreType.DMA,
        ],
        compiler_params=pltpu.CompilerParams(collective_id=2, has_side_effects=True),
    )(x)


def on_device(tokens, cotangent, expert_ids, gate_values, w_gate, w_up, w_down_t):
    micro_count, tok_count, d_model = tokens.shape
    top_count = expert_ids.shape[2]
    pipe_size = lax.axis_size("pipe")
    expert_size = lax.axis_size("ex") * lax.axis_size("ey") * lax.axis_size("core")
    capacity = CAP
    slot_total = EXPERTS * capacity
    highest_precision = lax.Precision.HIGHEST
    cols = w_gate.shape[1]
    routing_table = route_table(expert_ids, EXPERTS, capacity)
    routing_table_bfloat16 = routing_table.astype(jnp.bfloat16)
    lanes = 128
    flattened_gate = gate_values.reshape(micro_count, tok_count * top_count)
    payload = jnp.concatenate(
        [
            jnp.repeat(tokens, top_count, axis=1),
            jnp.repeat(cotangent, top_count, axis=1),
            jnp.broadcast_to(flattened_gate[:, :, None], flattened_gate.shape + (lanes,)),
        ],
        axis=2,
    )
    send = jnp.einsum(
        "egf,efh->egh", routing_table_bfloat16, payload, preferred_element_type=jnp.float32
    ).astype(jnp.bfloat16)
    width = payload.shape[2]
    block_rows = micro_count * capacity
    send = jnp.transpose(send.reshape(micro_count, EXPERTS, capacity, width), (1, 0, 2, 3))
    send = send.reshape(EXPERTS * block_rows, width)
    arrived = lax.all_to_all(send, "ex", split_axis=0, concat_axis=0, tiled=True)
    rows_all = lax.all_gather(arrived, SHARE, axis=0, tiled=True)
    w_local = jnp.concatenate([w_gate, w_up, w_down_t], axis=1)
    w_full = ring_gather(w_local, arrived).reshape(-1, w_local.shape[1])
    gate_full = w_full[:, :cols]
    up_full = w_full[:, cols : 2 * cols]
    down_full = w_full[:, 2 * cols :]
    row_count = rows_all.shape[0]
    share_count = row_count // arrived.shape[0]
    tok_rows = rows_all[:, :d_model]
    cot_rows = rows_all[:, d_model : 2 * d_model]
    gate_rows = rows_all[:, 2 * d_model : 2 * d_model + 1].astype(jnp.float32)
    pre_gate = jnp.dot(tok_rows, gate_full, preferred_element_type=jnp.float32)
    pre_up = jnp.dot(tok_rows, up_full, preferred_element_type=jnp.float32)
    back_proj = jnp.dot(cot_rows, down_full, preferred_element_type=jnp.float32)
    sigmoid_gate = jax.nn.sigmoid(pre_gate)
    activated = pre_gate * sigmoid_gate
    hidden = activated * pre_up
    gate_part = jnp.sum(back_proj * hidden, axis=1)
    scaled_hidden = (gate_rows * hidden).astype(jnp.bfloat16)
    d_hidden = gate_rows * back_proj
    d_pre_gate = (
        d_hidden * pre_up * sigmoid_gate * (1.0 + pre_gate * (1.0 - sigmoid_gate))
    ).astype(jnp.bfloat16)
    d_pre_up = (d_hidden * activated).astype(jnp.bfloat16)
    core_count = lax.axis_size("core")

    def core_major(rows):
        blocks = rows.reshape(row_count // (core_count * arrived.shape[0]), core_count, -1)
        return jnp.swapaxes(blocks, 0, 1).reshape(rows.shape)

    input_part = jnp.dot(core_major(d_pre_gate), gate_full.T, preferred_element_type=jnp.float32)
    input_part = input_part + jnp.dot(
        core_major(d_pre_up), up_full.T, preferred_element_type=jnp.float32
    )
    tokens_total = tok_count * pipe_size * expert_size
    grad_scale = 1.0 / math.sqrt(micro_count * tokens_total * top_count / EXPERTS)
    contract = (((0,), (0,)), ((), ()))
    part_gate = lax.dot_general(tok_rows, d_pre_gate, contract, preferred_element_type=jnp.float32)
    part_up = lax.dot_general(tok_rows, d_pre_up, contract, preferred_element_type=jnp.float32)
    part_down = lax.dot_general(
        cot_rows, scaled_hidden, contract, preferred_element_type=jnp.float32
    )
    me_share = lax.axis_index("ey") * lax.axis_size("core") + lax.axis_index("core")
    gate_high = gate_part.astype(jnp.bfloat16)
    gate_low = (gate_part - gate_high.astype(jnp.float32)).astype(jnp.bfloat16)
    lane = lax.broadcasted_iota(jnp.int32, (1, lanes), 1)
    gate_columns = jnp.where(lane == 2 * me_share, gate_high[:, None], 0).astype(jnp.bfloat16)
    gate_columns = jnp.where(lane == 2 * me_share + 1, gate_low[:, None], gate_columns)
    input_shares = jnp.concatenate(
        [input_part.astype(jnp.bfloat16), core_major(gate_columns)], axis=1
    )
    input_pair = pair_sum(input_shares.reshape(core_count, row_count // core_count, -1))
    input_mine = lax.psum_scatter(input_pair, "ey", scatter_dimension=0, tiled=True)
    summed = ring_sum(
        (jnp.concatenate([part_gate, part_up, part_down], 1) * grad_scale).astype(jnp.bfloat16),
        input_pair,
    ).astype(jnp.float32)
    hidden_width = gate_full.shape[1]
    dw_gate = summed[:, :hidden_width].astype(jnp.bfloat16)
    dw_up = summed[:, hidden_width : 2 * hidden_width].astype(jnp.bfloat16)
    dw_down_t = summed[:, 2 * hidden_width :].astype(jnp.bfloat16)
    back = lax.all_to_all(input_mine, "ex", 0, 0, tiled=True)
    back = jnp.transpose(back.reshape(EXPERTS, micro_count, capacity, back.shape[1]), (1, 0, 2, 3))
    back = back.reshape(micro_count, slot_total, back.shape[3])
    slot_input = back[:, :, :d_model].astype(jnp.float32)
    gate_split = back[:, :, d_model : d_model + 2 * share_count].astype(jnp.float32)
    gate_per_slot = jnp.sum(gate_split, axis=2)
    token_table = jnp.sum(
        routing_table.reshape(micro_count, slot_total, tok_count, top_count), axis=3
    )
    d_tokens = jnp.einsum(
        "msc,msd->mcd", token_table, slot_input, precision=highest_precision
    ).astype(jnp.bfloat16)
    gate_weight_gradient = jnp.einsum(
        "kxw,kx->kw", routing_table, gate_per_slot, precision=highest_precision
    ).reshape(micro_count, tok_count, top_count)
    return (d_tokens, gate_weight_gradient, dw_gate, dw_up, dw_down_t)


def solution(mesh):
    pipe_size, expert_size = mesh.devices.shape
    split = Mesh(
        np.asarray(mesh.devices).reshape(pipe_size, EXPERTS, expert_size // EXPERTS // 2, 2),
        TOKEN_AXES,
    )
    token_spec = P(None, TOKEN_AXES, None)
    weight_spec = P("pipe", ("ex", "ey", "core"))
    return jax.shard_map(
        on_device,
        mesh=split,
        in_specs=(token_spec,) * 4 + (weight_spec,) * 3,
        out_specs=(token_spec, token_spec) + (weight_spec,) * 3,
        check_vma=False,
    )
```

```python
import math

import jax
import jax.numpy as jnp
import numpy as np
from jax import lax
from jax.experimental import pallas as pl
from jax.experimental.pallas import tpu as pltpu
from jax.sharding import Mesh
from jax.sharding import PartitionSpec as P

EXPERTS = 4
CAP = 3
SHARE = ("ey", "core")
TOKEN_AXES = ("pipe", "ex", "ey", "core")


def route_table(expert_ids, expert_total, capacity):
    micro_count, tok_count, top_count = expert_ids.shape
    flat_ids = expert_ids.reshape(micro_count, tok_count * top_count)
    onehot = (
        flat_ids[:, :, None] == jnp.arange(expert_total, dtype=jnp.int32)[None, None, :]
    ).astype(jnp.int32)
    earlier = jnp.cumsum(onehot, axis=1) - onehot
    position = jnp.sum(earlier * onehot, axis=2)
    slot_index = flat_ids * capacity + position
    slot_ids = jnp.arange(expert_total * capacity, dtype=jnp.int32)
    return (slot_index[:, None, :] == slot_ids[None, :, None]).astype(jnp.float32)


def ring_gather_kernel(x_ref, after_ref, out_ref, send_sems, recv_sems, local_sem):
    del after_ref
    count = lax.axis_size("pipe")
    me = lax.axis_index("pipe")
    rest = tuple(lax.axis_index(name) for name in TOKEN_AXES[1:])
    right = lax.rem(me + 1, count)
    left = lax.rem(me + count - 1, count)
    barrier = pltpu.get_barrier_semaphore()
    for peer in (left, right):
        pl.semaphore_signal(
            barrier, inc=1, device_id=(peer,) + rest, device_id_type=pl.DeviceIdType.MESH
        )
    pl.semaphore_wait(barrier, 2)
    own = pltpu.make_async_copy(x_ref, out_ref.at[me], local_sem)
    own.start()
    plans = ((right, count // 2, lambda s: lax.rem(me - s + count, count)),
             (left, (count - 1) // 2, lambda s: lax.rem(me + s, count)))
    started = []

    def transfer(direction, step):
        peer, _, slab_of = plans[direction]
        slab = slab_of(step)
        return pltpu.make_async_remote_copy(
            src_ref=x_ref if step == 0 else out_ref.at[slab],
            dst_ref=out_ref.at[slab],
            send_sem=send_sems.at[direction, step],
            recv_sem=recv_sems.at[direction, step],
            device_id=(peer,) + rest,
            device_id_type=pl.DeviceIdType.MESH,
        )

    def arrival(direction, step):
        peer, _, slab_of = plans[direction]
        source = left if peer is right else right
        slab = lax.rem(slab_of(step + 1), count)
        return pltpu.make_async_remote_copy(
            src_ref=out_ref.at[slab],
            dst_ref=out_ref.at[slab],
            send_sem=send_sems.at[direction, step],
            recv_sem=recv_sems.at[direction, step],
            device_id=(source,) + rest,
            device_id_type=pl.DeviceIdType.MESH,
        )

    for step in range(count // 2):
        for direction in (0, 1):
            if step >= plans[direction][1]:
                continue
            if step > 0:
                arrival(direction, step - 1).wait_recv()
            copy = transfer(direction, step)
            copy.start()
            started.append(copy)
    for direction in (0, 1):
        arrival(direction, plans[direction][1] - 1).wait_recv()
    for copy in started:
        copy.wait_send()
    own.wait()


def ring_gather(x, after):
    count = lax.axis_size("pipe")
    steps = count // 2
    return pl.pallas_call(
        ring_gather_kernel,
        out_shape=jax.ShapeDtypeStruct((count,) + x.shape, x.dtype),
        in_specs=[pl.BlockSpec(memory_space=pl.ANY)] * 2,
        out_specs=pl.BlockSpec(memory_space=pl.ANY),
        scratch_shapes=[
            pltpu.SemaphoreType.DMA((2, steps)),
            pltpu.SemaphoreType.DMA((2, steps)),
            pltpu.SemaphoreType.DMA,
        ],
        compiler_params=pltpu.CompilerParams(collective_id=0, has_side_effects=True),
    )(x, after)


def ring_sum_kernel(part_ref, after_ref, out_ref, landing, outgoing, send_sems, recv_sems):
    del after_ref
    count = lax.axis_size("pipe")
    me = lax.axis_index("pipe")
    rest = tuple(lax.axis_index(name) for name in TOKEN_AXES[1:])
    right = lax.rem(me + 1, count)
    left = lax.rem(me + count - 1, count)
    lanes_count = landing.shape[0]
    piece = part_ref.shape[1] // lanes_count
    barrier = pltpu.get_barrier_semaphore()
    for peer in (left, right):
        pl.semaphore_signal(
            barrier, inc=1, device_id=(peer,) + rest, device_id_type=pl.DeviceIdType.MESH
        )
    pl.semaphore_wait(barrier, 2)
    rows = [pl.ds(k * piece, piece) for k in range(lanes_count)]

    def goes_right(k):
        return k % 2 == 0

    def chunk_at(k, step):
        if goes_right(k):
            return lax.rem(me - step - 1 + 2 * count, count)
        return lax.rem(me + step + 1, count)

    def copy(k, step, peer):
        return pltpu.make_async_remote_copy(
            src_ref=outgoing.at[k, step],
            dst_ref=landing.at[k, step],
            send_sem=send_sems.at[k, step],
            recv_sem=recv_sems.at[k, step],
            device_id=(peer,) + rest,
            device_id_type=pl.DeviceIdType.MESH,
        )

    def sender(k):
        return right if goes_right(k) else left

    def source(k):
        return left if goes_right(k) else right

    started = []
    for step in range(count - 1):
        for k in range(lanes_count):
            own = part_ref[chunk_at(k, step), rows[k], :].astype(jnp.float32)
            if step > 0:
                copy(k, step - 1, source(k)).wait_recv()
                own = own + landing[k, step - 1].astype(jnp.float32)
            outgoing[k, step] = own.astype(outgoing.dtype)
            sending = copy(k, step, sender(k))
            sending.start()
            started.append(sending)
    for k in range(lanes_count):
        copy(k, count - 2, source(k)).wait_recv()
        total = part_ref[me, rows[k], :].astype(jnp.float32)
        total = total + landing[k, count - 2].astype(jnp.float32)
        out_ref[rows[k], :] = total.astype(out_ref.dtype)
    for sending in started:
        sending.wait_send()


def ring_sum(parts, after):
    count = lax.axis_size("pipe")
    rows = parts.shape[0] // count
    parts = parts.reshape(count, rows, parts.shape[1])
    pieces = 14
    slot = (pieces, count - 1, rows // pieces, parts.shape[2])
    return pl.pallas_call(
        ring_sum_kernel,
        out_shape=jax.ShapeDtypeStruct((rows, parts.shape[2]), parts.dtype),
        in_specs=[
            pl.BlockSpec(memory_space=pltpu.VMEM),
            pl.BlockSpec(memory_space=pl.ANY),
        ],
        out_specs=pl.BlockSpec(memory_space=pltpu.VMEM),
        scratch_shapes=[
            pltpu.VMEM(slot, parts.dtype),
            pltpu.VMEM(slot, parts.dtype),
            pltpu.SemaphoreType.DMA(slot[:2]),
            pltpu.SemaphoreType.DMA(slot[:2]),
        ],
        compiler_params=pltpu.CompilerParams(collective_id=1, has_side_effects=True),
    )(parts, after)


def pair_sum_kernel(x_ref, out_ref, landing, mine, send_sem, recv_sem, local_sem):
    me = lax.axis_index("core")
    other = 1 - me
    head = tuple(lax.axis_index(name) for name in TOKEN_AXES[:3])
    partner = head + (other,)
    barrier = pltpu.get_barrier_semaphore()
    pl.semaphore_signal(
        barrier, inc=1, device_id=partner, device_id_type=pl.DeviceIdType.MESH
    )
    pl.semaphore_wait(barrier, 1)
    sending = pltpu.make_async_remote_copy(
        src_ref=x_ref.at[other],
        dst_ref=landing,
        send_sem=send_sem,
        recv_sem=recv_sem,
        device_id=partner,
        device_id_type=pl.DeviceIdType.MESH,
    )
    sending.start()
    own = pltpu.make_async_copy(x_ref.at[me], mine, local_sem)
    own.start()
    own.wait()
    sending.wait_recv()
    total = mine[...].astype(jnp.float32) + landing[...].astype(jnp.float32)
    out_ref[...] = total.astype(out_ref.dtype)
    sending.wait_send()


def pair_sum(x):
    return pl.pallas_call(
        pair_sum_kernel,
        out_shape=jax.ShapeDtypeStruct(x.shape[1:], x.dtype),
        in_specs=[pl.BlockSpec(memory_space=pl.ANY)],
        out_specs=pl.BlockSpec(memory_space=pltpu.VMEM),
        scratch_shapes=[
            pltpu.VMEM(x.shape[1:], x.dtype),
            pltpu.VMEM(x.shape[1:], x.dtype),
            pltpu.SemaphoreType.DMA,
            pltpu.SemaphoreType.DMA,
            pltpu.SemaphoreType.DMA,
        ],
        compiler_params=pltpu.CompilerParams(collective_id=2, has_side_effects=True),
    )(x)


def pair_gather_kernel(x_ref, out_ref, send_sem, recv_sem, local_sem):
    me = lax.axis_index("core")
    other = 1 - me
    partner = tuple(lax.axis_index(name) for name in TOKEN_AXES[:3]) + (other,)
    barrier = pltpu.get_barrier_semaphore()
    pl.semaphore_signal(
        barrier, inc=1, device_id=partner, device_id_type=pl.DeviceIdType.MESH
    )
    pl.semaphore_wait(barrier, 1)
    sending = pltpu.make_async_remote_copy(
        src_ref=x_ref,
        dst_ref=out_ref.at[me],
        send_sem=send_sem,
        recv_sem=recv_sem,
        device_id=partner,
        device_id_type=pl.DeviceIdType.MESH,
    )
    sending.start()
    own = pltpu.make_async_copy(x_ref, out_ref.at[me], local_sem)
    own.start()
    own.wait()
    pltpu.make_async_remote_copy(
        src_ref=x_ref,
        dst_ref=out_ref.at[other],
        send_sem=send_sem,
        recv_sem=recv_sem,
        device_id=partner,
        device_id_type=pl.DeviceIdType.MESH,
    ).wait_recv()
    sending.wait_send()


def pair_gather(x):
    return pl.pallas_call(
        pair_gather_kernel,
        out_shape=jax.ShapeDtypeStruct((2,) + x.shape, x.dtype),
        in_specs=[pl.BlockSpec(memory_space=pltpu.VMEM)],
        out_specs=pl.BlockSpec(memory_space=pltpu.VMEM),
        scratch_shapes=[pltpu.SemaphoreType.DMA] * 3,
        compiler_params=pltpu.CompilerParams(collective_id=3, has_side_effects=True),
    )(x)


def on_device(tokens, cotangent, expert_ids, gate_values, w_gate, w_up, w_down_t):
    micro_count, tok_count, d_model = tokens.shape
    top_count = expert_ids.shape[2]
    pipe_size = lax.axis_size("pipe")
    expert_size = lax.axis_size("ex") * lax.axis_size("ey") * lax.axis_size("core")
    capacity = CAP
    slot_total = EXPERTS * capacity
    highest_precision = lax.Precision.HIGHEST
    cols = w_gate.shape[1]
    routing_table = route_table(expert_ids, EXPERTS, capacity)
    routing_table_bfloat16 = routing_table.astype(jnp.bfloat16)
    lanes = 128
    flattened_gate = gate_values.reshape(micro_count, tok_count * top_count)
    payload = jnp.concatenate(
        [
            jnp.repeat(tokens, top_count, axis=1),
            jnp.repeat(cotangent, top_count, axis=1),
            jnp.broadcast_to(flattened_gate[:, :, None], flattened_gate.shape + (lanes,)),
        ],
        axis=2,
    )
    send = jnp.einsum(
        "egf,efh->egh", routing_table_bfloat16, payload, preferred_element_type=jnp.float32
    ).astype(jnp.bfloat16)
    width = payload.shape[2]
    block_rows = micro_count * capacity
    send = jnp.transpose(send.reshape(micro_count, EXPERTS, capacity, width), (1, 0, 2, 3))
    send = send.reshape(EXPERTS * block_rows, width)
    arrived = lax.all_to_all(send, "ex", split_axis=0, concat_axis=0, tiled=True)
    rows_all = pair_gather(lax.all_gather(arrived, "ey", axis=0, tiled=True))
    rows_all = rows_all.reshape(-1, rows_all.shape[2])
    w_local = jnp.concatenate([w_gate, w_up, w_down_t], axis=1)
    w_full = ring_gather(w_local, arrived).reshape(-1, w_local.shape[1])
    gate_full = w_full[:, :cols]
    up_full = w_full[:, cols : 2 * cols]
    down_full = w_full[:, 2 * cols :]
    row_count = rows_all.shape[0]
    share_count = row_count // arrived.shape[0]
    tok_rows = rows_all[:, :d_model]
    cot_rows = rows_all[:, d_model : 2 * d_model]
    gate_rows = rows_all[:, 2 * d_model : 2 * d_model + 1].astype(jnp.float32)
    pre_gate = jnp.dot(tok_rows, gate_full, preferred_element_type=jnp.float32)
    pre_up = jnp.dot(tok_rows, up_full, preferred_element_type=jnp.float32)
    back_proj = jnp.dot(cot_rows, down_full, preferred_element_type=jnp.float32)
    sigmoid_gate = jax.nn.sigmoid(pre_gate)
    activated = pre_gate * sigmoid_gate
    hidden = activated * pre_up
    gate_part = jnp.sum(back_proj * hidden, axis=1)
    scaled_hidden = (gate_rows * hidden).astype(jnp.bfloat16)
    d_hidden = gate_rows * back_proj
    d_pre_gate = (
        d_hidden * pre_up * sigmoid_gate * (1.0 + pre_gate * (1.0 - sigmoid_gate))
    ).astype(jnp.bfloat16)
    d_pre_up = (d_hidden * activated).astype(jnp.bfloat16)
    core_count = lax.axis_size("core")
    input_part = jnp.dot(d_pre_gate, gate_full.T, preferred_element_type=jnp.float32)
    input_part = input_part + jnp.dot(d_pre_up, up_full.T, preferred_element_type=jnp.float32)
    tokens_total = tok_count * pipe_size * expert_size
    grad_scale = 1.0 / math.sqrt(micro_count * tokens_total * top_count / EXPERTS)
    contract = (((0,), (0,)), ((), ()))
    part_gate = lax.dot_general(tok_rows, d_pre_gate, contract, preferred_element_type=jnp.float32)
    part_up = lax.dot_general(tok_rows, d_pre_up, contract, preferred_element_type=jnp.float32)
    part_down = lax.dot_general(
        cot_rows, scaled_hidden, contract, preferred_element_type=jnp.float32
    )
    me_share = lax.axis_index("core") * lax.axis_size("ey") + lax.axis_index("ey")
    gate_high = gate_part.astype(jnp.bfloat16)
    gate_low = (gate_part - gate_high.astype(jnp.float32)).astype(jnp.bfloat16)
    lane = lax.broadcasted_iota(jnp.int32, (1, lanes), 1)
    gate_columns = jnp.where(lane == 2 * me_share, gate_high[:, None], 0).astype(jnp.bfloat16)
    gate_columns = jnp.where(lane == 2 * me_share + 1, gate_low[:, None], gate_columns)
    input_shares = jnp.concatenate(
        [input_part.astype(jnp.bfloat16), gate_columns], axis=1
    )
    input_pair = pair_sum(input_shares.reshape(core_count, row_count // core_count, -1))
    input_mine = lax.psum_scatter(input_pair, "ey", scatter_dimension=0, tiled=True)
    summed = ring_sum(
        (jnp.concatenate([part_gate, part_up, part_down], 1) * grad_scale).astype(jnp.bfloat16),
        input_pair,
    ).astype(jnp.float32)
    hidden_width = gate_full.shape[1]
    dw_gate = summed[:, :hidden_width].astype(jnp.bfloat16)
    dw_up = summed[:, hidden_width : 2 * hidden_width].astype(jnp.bfloat16)
    dw_down_t = summed[:, 2 * hidden_width :].astype(jnp.bfloat16)
    back = lax.all_to_all(input_mine, "ex", 0, 0, tiled=True)
    back = jnp.transpose(back.reshape(EXPERTS, micro_count, capacity, back.shape[1]), (1, 0, 2, 3))
    back = back.reshape(micro_count, slot_total, back.shape[3])
    slot_input = back[:, :, :d_model].astype(jnp.float32)
    gate_split = back[:, :, d_model : d_model + 2 * share_count].astype(jnp.float32)
    gate_per_slot = jnp.sum(gate_split, axis=2)
    token_table = jnp.sum(
        routing_table.reshape(micro_count, slot_total, tok_count, top_count), axis=3
    )
    d_tokens = jnp.einsum(
        "msc,msd->mcd", token_table, slot_input, precision=highest_precision
    ).astype(jnp.bfloat16)
    gate_weight_gradient = jnp.einsum(
        "kxw,kx->kw", routing_table, gate_per_slot, precision=highest_precision
    ).reshape(micro_count, tok_count, top_count)
    return (d_tokens, gate_weight_gradient, dw_gate, dw_up, dw_down_t)


def solution(mesh):
    pipe_size, expert_size = mesh.devices.shape
    split = Mesh(
        np.asarray(mesh.devices).reshape(pipe_size, EXPERTS, expert_size // EXPERTS // 2, 2),
        TOKEN_AXES,
    )
    token_spec = P(None, TOKEN_AXES, None)
    weight_spec = P("pipe", ("ex", "ey", "core"))
    return jax.shard_map(
        on_device,
        mesh=split,
        in_specs=(token_spec,) * 4 + (weight_spec,) * 3,
        out_specs=(token_spec, token_spec) + (weight_spec,) * 3,
        check_vma=False,
    )
```

```python
import math

import jax
import jax.numpy as jnp
import numpy as np
from jax import lax
from jax.experimental import pallas as pl
from jax.experimental.pallas import tpu as pltpu
from jax.sharding import Mesh
from jax.sharding import PartitionSpec as P

EXPERTS = 4
CAP = 3
SHARE = ("ey", "core")
TOKEN_AXES = ("pipe", "ex", "ey", "core")


def route_table(expert_ids, expert_total, capacity):
    micro_count, tok_count, top_count = expert_ids.shape
    flat_ids = expert_ids.reshape(micro_count, tok_count * top_count)
    onehot = (
        flat_ids[:, :, None] == jnp.arange(expert_total, dtype=jnp.int32)[None, None, :]
    ).astype(jnp.int32)
    earlier = jnp.cumsum(onehot, axis=1) - onehot
    position = jnp.sum(earlier * onehot, axis=2)
    slot_index = flat_ids * capacity + position
    slot_ids = jnp.arange(expert_total * capacity, dtype=jnp.int32)
    return (slot_index[:, None, :] == slot_ids[None, :, None]).astype(jnp.float32)


def ring_gather_kernel(x_ref, after_ref, out_ref, send_sems, recv_sems, local_sem):
    del after_ref
    count = lax.axis_size("pipe")
    me = lax.axis_index("pipe")
    rest = tuple(lax.axis_index(name) for name in TOKEN_AXES[1:])
    right = lax.rem(me + 1, count)
    left = lax.rem(me + count - 1, count)
    barrier = pltpu.get_barrier_semaphore()
    for peer in (left, right):
        pl.semaphore_signal(
            barrier, inc=1, device_id=(peer,) + rest, device_id_type=pl.DeviceIdType.MESH
        )
    pl.semaphore_wait(barrier, 2)
    own = pltpu.make_async_copy(x_ref, out_ref.at[me], local_sem)
    own.start()
    plans = ((right, count // 2, lambda s: lax.rem(me - s + count, count)),
             (left, (count - 1) // 2, lambda s: lax.rem(me + s, count)))
    started = []

    def transfer(direction, step):
        peer, _, slab_of = plans[direction]
        slab = slab_of(step)
        return pltpu.make_async_remote_copy(
            src_ref=x_ref if step == 0 else out_ref.at[slab],
            dst_ref=out_ref.at[slab],
            send_sem=send_sems.at[direction, step],
            recv_sem=recv_sems.at[direction, step],
            device_id=(peer,) + rest,
            device_id_type=pl.DeviceIdType.MESH,
        )

    def arrival(direction, step):
        peer, _, slab_of = plans[direction]
        source = left if peer is right else right
        slab = lax.rem(slab_of(step + 1), count)
        return pltpu.make_async_remote_copy(
            src_ref=out_ref.at[slab],
            dst_ref=out_ref.at[slab],
            send_sem=send_sems.at[direction, step],
            recv_sem=recv_sems.at[direction, step],
            device_id=(source,) + rest,
            device_id_type=pl.DeviceIdType.MESH,
        )

    for step in range(count // 2):
        for direction in (0, 1):
            if step >= plans[direction][1]:
                continue
            if step > 0:
                arrival(direction, step - 1).wait_recv()
            copy = transfer(direction, step)
            copy.start()
            started.append(copy)
    for direction in (0, 1):
        arrival(direction, plans[direction][1] - 1).wait_recv()
    for copy in started:
        copy.wait_send()
    own.wait()


def ring_gather(x, after):
    count = lax.axis_size("pipe")
    steps = count // 2
    return pl.pallas_call(
        ring_gather_kernel,
        out_shape=jax.ShapeDtypeStruct((count,) + x.shape, x.dtype),
        in_specs=[pl.BlockSpec(memory_space=pl.ANY)] * 2,
        out_specs=pl.BlockSpec(memory_space=pl.ANY),
        scratch_shapes=[
            pltpu.SemaphoreType.DMA((2, steps)),
            pltpu.SemaphoreType.DMA((2, steps)),
            pltpu.SemaphoreType.DMA,
        ],
        compiler_params=pltpu.CompilerParams(collective_id=0, has_side_effects=True),
    )(x, after)


def ring_sum_kernel(part_ref, after_ref, out_ref, landing, outgoing, send_sems, recv_sems):
    del after_ref
    count = lax.axis_size("pipe")
    me = lax.axis_index("pipe")
    rest = tuple(lax.axis_index(name) for name in TOKEN_AXES[1:])
    right = lax.rem(me + 1, count)
    left = lax.rem(me + count - 1, count)
    lanes_count = landing.shape[0]
    piece = part_ref.shape[1] // lanes_count
    barrier = pltpu.get_barrier_semaphore()
    for peer in (left, right):
        pl.semaphore_signal(
            barrier, inc=1, device_id=(peer,) + rest, device_id_type=pl.DeviceIdType.MESH
        )
    pl.semaphore_wait(barrier, 2)
    rows = [pl.ds(k * piece, piece) for k in range(lanes_count)]

    def goes_right(k):
        return k % 2 == 0

    def chunk_at(k, step):
        if goes_right(k):
            return lax.rem(me - step - 1 + 2 * count, count)
        return lax.rem(me + step + 1, count)

    def copy(k, step, peer):
        return pltpu.make_async_remote_copy(
            src_ref=outgoing.at[k, step],
            dst_ref=landing.at[k, step],
            send_sem=send_sems.at[k, step],
            recv_sem=recv_sems.at[k, step],
            device_id=(peer,) + rest,
            device_id_type=pl.DeviceIdType.MESH,
        )

    def sender(k):
        return right if goes_right(k) else left

    def source(k):
        return left if goes_right(k) else right

    started = []
    for step in range(count - 1):
        for k in range(lanes_count):
            own = part_ref[chunk_at(k, step), rows[k], :].astype(jnp.float32)
            if step > 0:
                copy(k, step - 1, source(k)).wait_recv()
                own = own + landing[k, step - 1].astype(jnp.float32)
            outgoing[k, step] = own.astype(outgoing.dtype)
            sending = copy(k, step, sender(k))
            sending.start()
            started.append(sending)
    for k in range(lanes_count):
        copy(k, count - 2, source(k)).wait_recv()
        total = part_ref[me, rows[k], :].astype(jnp.float32)
        total = total + landing[k, count - 2].astype(jnp.float32)
        out_ref[rows[k], :] = total.astype(out_ref.dtype)
    for sending in started:
        sending.wait_send()


def ring_sum(parts, after):
    count = lax.axis_size("pipe")
    rows = parts.shape[0] // count
    parts = parts.reshape(count, rows, parts.shape[1])
    pieces = 28
    slot = (pieces, count - 1, rows // pieces, parts.shape[2])
    return pl.pallas_call(
        ring_sum_kernel,
        out_shape=jax.ShapeDtypeStruct((rows, parts.shape[2]), parts.dtype),
        in_specs=[
            pl.BlockSpec(memory_space=pltpu.VMEM),
            pl.BlockSpec(memory_space=pl.ANY),
        ],
        out_specs=pl.BlockSpec(memory_space=pltpu.VMEM),
        scratch_shapes=[
            pltpu.VMEM(slot, parts.dtype),
            pltpu.VMEM(slot, parts.dtype),
            pltpu.SemaphoreType.DMA(slot[:2]),
            pltpu.SemaphoreType.DMA(slot[:2]),
        ],
        compiler_params=pltpu.CompilerParams(collective_id=1, has_side_effects=True),
    )(parts, after)


def pair_sum_kernel(x_ref, out_ref, landing, mine, send_sem, recv_sem, local_sem):
    me = lax.axis_index("core")
    other = 1 - me
    head = tuple(lax.axis_index(name) for name in TOKEN_AXES[:3])
    partner = head + (other,)
    barrier = pltpu.get_barrier_semaphore()
    pl.semaphore_signal(
        barrier, inc=1, device_id=partner, device_id_type=pl.DeviceIdType.MESH
    )
    pl.semaphore_wait(barrier, 1)
    sending = pltpu.make_async_remote_copy(
        src_ref=x_ref.at[other],
        dst_ref=landing,
        send_sem=send_sem,
        recv_sem=recv_sem,
        device_id=partner,
        device_id_type=pl.DeviceIdType.MESH,
    )
    sending.start()
    own = pltpu.make_async_copy(x_ref.at[me], mine, local_sem)
    own.start()
    own.wait()
    sending.wait_recv()
    total = mine[...].astype(jnp.float32) + landing[...].astype(jnp.float32)
    out_ref[...] = total.astype(out_ref.dtype)
    sending.wait_send()


def pair_sum(x):
    return pl.pallas_call(
        pair_sum_kernel,
        out_shape=jax.ShapeDtypeStruct(x.shape[1:], x.dtype),
        in_specs=[pl.BlockSpec(memory_space=pl.ANY)],
        out_specs=pl.BlockSpec(memory_space=pltpu.VMEM),
        scratch_shapes=[
            pltpu.VMEM(x.shape[1:], x.dtype),
            pltpu.VMEM(x.shape[1:], x.dtype),
            pltpu.SemaphoreType.DMA,
            pltpu.SemaphoreType.DMA,
            pltpu.SemaphoreType.DMA,
        ],
        compiler_params=pltpu.CompilerParams(collective_id=2, has_side_effects=True),
    )(x)


def on_device(tokens, cotangent, expert_ids, gate_values, w_gate, w_up, w_down_t):
    micro_count, tok_count, d_model = tokens.shape
    top_count = expert_ids.shape[2]
    pipe_size = lax.axis_size("pipe")
    expert_size = lax.axis_size("ex") * lax.axis_size("ey") * lax.axis_size("core")
    capacity = CAP
    slot_total = EXPERTS * capacity
    highest_precision = lax.Precision.HIGHEST
    cols = w_gate.shape[1]
    routing_table = route_table(expert_ids, EXPERTS, capacity)
    routing_table_bfloat16 = routing_table.astype(jnp.bfloat16)
    lanes = 128
    flattened_gate = gate_values.reshape(micro_count, tok_count * top_count)
    payload = jnp.concatenate(
        [
            jnp.repeat(tokens, top_count, axis=1),
            jnp.repeat(cotangent, top_count, axis=1),
            jnp.broadcast_to(flattened_gate[:, :, None], flattened_gate.shape + (lanes,)),
        ],
        axis=2,
    )
    send = jnp.einsum(
        "egf,efh->egh", routing_table_bfloat16, payload, preferred_element_type=jnp.float32
    ).astype(jnp.bfloat16)
    width = payload.shape[2]
    block_rows = micro_count * capacity
    send = jnp.transpose(send.reshape(micro_count, EXPERTS, capacity, width), (1, 0, 2, 3))
    send = send.reshape(EXPERTS * block_rows, width)
    arrived = lax.all_to_all(send, "ex", split_axis=0, concat_axis=0, tiled=True)
    rows_all = lax.all_gather(arrived, SHARE, axis=0, tiled=True)
    w_local = jnp.concatenate([w_gate, w_up, w_down_t], axis=1)
    w_full = ring_gather(w_local, arrived).reshape(-1, w_local.shape[1])
    gate_full = w_full[:, :cols]
    up_full = w_full[:, cols : 2 * cols]
    down_full = w_full[:, 2 * cols :]
    row_count = rows_all.shape[0]
    share_count = row_count // arrived.shape[0]
    tok_rows = rows_all[:, :d_model]
    cot_rows = rows_all[:, d_model : 2 * d_model]
    gate_rows = rows_all[:, 2 * d_model : 2 * d_model + 1].astype(jnp.float32)
    pre_gate = jnp.dot(tok_rows, gate_full, preferred_element_type=jnp.float32)
    pre_up = jnp.dot(tok_rows, up_full, preferred_element_type=jnp.float32)
    back_proj = jnp.dot(cot_rows, down_full, preferred_element_type=jnp.float32)
    sigmoid_gate = jax.nn.sigmoid(pre_gate)
    activated = pre_gate * sigmoid_gate
    hidden = activated * pre_up
    gate_part = jnp.sum(back_proj * hidden, axis=1)
    scaled_hidden = (gate_rows * hidden).astype(jnp.bfloat16)
    d_hidden = gate_rows * back_proj
    d_pre_gate = (
        d_hidden * pre_up * sigmoid_gate * (1.0 + pre_gate * (1.0 - sigmoid_gate))
    ).astype(jnp.bfloat16)
    d_pre_up = (d_hidden * activated).astype(jnp.bfloat16)
    core_count = lax.axis_size("core")

    def core_major(rows):
        blocks = rows.reshape(row_count // (core_count * arrived.shape[0]), core_count, -1)
        return jnp.swapaxes(blocks, 0, 1).reshape(rows.shape)

    input_part = jnp.dot(core_major(d_pre_gate), gate_full.T, preferred_element_type=jnp.float32)
    input_part = input_part + jnp.dot(
        core_major(d_pre_up), up_full.T, preferred_element_type=jnp.float32
    )
    tokens_total = tok_count * pipe_size * expert_size
    grad_scale = 1.0 / math.sqrt(micro_count * tokens_total * top_count / EXPERTS)
    contract = (((0,), (0,)), ((), ()))
    part_gate = lax.dot_general(tok_rows, d_pre_gate, contract, preferred_element_type=jnp.float32)
    part_up = lax.dot_general(tok_rows, d_pre_up, contract, preferred_element_type=jnp.float32)
    part_down = lax.dot_general(
        cot_rows, scaled_hidden, contract, preferred_element_type=jnp.float32
    )
    me_share = lax.axis_index("ey") * lax.axis_size("core") + lax.axis_index("core")
    gate_high = gate_part.astype(jnp.bfloat16)
    gate_low = (gate_part - gate_high.astype(jnp.float32)).astype(jnp.bfloat16)
    lane = lax.broadcasted_iota(jnp.int32, (1, lanes), 1)
    gate_columns = jnp.where(lane == 2 * me_share, gate_high[:, None], 0).astype(jnp.bfloat16)
    gate_columns = jnp.where(lane == 2 * me_share + 1, gate_low[:, None], gate_columns)
    input_shares = jnp.concatenate(
        [input_part.astype(jnp.bfloat16), core_major(gate_columns)], axis=1
    )
    input_pair = pair_sum(input_shares.reshape(core_count, row_count // core_count, -1))
    input_mine = lax.psum_scatter(input_pair, "ey", scatter_dimension=0, tiled=True)
    summed = ring_sum(
        (jnp.concatenate([part_gate, part_up, part_down], 1) * grad_scale).astype(jnp.bfloat16),
        input_pair,
    ).astype(jnp.float32)
    hidden_width = gate_full.shape[1]
    dw_gate = summed[:, :hidden_width].astype(jnp.bfloat16)
    dw_up = summed[:, hidden_width : 2 * hidden_width].astype(jnp.bfloat16)
    dw_down_t = summed[:, 2 * hidden_width :].astype(jnp.bfloat16)
    back = lax.all_to_all(input_mine, "ex", 0, 0, tiled=True)
    back = jnp.transpose(back.reshape(EXPERTS, micro_count, capacity, back.shape[1]), (1, 0, 2, 3))
    back = back.reshape(micro_count, slot_total, back.shape[3])
    slot_input = back[:, :, :d_model].astype(jnp.float32)
    gate_split = back[:, :, d_model : d_model + 2 * share_count].astype(jnp.float32)
    gate_per_slot = jnp.sum(gate_split, axis=2)
    token_table = jnp.sum(
        routing_table.reshape(micro_count, slot_total, tok_count, top_count), axis=3
    )
    d_tokens = jnp.einsum(
        "msc,msd->mcd", token_table, slot_input, precision=highest_precision
    ).astype(jnp.bfloat16)
    gate_weight_gradient = jnp.einsum(
        "kxw,kx->kw", routing_table, gate_per_slot, precision=highest_precision
    ).reshape(micro_count, tok_count, top_count)
    return (d_tokens, gate_weight_gradient, dw_gate, dw_up, dw_down_t)


def solution(mesh):
    pipe_size, expert_size = mesh.devices.shape
    split = Mesh(
        np.asarray(mesh.devices).reshape(pipe_size, EXPERTS, expert_size // EXPERTS // 2, 2),
        TOKEN_AXES,
    )
    token_spec = P(None, TOKEN_AXES, None)
    weight_spec = P("pipe", ("ex", "ey", "core"))
    return jax.shard_map(
        on_device,
        mesh=split,
        in_specs=(token_spec,) * 4 + (weight_spec,) * 3,
        out_specs=(token_spec, token_spec) + (weight_spec,) * 3,
        check_vma=False,
    )
```

```python
import math

import jax
import jax.numpy as jnp
import numpy as np
from jax import lax
from jax.experimental import pallas as pl
from jax.experimental.pallas import tpu as pltpu
from jax.sharding import Mesh
from jax.sharding import PartitionSpec as P

EXPERTS = 4
CAP = 3
SHARE = ("ey", "core")
TOKEN_AXES = ("pipe", "ex", "ey", "core")


def route_table(expert_ids, expert_total, capacity):
    micro_count, tok_count, top_count = expert_ids.shape
    flat_ids = expert_ids.reshape(micro_count, tok_count * top_count)
    onehot = (
        flat_ids[:, :, None] == jnp.arange(expert_total, dtype=jnp.int32)[None, None, :]
    ).astype(jnp.int32)
    earlier = jnp.cumsum(onehot, axis=1) - onehot
    position = jnp.sum(earlier * onehot, axis=2)
    slot_index = flat_ids * capacity + position
    slot_ids = jnp.arange(expert_total * capacity, dtype=jnp.int32)
    return (slot_index[:, None, :] == slot_ids[None, :, None]).astype(jnp.float32)


def ring_gather_kernel(x_ref, after_ref, out_ref, send_sems, recv_sems, local_sem):
    del after_ref
    count = lax.axis_size("pipe")
    me = lax.axis_index("pipe")
    rest = tuple(lax.axis_index(name) for name in TOKEN_AXES[1:])
    right = lax.rem(me + 1, count)
    left = lax.rem(me + count - 1, count)
    barrier = pltpu.get_barrier_semaphore()
    for peer in (left, right):
        pl.semaphore_signal(
            barrier, inc=1, device_id=(peer,) + rest, device_id_type=pl.DeviceIdType.MESH
        )
    pl.semaphore_wait(barrier, 2)
    own = pltpu.make_async_copy(x_ref, out_ref.at[me], local_sem)
    own.start()
    plans = ((right, count // 2, lambda s: lax.rem(me - s + count, count)),
             (left, (count - 1) // 2, lambda s: lax.rem(me + s, count)))
    started = []

    def transfer(direction, step):
        peer, _, slab_of = plans[direction]
        slab = slab_of(step)
        return pltpu.make_async_remote_copy(
            src_ref=x_ref if step == 0 else out_ref.at[slab],
            dst_ref=out_ref.at[slab],
            send_sem=send_sems.at[direction, step],
            recv_sem=recv_sems.at[direction, step],
            device_id=(peer,) + rest,
            device_id_type=pl.DeviceIdType.MESH,
        )

    def arrival(direction, step):
        peer, _, slab_of = plans[direction]
        source = left if peer is right else right
        slab = lax.rem(slab_of(step + 1), count)
        return pltpu.make_async_remote_copy(
            src_ref=out_ref.at[slab],
            dst_ref=out_ref.at[slab],
            send_sem=send_sems.at[direction, step],
            recv_sem=recv_sems.at[direction, step],
            device_id=(source,) + rest,
            device_id_type=pl.DeviceIdType.MESH,
        )

    for step in range(count // 2):
        for direction in (0, 1):
            if step >= plans[direction][1]:
                continue
            if step > 0:
                arrival(direction, step - 1).wait_recv()
            copy = transfer(direction, step)
            copy.start()
            started.append(copy)
    for direction in (0, 1):
        arrival(direction, plans[direction][1] - 1).wait_recv()
    for copy in started:
        copy.wait_send()
    own.wait()


def ring_gather(x, after):
    count = lax.axis_size("pipe")
    steps = count // 2
    return pl.pallas_call(
        ring_gather_kernel,
        out_shape=jax.ShapeDtypeStruct((count,) + x.shape, x.dtype),
        in_specs=[pl.BlockSpec(memory_space=pl.ANY)] * 2,
        out_specs=pl.BlockSpec(memory_space=pl.ANY),
        scratch_shapes=[
            pltpu.SemaphoreType.DMA((2, steps)),
            pltpu.SemaphoreType.DMA((2, steps)),
            pltpu.SemaphoreType.DMA,
        ],
        compiler_params=pltpu.CompilerParams(collective_id=0, has_side_effects=True),
    )(x, after)


def ring_sum_kernel(part_ref, after_ref, out_ref, landing, outgoing, send_sems, recv_sems):
    del after_ref
    count = lax.axis_size("pipe")
    me = lax.axis_index("pipe")
    rest = tuple(lax.axis_index(name) for name in TOKEN_AXES[1:])
    right = lax.rem(me + 1, count)
    left = lax.rem(me + count - 1, count)
    lanes_count = landing.shape[0]
    piece = part_ref.shape[1] // lanes_count
    barrier = pltpu.get_barrier_semaphore()
    for peer in (left, right):
        pl.semaphore_signal(
            barrier, inc=1, device_id=(peer,) + rest, device_id_type=pl.DeviceIdType.MESH
        )
    pl.semaphore_wait(barrier, 2)
    rows = [pl.ds(k * piece, piece) for k in range(lanes_count)]

    def goes_right(k):
        return k % 2 == 0

    def chunk_at(k, step):
        if goes_right(k):
            return lax.rem(me - step - 1 + 2 * count, count)
        return lax.rem(me + step + 1, count)

    def copy(k, step, peer):
        return pltpu.make_async_remote_copy(
            src_ref=outgoing.at[k, step],
            dst_ref=landing.at[k, step],
            send_sem=send_sems.at[k, step],
            recv_sem=recv_sems.at[k, step],
            device_id=(peer,) + rest,
            device_id_type=pl.DeviceIdType.MESH,
        )

    def sender(k):
        return right if goes_right(k) else left

    def source(k):
        return left if goes_right(k) else right

    started = []
    for step in range(count - 1):
        for k in range(lanes_count):
            own = part_ref[chunk_at(k, step), rows[k], :].astype(jnp.float32)
            if step > 0:
                copy(k, step - 1, source(k)).wait_recv()
                own = own + landing[k, step - 1].astype(jnp.float32)
            outgoing[k, step] = own.astype(outgoing.dtype)
            sending = copy(k, step, sender(k))
            sending.start()
            started.append(sending)
    for k in range(lanes_count):
        copy(k, count - 2, source(k)).wait_recv()
        total = part_ref[me, rows[k], :].astype(jnp.float32)
        total = total + landing[k, count - 2].astype(jnp.float32)
        out_ref[rows[k], :] = total.astype(out_ref.dtype)
    for sending in started:
        sending.wait_send()


def ring_sum(parts, after):
    count = lax.axis_size("pipe")
    rows = parts.shape[0] // count
    parts = parts.reshape(count, rows, parts.shape[1])
    pieces = 14
    slot = (pieces, count - 1, rows // pieces, parts.shape[2])
    return pl.pallas_call(
        ring_sum_kernel,
        out_shape=jax.ShapeDtypeStruct((rows, parts.shape[2]), parts.dtype),
        in_specs=[
            pl.BlockSpec(memory_space=pltpu.VMEM),
            pl.BlockSpec(memory_space=pl.ANY),
        ],
        out_specs=pl.BlockSpec(memory_space=pltpu.VMEM),
        scratch_shapes=[
            pltpu.VMEM(slot, parts.dtype),
            pltpu.VMEM(slot, parts.dtype),
            pltpu.SemaphoreType.DMA(slot[:2]),
            pltpu.SemaphoreType.DMA(slot[:2]),
        ],
        compiler_params=pltpu.CompilerParams(collective_id=1, has_side_effects=True),
    )(parts, after)


def pair_sum_kernel(x_ref, out_ref, landing, mine, send_sem, recv_sem, local_sem):
    me = lax.axis_index("core")
    other = 1 - me
    head = tuple(lax.axis_index(name) for name in TOKEN_AXES[:3])
    partner = head + (other,)
    barrier = pltpu.get_barrier_semaphore()
    pl.semaphore_signal(
        barrier, inc=1, device_id=partner, device_id_type=pl.DeviceIdType.MESH
    )
    pl.semaphore_wait(barrier, 1)
    sending = pltpu.make_async_remote_copy(
        src_ref=x_ref.at[other],
        dst_ref=landing,
        send_sem=send_sem,
        recv_sem=recv_sem,
        device_id=partner,
        device_id_type=pl.DeviceIdType.MESH,
    )
    sending.start()
    own = pltpu.make_async_copy(x_ref.at[me], mine, local_sem)
    own.start()
    own.wait()
    sending.wait_recv()
    total = mine[...].astype(jnp.float32) + landing[...].astype(jnp.float32)
    out_ref[...] = total.astype(out_ref.dtype)
    sending.wait_send()


def pair_sum(x):
    return pl.pallas_call(
        pair_sum_kernel,
        out_shape=jax.ShapeDtypeStruct(x.shape[1:], x.dtype),
        in_specs=[pl.BlockSpec(memory_space=pl.ANY)],
        out_specs=pl.BlockSpec(memory_space=pltpu.VMEM),
        scratch_shapes=[
            pltpu.VMEM(x.shape[1:], x.dtype),
            pltpu.VMEM(x.shape[1:], x.dtype),
            pltpu.SemaphoreType.DMA,
            pltpu.SemaphoreType.DMA,
            pltpu.SemaphoreType.DMA,
        ],
        compiler_params=pltpu.CompilerParams(collective_id=2, has_side_effects=True),
    )(x)


def on_device(tokens, cotangent, expert_ids, gate_values, w_gate, w_up, w_down_t):
    micro_count, tok_count, d_model = tokens.shape
    top_count = expert_ids.shape[2]
    pipe_size = lax.axis_size("pipe")
    expert_size = lax.axis_size("ex") * lax.axis_size("ey") * lax.axis_size("core")
    capacity = CAP
    slot_total = EXPERTS * capacity
    highest_precision = lax.Precision.HIGHEST
    cols = w_gate.shape[1]
    routing_table = route_table(expert_ids, EXPERTS, capacity)
    routing_table_bfloat16 = routing_table.astype(jnp.bfloat16)
    lanes = 128
    flattened_gate = gate_values.reshape(micro_count, tok_count * top_count)
    token_table = jnp.sum(
        routing_table.reshape(micro_count, slot_total, tok_count, top_count), axis=3
    )
    rows_sent = jnp.einsum(
        "mst,mtd->msd",
        token_table.astype(jnp.bfloat16),
        jnp.concatenate([tokens, cotangent], axis=2),
        preferred_element_type=jnp.float32,
    ).astype(jnp.bfloat16)
    gate_sent = jnp.einsum(
        "msr,mr->ms", routing_table_bfloat16, flattened_gate, preferred_element_type=jnp.float32
    ).astype(jnp.bfloat16)
    send = jnp.concatenate(
        [rows_sent, jnp.broadcast_to(gate_sent[:, :, None], gate_sent.shape + (lanes,))], axis=2
    )
    width = send.shape[2]
    block_rows = micro_count * capacity
    send = jnp.transpose(send.reshape(micro_count, EXPERTS, capacity, width), (1, 0, 2, 3))
    send = send.reshape(EXPERTS * block_rows, width)
    arrived = lax.all_to_all(send, "ex", split_axis=0, concat_axis=0, tiled=True)
    rows_all = lax.all_gather(arrived, SHARE, axis=0, tiled=True)
    w_local = jnp.concatenate([w_gate, w_up, w_down_t], axis=1)
    w_full = ring_gather(w_local, arrived).reshape(-1, w_local.shape[1])
    gate_full = w_full[:, :cols]
    up_full = w_full[:, cols : 2 * cols]
    down_full = w_full[:, 2 * cols :]
    row_count = rows_all.shape[0]
    share_count = row_count // arrived.shape[0]
    tok_rows = rows_all[:, :d_model]
    cot_rows = rows_all[:, d_model : 2 * d_model]
    gate_rows = rows_all[:, 2 * d_model : 2 * d_model + 1].astype(jnp.float32)
    pre_gate = jnp.dot(tok_rows, gate_full, preferred_element_type=jnp.float32)
    pre_up = jnp.dot(tok_rows, up_full, preferred_element_type=jnp.float32)
    back_proj = jnp.dot(cot_rows, down_full, preferred_element_type=jnp.float32)
    sigmoid_gate = jax.nn.sigmoid(pre_gate)
    activated = pre_gate * sigmoid_gate
    hidden = activated * pre_up
    gate_part = jnp.sum(back_proj * hidden, axis=1)
    scaled_hidden = (gate_rows * hidden).astype(jnp.bfloat16)
    d_hidden = gate_rows * back_proj
    d_pre_gate = (
        d_hidden * pre_up * sigmoid_gate * (1.0 + pre_gate * (1.0 - sigmoid_gate))
    ).astype(jnp.bfloat16)
    d_pre_up = (d_hidden * activated).astype(jnp.bfloat16)
    core_count = lax.axis_size("core")

    def core_major(rows):
        blocks = rows.reshape(row_count // (core_count * arrived.shape[0]), core_count, -1)
        return jnp.swapaxes(blocks, 0, 1).reshape(rows.shape)

    input_part = jnp.dot(core_major(d_pre_gate), gate_full.T, preferred_element_type=jnp.float32)
    input_part = input_part + jnp.dot(
        core_major(d_pre_up), up_full.T, preferred_element_type=jnp.float32
    )
    tokens_total = tok_count * pipe_size * expert_size
    grad_scale = 1.0 / math.sqrt(micro_count * tokens_total * top_count / EXPERTS)
    contract = (((0,), (0,)), ((), ()))
    part_gate = lax.dot_general(tok_rows, d_pre_gate, contract, preferred_element_type=jnp.float32)
    part_up = lax.dot_general(tok_rows, d_pre_up, contract, preferred_element_type=jnp.float32)
    part_down = lax.dot_general(
        cot_rows, scaled_hidden, contract, preferred_element_type=jnp.float32
    )
    me_share = lax.axis_index("ey") * lax.axis_size("core") + lax.axis_index("core")
    gate_high = gate_part.astype(jnp.bfloat16)
    gate_low = (gate_part - gate_high.astype(jnp.float32)).astype(jnp.bfloat16)
    lane = lax.broadcasted_iota(jnp.int32, (1, lanes), 1)
    gate_columns = jnp.where(lane == 2 * me_share, gate_high[:, None], 0).astype(jnp.bfloat16)
    gate_columns = jnp.where(lane == 2 * me_share + 1, gate_low[:, None], gate_columns)
    input_shares = jnp.concatenate(
        [input_part.astype(jnp.bfloat16), core_major(gate_columns)], axis=1
    )
    input_pair = pair_sum(input_shares.reshape(core_count, row_count // core_count, -1))
    input_mine = lax.psum_scatter(input_pair, "ey", scatter_dimension=0, tiled=True)
    summed = ring_sum(
        (jnp.concatenate([part_gate, part_up, part_down], 1) * grad_scale).astype(jnp.bfloat16),
        input_pair,
    ).astype(jnp.float32)
    hidden_width = gate_full.shape[1]
    dw_gate = summed[:, :hidden_width].astype(jnp.bfloat16)
    dw_up = summed[:, hidden_width : 2 * hidden_width].astype(jnp.bfloat16)
    dw_down_t = summed[:, 2 * hidden_width :].astype(jnp.bfloat16)
    back = lax.all_to_all(input_mine, "ex", 0, 0, tiled=True)
    back = jnp.transpose(back.reshape(EXPERTS, micro_count, capacity, back.shape[1]), (1, 0, 2, 3))
    back = back.reshape(micro_count, slot_total, back.shape[3])
    slot_input = back[:, :, :d_model].astype(jnp.float32)
    gate_split = back[:, :, d_model : d_model + 2 * share_count].astype(jnp.float32)
    gate_per_slot = jnp.sum(gate_split, axis=2)
    d_tokens = jnp.einsum(
        "msc,msd->mcd", token_table, slot_input, precision=highest_precision
    ).astype(jnp.bfloat16)
    gate_weight_gradient = jnp.einsum(
        "kxw,kx->kw", routing_table, gate_per_slot, precision=highest_precision
    ).reshape(micro_count, tok_count, top_count)
    return (d_tokens, gate_weight_gradient, dw_gate, dw_up, dw_down_t)


def solution(mesh):
    pipe_size, expert_size = mesh.devices.shape
    split = Mesh(
        np.asarray(mesh.devices).reshape(pipe_size, EXPERTS, expert_size // EXPERTS // 2, 2),
        TOKEN_AXES,
    )
    token_spec = P(None, TOKEN_AXES, None)
    weight_spec = P("pipe", ("ex", "ey", "core"))
    return jax.shard_map(
        on_device,
        mesh=split,
        in_specs=(token_spec,) * 4 + (weight_spec,) * 3,
        out_specs=(token_spec, token_spec) + (weight_spec,) * 3,
        check_vma=False,
    )
```

```python
import math

import jax
import jax.numpy as jnp
import numpy as np
from jax import lax
from jax.experimental import pallas as pl
from jax.experimental.pallas import tpu as pltpu
from jax.sharding import Mesh
from jax.sharding import PartitionSpec as P

EXPERTS = 4
CAP = 3
SHARE = ("ey", "core")
TOKEN_AXES = ("pipe", "ex", "ey", "core")


def route_table(expert_ids, expert_total, capacity):
    micro_count, tok_count, top_count = expert_ids.shape
    flat_ids = expert_ids.reshape(micro_count, tok_count * top_count)
    onehot = (
        flat_ids[:, :, None] == jnp.arange(expert_total, dtype=jnp.int32)[None, None, :]
    ).astype(jnp.int32)
    earlier = jnp.cumsum(onehot, axis=1) - onehot
    position = jnp.sum(earlier * onehot, axis=2)
    slot_index = flat_ids * capacity + position
    slot_ids = jnp.arange(expert_total * capacity, dtype=jnp.int32)
    return (slot_index[:, None, :] == slot_ids[None, :, None]).astype(jnp.float32)


def ring_gather_kernel(x_ref, after_ref, out_ref, send_sems, recv_sems, local_sem):
    del after_ref
    count = lax.axis_size("pipe")
    me = lax.axis_index("pipe")
    rest = tuple(lax.axis_index(name) for name in TOKEN_AXES[1:])
    right = lax.rem(me + 1, count)
    left = lax.rem(me + count - 1, count)
    barrier = pltpu.get_barrier_semaphore()
    for peer in (left, right):
        pl.semaphore_signal(
            barrier, inc=1, device_id=(peer,) + rest, device_id_type=pl.DeviceIdType.MESH
        )
    pl.semaphore_wait(barrier, 2)
    own = pltpu.make_async_copy(x_ref, out_ref.at[me], local_sem)
    own.start()
    plans = ((right, count // 2, lambda s: lax.rem(me - s + count, count)),
             (left, (count - 1) // 2, lambda s: lax.rem(me + s, count)))
    started = []

    def transfer(direction, step):
        peer, _, slab_of = plans[direction]
        slab = slab_of(step)
        return pltpu.make_async_remote_copy(
            src_ref=x_ref if step == 0 else out_ref.at[slab],
            dst_ref=out_ref.at[slab],
            send_sem=send_sems.at[direction, step],
            recv_sem=recv_sems.at[direction, step],
            device_id=(peer,) + rest,
            device_id_type=pl.DeviceIdType.MESH,
        )

    def arrival(direction, step):
        peer, _, slab_of = plans[direction]
        source = left if peer is right else right
        slab = lax.rem(slab_of(step + 1), count)
        return pltpu.make_async_remote_copy(
            src_ref=out_ref.at[slab],
            dst_ref=out_ref.at[slab],
            send_sem=send_sems.at[direction, step],
            recv_sem=recv_sems.at[direction, step],
            device_id=(source,) + rest,
            device_id_type=pl.DeviceIdType.MESH,
        )

    for step in range(count // 2):
        for direction in (0, 1):
            if step >= plans[direction][1]:
                continue
            if step > 0:
                arrival(direction, step - 1).wait_recv()
            copy = transfer(direction, step)
            copy.start()
            started.append(copy)
    for direction in (0, 1):
        arrival(direction, plans[direction][1] - 1).wait_recv()
    for copy in started:
        copy.wait_send()
    own.wait()


def ring_gather(x, after):
    count = lax.axis_size("pipe")
    steps = count // 2
    return pl.pallas_call(
        ring_gather_kernel,
        out_shape=jax.ShapeDtypeStruct((count,) + x.shape, x.dtype),
        in_specs=[pl.BlockSpec(memory_space=pl.ANY)] * 2,
        out_specs=pl.BlockSpec(memory_space=pl.ANY),
        scratch_shapes=[
            pltpu.SemaphoreType.DMA((2, steps)),
            pltpu.SemaphoreType.DMA((2, steps)),
            pltpu.SemaphoreType.DMA,
        ],
        compiler_params=pltpu.CompilerParams(collective_id=0, has_side_effects=True),
    )(x, after)


def ring_sum_kernel(part_ref, after_ref, out_ref, landing, outgoing, send_sems, recv_sems):
    del after_ref
    count = lax.axis_size("pipe")
    me = lax.axis_index("pipe")
    rest = tuple(lax.axis_index(name) for name in TOKEN_AXES[1:])
    right = lax.rem(me + 1, count)
    left = lax.rem(me + count - 1, count)
    lanes_count = landing.shape[0]
    piece = part_ref.shape[1] // lanes_count
    barrier = pltpu.get_barrier_semaphore()
    for peer in (left, right):
        pl.semaphore_signal(
            barrier, inc=1, device_id=(peer,) + rest, device_id_type=pl.DeviceIdType.MESH
        )
    pl.semaphore_wait(barrier, 2)
    rows = [pl.ds(k * piece, piece) for k in range(lanes_count)]

    def goes_right(k):
        return k % 2 == 0

    def chunk_at(k, step):
        if goes_right(k):
            return lax.rem(me - step - 1 + 2 * count, count)
        return lax.rem(me + step + 1, count)

    def copy(k, step, peer):
        return pltpu.make_async_remote_copy(
            src_ref=outgoing.at[k, step],
            dst_ref=landing.at[k, step],
            send_sem=send_sems.at[k, step],
            recv_sem=recv_sems.at[k, step],
            device_id=(peer,) + rest,
            device_id_type=pl.DeviceIdType.MESH,
        )

    def sender(k):
        return right if goes_right(k) else left

    def source(k):
        return left if goes_right(k) else right

    started = []
    for step in range(count - 1):
        for k in range(lanes_count):
            own = part_ref[chunk_at(k, step), rows[k], :].astype(jnp.float32)
            if step > 0:
                copy(k, step - 1, source(k)).wait_recv()
                own = own + landing[k, step - 1].astype(jnp.float32)
            outgoing[k, step] = own.astype(outgoing.dtype)
            sending = copy(k, step, sender(k))
            sending.start()
            started.append(sending)
    for k in range(lanes_count):
        copy(k, count - 2, source(k)).wait_recv()
        total = part_ref[me, rows[k], :].astype(jnp.float32)
        total = total + landing[k, count - 2].astype(jnp.float32)
        out_ref[rows[k], :] = total.astype(out_ref.dtype)
    for sending in started:
        sending.wait_send()


def ring_sum(parts, after):
    count = lax.axis_size("pipe")
    rows = parts.shape[0] // count
    parts = parts.reshape(count, rows, parts.shape[1])
    pieces = 14
    slot = (pieces, count - 1, rows // pieces, parts.shape[2])
    return pl.pallas_call(
        ring_sum_kernel,
        out_shape=jax.ShapeDtypeStruct((rows, parts.shape[2]), parts.dtype),
        in_specs=[
            pl.BlockSpec(memory_space=pltpu.VMEM),
            pl.BlockSpec(memory_space=pl.ANY),
        ],
        out_specs=pl.BlockSpec(memory_space=pltpu.VMEM),
        scratch_shapes=[
            pltpu.VMEM(slot, parts.dtype),
            pltpu.VMEM(slot, parts.dtype),
            pltpu.SemaphoreType.DMA(slot[:2]),
            pltpu.SemaphoreType.DMA(slot[:2]),
        ],
        compiler_params=pltpu.CompilerParams(collective_id=1, has_side_effects=True),
    )(parts, after)


def pair_sum_kernel(x_ref, out_ref, landing, mine, send_sems, recv_sems, local_sems):
    me = lax.axis_index("core")
    other = 1 - me
    head = tuple(lax.axis_index(name) for name in TOKEN_AXES[:3])
    partner = head + (other,)
    barrier = pltpu.get_barrier_semaphore()
    pl.semaphore_signal(
        barrier, inc=1, device_id=partner, device_id_type=pl.DeviceIdType.MESH
    )
    pl.semaphore_wait(barrier, 1)
    half = x_ref.shape[1] // 2
    parts = (pl.ds(0, half), pl.ds(half, half))
    sends, owns = [], []
    for k in range(2):
        sending = pltpu.make_async_remote_copy(
            src_ref=x_ref.at[other, parts[k]],
            dst_ref=landing.at[parts[k]],
            send_sem=send_sems.at[k],
            recv_sem=recv_sems.at[k],
            device_id=partner,
            device_id_type=pl.DeviceIdType.MESH,
        )
        sending.start()
        sends.append(sending)
        own = pltpu.make_async_copy(x_ref.at[me, parts[k]], mine.at[parts[k]], local_sems.at[k])
        own.start()
        owns.append(own)
    for k in range(2):
        owns[k].wait()
        sends[k].wait_recv()
        total = mine[parts[k], :].astype(jnp.float32) + landing[parts[k], :].astype(jnp.float32)
        out_ref[parts[k], :] = total.astype(out_ref.dtype)
    for sending in sends:
        sending.wait_send()


def pair_sum(x):
    return pl.pallas_call(
        pair_sum_kernel,
        out_shape=jax.ShapeDtypeStruct(x.shape[1:], x.dtype),
        in_specs=[pl.BlockSpec(memory_space=pl.ANY)],
        out_specs=pl.BlockSpec(memory_space=pltpu.VMEM),
        scratch_shapes=[
            pltpu.VMEM(x.shape[1:], x.dtype),
            pltpu.VMEM(x.shape[1:], x.dtype),
            pltpu.SemaphoreType.DMA((2,)),
            pltpu.SemaphoreType.DMA((2,)),
            pltpu.SemaphoreType.DMA((2,)),
        ],
        compiler_params=pltpu.CompilerParams(collective_id=2, has_side_effects=True),
    )(x)


def on_device(tokens, cotangent, expert_ids, gate_values, w_gate, w_up, w_down_t):
    micro_count, tok_count, d_model = tokens.shape
    top_count = expert_ids.shape[2]
    pipe_size = lax.axis_size("pipe")
    expert_size = lax.axis_size("ex") * lax.axis_size("ey") * lax.axis_size("core")
    capacity = CAP
    slot_total = EXPERTS * capacity
    highest_precision = lax.Precision.HIGHEST
    cols = w_gate.shape[1]
    routing_table = route_table(expert_ids, EXPERTS, capacity)
    routing_table_bfloat16 = routing_table.astype(jnp.bfloat16)
    lanes = 128
    flattened_gate = gate_values.reshape(micro_count, tok_count * top_count)
    token_table = jnp.sum(
        routing_table.reshape(micro_count, slot_total, tok_count, top_count), axis=3
    )
    rows_sent = jnp.einsum(
        "mst,mtd->msd",
        token_table.astype(jnp.bfloat16),
        jnp.concatenate([tokens, cotangent], axis=2),
        preferred_element_type=jnp.float32,
    ).astype(jnp.bfloat16)
    gate_sent = jnp.einsum(
        "msr,mr->ms", routing_table_bfloat16, flattened_gate, preferred_element_type=jnp.float32
    ).astype(jnp.bfloat16)
    send = jnp.concatenate(
        [rows_sent, jnp.broadcast_to(gate_sent[:, :, None], gate_sent.shape + (lanes,))], axis=2
    )
    width = send.shape[2]
    block_rows = micro_count * capacity
    send = jnp.transpose(send.reshape(micro_count, EXPERTS, capacity, width), (1, 0, 2, 3))
    send = send.reshape(EXPERTS * block_rows, width)
    arrived = lax.all_to_all(send, "ex", split_axis=0, concat_axis=0, tiled=True)
    rows_all = lax.all_gather(arrived, SHARE, axis=0, tiled=True)
    w_local = jnp.concatenate([w_gate, w_up, w_down_t], axis=1)
    w_full = ring_gather(w_local, arrived).reshape(-1, w_local.shape[1])
    gate_full = w_full[:, :cols]
    up_full = w_full[:, cols : 2 * cols]
    down_full = w_full[:, 2 * cols :]
    row_count = rows_all.shape[0]
    share_count = row_count // arrived.shape[0]
    tok_rows = rows_all[:, :d_model]
    cot_rows = rows_all[:, d_model : 2 * d_model]
    gate_rows = rows_all[:, 2 * d_model : 2 * d_model + 1].astype(jnp.float32)
    pre_gate = jnp.dot(tok_rows, gate_full, preferred_element_type=jnp.float32)
    pre_up = jnp.dot(tok_rows, up_full, preferred_element_type=jnp.float32)
    back_proj = jnp.dot(cot_rows, down_full, preferred_element_type=jnp.float32)
    sigmoid_gate = jax.nn.sigmoid(pre_gate)
    activated = pre_gate * sigmoid_gate
    hidden = activated * pre_up
    gate_part = jnp.sum(back_proj * hidden, axis=1)
    scaled_hidden = (gate_rows * hidden).astype(jnp.bfloat16)
    d_hidden = gate_rows * back_proj
    d_pre_gate = (
        d_hidden * pre_up * sigmoid_gate * (1.0 + pre_gate * (1.0 - sigmoid_gate))
    ).astype(jnp.bfloat16)
    d_pre_up = (d_hidden * activated).astype(jnp.bfloat16)
    core_count = lax.axis_size("core")

    def core_major(rows):
        blocks = rows.reshape(row_count // (core_count * arrived.shape[0]), core_count, -1)
        return jnp.swapaxes(blocks, 0, 1).reshape(rows.shape)

    input_part = jnp.dot(core_major(d_pre_gate), gate_full.T, preferred_element_type=jnp.float32)
    input_part = input_part + jnp.dot(
        core_major(d_pre_up), up_full.T, preferred_element_type=jnp.float32
    )
    tokens_total = tok_count * pipe_size * expert_size
    grad_scale = 1.0 / math.sqrt(micro_count * tokens_total * top_count / EXPERTS)
    contract = (((0,), (0,)), ((), ()))
    part_gate = lax.dot_general(tok_rows, d_pre_gate, contract, preferred_element_type=jnp.float32)
    part_up = lax.dot_general(tok_rows, d_pre_up, contract, preferred_element_type=jnp.float32)
    part_down = lax.dot_general(
        cot_rows, scaled_hidden, contract, preferred_element_type=jnp.float32
    )
    me_share = lax.axis_index("ey") * lax.axis_size("core") + lax.axis_index("core")
    gate_high = gate_part.astype(jnp.bfloat16)
    gate_low = (gate_part - gate_high.astype(jnp.float32)).astype(jnp.bfloat16)
    lane = lax.broadcasted_iota(jnp.int32, (1, lanes), 1)
    gate_columns = jnp.where(lane == 2 * me_share, gate_high[:, None], 0).astype(jnp.bfloat16)
    gate_columns = jnp.where(lane == 2 * me_share + 1, gate_low[:, None], gate_columns)
    input_shares = jnp.concatenate(
        [input_part.astype(jnp.bfloat16), core_major(gate_columns)], axis=1
    )
    input_pair = pair_sum(input_shares.reshape(core_count, row_count // core_count, -1))
    input_mine = lax.psum_scatter(input_pair, "ey", scatter_dimension=0, tiled=True)
    summed = ring_sum(
        (jnp.concatenate([part_gate, part_up, part_down], 1) * grad_scale).astype(jnp.bfloat16),
        input_pair,
    ).astype(jnp.float32)
    hidden_width = gate_full.shape[1]
    dw_gate = summed[:, :hidden_width].astype(jnp.bfloat16)
    dw_up = summed[:, hidden_width : 2 * hidden_width].astype(jnp.bfloat16)
    dw_down_t = summed[:, 2 * hidden_width :].astype(jnp.bfloat16)
    back = lax.all_to_all(input_mine, "ex", 0, 0, tiled=True)
    back = jnp.transpose(back.reshape(EXPERTS, micro_count, capacity, back.shape[1]), (1, 0, 2, 3))
    back = back.reshape(micro_count, slot_total, back.shape[3])
    slot_input = back[:, :, :d_model].astype(jnp.float32)
    gate_split = back[:, :, d_model : d_model + 2 * share_count].astype(jnp.float32)
    gate_per_slot = jnp.sum(gate_split, axis=2)
    d_tokens = jnp.einsum(
        "msc,msd->mcd", token_table, slot_input, precision=highest_precision
    ).astype(jnp.bfloat16)
    gate_weight_gradient = jnp.einsum(
        "kxw,kx->kw", routing_table, gate_per_slot, precision=highest_precision
    ).reshape(micro_count, tok_count, top_count)
    return (d_tokens, gate_weight_gradient, dw_gate, dw_up, dw_down_t)


def solution(mesh):
    pipe_size, expert_size = mesh.devices.shape
    split = Mesh(
        np.asarray(mesh.devices).reshape(pipe_size, EXPERTS, expert_size // EXPERTS // 2, 2),
        TOKEN_AXES,
    )
    token_spec = P(None, TOKEN_AXES, None)
    weight_spec = P("pipe", ("ex", "ey", "core"))
    return jax.shard_map(
        on_device,
        mesh=split,
        in_specs=(token_spec,) * 4 + (weight_spec,) * 3,
        out_specs=(token_spec, token_spec) + (weight_spec,) * 3,
        check_vma=False,
    )
```

```python
import math

import jax
import jax.numpy as jnp
import numpy as np
from jax import lax
from jax.experimental import pallas as pl
from jax.experimental.pallas import tpu as pltpu
from jax.sharding import Mesh
from jax.sharding import PartitionSpec as P

EXPERTS = 4
CAP = 3
SHARE = ("ey", "core")
TOKEN_AXES = ("pipe", "ex", "ey", "core")


def route_table(expert_ids, expert_total, capacity):
    micro_count, tok_count, top_count = expert_ids.shape
    flat_ids = expert_ids.reshape(micro_count, tok_count * top_count)
    onehot = (
        flat_ids[:, :, None] == jnp.arange(expert_total, dtype=jnp.int32)[None, None, :]
    ).astype(jnp.int32)
    earlier = jnp.cumsum(onehot, axis=1) - onehot
    position = jnp.sum(earlier * onehot, axis=2)
    slot_index = flat_ids * capacity + position
    slot_ids = jnp.arange(expert_total * capacity, dtype=jnp.int32)
    return (slot_index[:, None, :] == slot_ids[None, :, None]).astype(jnp.float32)


def ring_gather_kernel(x_ref, after_ref, out_ref, send_sems, recv_sems, local_sem):
    del after_ref
    count = lax.axis_size("pipe")
    me = lax.axis_index("pipe")
    rest = tuple(lax.axis_index(name) for name in TOKEN_AXES[1:])
    right = lax.rem(me + 1, count)
    left = lax.rem(me + count - 1, count)
    barrier = pltpu.get_barrier_semaphore()
    for peer in (left, right):
        pl.semaphore_signal(
            barrier, inc=1, device_id=(peer,) + rest, device_id_type=pl.DeviceIdType.MESH
        )
    pl.semaphore_wait(barrier, 2)
    own = pltpu.make_async_copy(x_ref, out_ref.at[me], local_sem)
    own.start()
    plans = ((right, count // 2, lambda s: lax.rem(me - s + count, count)),
             (left, (count - 1) // 2, lambda s: lax.rem(me + s, count)))
    started = []

    def transfer(direction, step):
        peer, _, slab_of = plans[direction]
        slab = slab_of(step)
        return pltpu.make_async_remote_copy(
            src_ref=x_ref if step == 0 else out_ref.at[slab],
            dst_ref=out_ref.at[slab],
            send_sem=send_sems.at[direction, step],
            recv_sem=recv_sems.at[direction, step],
            device_id=(peer,) + rest,
            device_id_type=pl.DeviceIdType.MESH,
        )

    def arrival(direction, step):
        peer, _, slab_of = plans[direction]
        source = left if peer is right else right
        slab = lax.rem(slab_of(step + 1), count)
        return pltpu.make_async_remote_copy(
            src_ref=out_ref.at[slab],
            dst_ref=out_ref.at[slab],
            send_sem=send_sems.at[direction, step],
            recv_sem=recv_sems.at[direction, step],
            device_id=(source,) + rest,
            device_id_type=pl.DeviceIdType.MESH,
        )

    for step in range(count // 2):
        for direction in (0, 1):
            if step >= plans[direction][1]:
                continue
            if step > 0:
                arrival(direction, step - 1).wait_recv()
            copy = transfer(direction, step)
            copy.start()
            started.append(copy)
    for direction in (0, 1):
        arrival(direction, plans[direction][1] - 1).wait_recv()
    for copy in started:
        copy.wait_send()
    own.wait()


def ring_gather(x, after):
    count = lax.axis_size("pipe")
    steps = count // 2
    return pl.pallas_call(
        ring_gather_kernel,
        out_shape=jax.ShapeDtypeStruct((count,) + x.shape, x.dtype),
        in_specs=[pl.BlockSpec(memory_space=pl.ANY)] * 2,
        out_specs=pl.BlockSpec(memory_space=pl.ANY),
        scratch_shapes=[
            pltpu.SemaphoreType.DMA((2, steps)),
            pltpu.SemaphoreType.DMA((2, steps)),
            pltpu.SemaphoreType.DMA,
        ],
        compiler_params=pltpu.CompilerParams(collective_id=0, has_side_effects=True),
    )(x, after)


def ring_sum_kernel(part_ref, after_ref, out_ref, landing, outgoing, send_sems, recv_sems):
    del after_ref
    count = lax.axis_size("pipe")
    me = lax.axis_index("pipe")
    rest = tuple(lax.axis_index(name) for name in TOKEN_AXES[1:])
    right = lax.rem(me + 1, count)
    left = lax.rem(me + count - 1, count)
    lanes_count = landing.shape[0]
    piece = part_ref.shape[1] // lanes_count
    barrier = pltpu.get_barrier_semaphore()
    for peer in (left, right):
        pl.semaphore_signal(
            barrier, inc=1, device_id=(peer,) + rest, device_id_type=pl.DeviceIdType.MESH
        )
    pl.semaphore_wait(barrier, 2)
    rows = [pl.ds(k * piece, piece) for k in range(lanes_count)]

    def goes_right(k):
        return k % 2 == 0

    def chunk_at(k, step):
        if goes_right(k):
            return lax.rem(me - step - 1 + 2 * count, count)
        return lax.rem(me + step + 1, count)

    def copy(k, step, peer):
        return pltpu.make_async_remote_copy(
            src_ref=outgoing.at[k, step],
            dst_ref=landing.at[k, step],
            send_sem=send_sems.at[k, step],
            recv_sem=recv_sems.at[k, step],
            device_id=(peer,) + rest,
            device_id_type=pl.DeviceIdType.MESH,
        )

    def sender(k):
        return right if goes_right(k) else left

    def source(k):
        return left if goes_right(k) else right

    started = []
    for step in range(count - 1):
        for k in range(lanes_count):
            own = part_ref[chunk_at(k, step), rows[k], :].astype(jnp.float32)
            if step > 0:
                copy(k, step - 1, source(k)).wait_recv()
                own = own + landing[k, step - 1].astype(jnp.float32)
            outgoing[k, step] = own.astype(outgoing.dtype)
            sending = copy(k, step, sender(k))
            sending.start()
            started.append(sending)
    for k in range(lanes_count):
        copy(k, count - 2, source(k)).wait_recv()
        total = part_ref[me, rows[k], :].astype(jnp.float32)
        total = total + landing[k, count - 2].astype(jnp.float32)
        out_ref[rows[k], :] = total.astype(out_ref.dtype)
    for sending in started:
        sending.wait_send()


def ring_sum(parts, after):
    count = lax.axis_size("pipe")
    rows = parts.shape[0] // count
    parts = parts.reshape(count, rows, parts.shape[1])
    pieces = 14
    slot = (pieces, count - 1, rows // pieces, parts.shape[2])
    return pl.pallas_call(
        ring_sum_kernel,
        out_shape=jax.ShapeDtypeStruct((rows, parts.shape[2]), parts.dtype),
        in_specs=[
            pl.BlockSpec(memory_space=pltpu.VMEM),
            pl.BlockSpec(memory_space=pl.ANY),
        ],
        out_specs=pl.BlockSpec(memory_space=pltpu.VMEM),
        scratch_shapes=[
            pltpu.VMEM(slot, parts.dtype),
            pltpu.VMEM(slot, parts.dtype),
            pltpu.SemaphoreType.DMA(slot[:2]),
            pltpu.SemaphoreType.DMA(slot[:2]),
        ],
        compiler_params=pltpu.CompilerParams(collective_id=1, has_side_effects=True),
    )(parts, after)


def pair_sum_kernel(x_ref, out_ref, landing, mine, send_sems, recv_sems, local_sems):
    me = lax.axis_index("core")
    other = 1 - me
    head = tuple(lax.axis_index(name) for name in TOKEN_AXES[:3])
    partner = head + (other,)
    barrier = pltpu.get_barrier_semaphore()
    pl.semaphore_signal(
        barrier, inc=1, device_id=partner, device_id_type=pl.DeviceIdType.MESH
    )
    pl.semaphore_wait(barrier, 1)
    half = x_ref.shape[1] // 2
    parts = (pl.ds(0, half), pl.ds(half, half))
    sends, owns = [], []
    for k in range(2):
        sending = pltpu.make_async_remote_copy(
            src_ref=x_ref.at[other, parts[k]],
            dst_ref=landing.at[parts[k]],
            send_sem=send_sems.at[k],
            recv_sem=recv_sems.at[k],
            device_id=partner,
            device_id_type=pl.DeviceIdType.MESH,
        )
        sending.start()
        sends.append(sending)
        own = pltpu.make_async_copy(x_ref.at[me, parts[k]], mine.at[parts[k]], local_sems.at[k])
        own.start()
        owns.append(own)
    for k in range(2):
        owns[k].wait()
        sends[k].wait_recv()
        total = mine[parts[k], :].astype(jnp.float32) + landing[parts[k], :].astype(jnp.float32)
        out_ref[parts[k], :] = total.astype(out_ref.dtype)
    for sending in sends:
        sending.wait_send()


def pair_sum(x):
    return pl.pallas_call(
        pair_sum_kernel,
        out_shape=jax.ShapeDtypeStruct(x.shape[1:], x.dtype),
        in_specs=[pl.BlockSpec(memory_space=pl.ANY)],
        out_specs=pl.BlockSpec(memory_space=pltpu.VMEM),
        scratch_shapes=[
            pltpu.VMEM(x.shape[1:], x.dtype),
            pltpu.VMEM(x.shape[1:], x.dtype),
            pltpu.SemaphoreType.DMA((2,)),
            pltpu.SemaphoreType.DMA((2,)),
            pltpu.SemaphoreType.DMA((2,)),
        ],
        compiler_params=pltpu.CompilerParams(collective_id=2, has_side_effects=True),
    )(x)


def exchange_kernel(x_ref, out_ref, send_sems, recv_sems, local_sem):
    count = lax.axis_size("ex")
    me = lax.axis_index("ex")
    pipe = lax.axis_index("pipe")
    rest = tuple(lax.axis_index(name) for name in TOKEN_AXES[2:])

    def device(peer):
        return (pipe, peer) + rest

    barrier = pltpu.get_barrier_semaphore()
    for shift in range(1, count):
        pl.semaphore_signal(
            barrier,
            inc=1,
            device_id=device(lax.rem(me + shift, count)),
            device_id_type=pl.DeviceIdType.MESH,
        )
    pl.semaphore_wait(barrier, count - 1)
    own = pltpu.make_async_copy(x_ref.at[me], out_ref.at[me], local_sem)
    own.start()
    started = []
    for shift in range(1, count):
        peer = lax.rem(me + shift, count)
        sending = pltpu.make_async_remote_copy(
            src_ref=x_ref.at[peer],
            dst_ref=out_ref.at[me],
            send_sem=send_sems.at[peer],
            recv_sem=recv_sems.at[me],
            device_id=device(peer),
            device_id_type=pl.DeviceIdType.MESH,
        )
        sending.start()
        started.append(sending)
    for shift in range(1, count):
        source = lax.rem(me + count - shift, count)
        pltpu.make_async_remote_copy(
            src_ref=x_ref.at[source],
            dst_ref=out_ref.at[source],
            send_sem=send_sems.at[source],
            recv_sem=recv_sems.at[source],
            device_id=device(source),
            device_id_type=pl.DeviceIdType.MESH,
        ).wait_recv()
    for sending in started:
        sending.wait_send()
    own.wait()


def exchange(x, collective):
    count = lax.axis_size("ex")
    return pl.pallas_call(
        exchange_kernel,
        out_shape=jax.ShapeDtypeStruct(x.shape, x.dtype),
        in_specs=[pl.BlockSpec(memory_space=pl.ANY)],
        out_specs=pl.BlockSpec(memory_space=pl.ANY),
        scratch_shapes=[
            pltpu.SemaphoreType.DMA((count,)),
            pltpu.SemaphoreType.DMA((count,)),
            pltpu.SemaphoreType.DMA,
        ],
        compiler_params=pltpu.CompilerParams(collective_id=collective, has_side_effects=True),
    )(x)


def on_device(tokens, cotangent, expert_ids, gate_values, w_gate, w_up, w_down_t):
    micro_count, tok_count, d_model = tokens.shape
    top_count = expert_ids.shape[2]
    pipe_size = lax.axis_size("pipe")
    expert_size = lax.axis_size("ex") * lax.axis_size("ey") * lax.axis_size("core")
    capacity = CAP
    slot_total = EXPERTS * capacity
    highest_precision = lax.Precision.HIGHEST
    cols = w_gate.shape[1]
    routing_table = route_table(expert_ids, EXPERTS, capacity)
    routing_table_bfloat16 = routing_table.astype(jnp.bfloat16)
    lanes = 128
    flattened_gate = gate_values.reshape(micro_count, tok_count * top_count)
    token_table = jnp.sum(
        routing_table.reshape(micro_count, slot_total, tok_count, top_count), axis=3
    )
    rows_sent = jnp.einsum(
        "mst,mtd->msd",
        token_table.astype(jnp.bfloat16),
        jnp.concatenate([tokens, cotangent], axis=2),
        preferred_element_type=jnp.float32,
    ).astype(jnp.bfloat16)
    gate_sent = jnp.einsum(
        "msr,mr->ms", routing_table_bfloat16, flattened_gate, preferred_element_type=jnp.float32
    ).astype(jnp.bfloat16)
    send = jnp.concatenate(
        [rows_sent, jnp.broadcast_to(gate_sent[:, :, None], gate_sent.shape + (lanes,))], axis=2
    )
    width = send.shape[2]
    block_rows = micro_count * capacity
    send = jnp.transpose(send.reshape(micro_count, EXPERTS, capacity, width), (1, 0, 2, 3))
    send = send.reshape(EXPERTS * block_rows, width)
    arrived = lax.all_to_all(send, "ex", split_axis=0, concat_axis=0, tiled=True)
    rows_all = lax.all_gather(arrived, SHARE, axis=0, tiled=True)
    w_local = jnp.concatenate([w_gate, w_up, w_down_t], axis=1)
    w_full = ring_gather(w_local, arrived).reshape(-1, w_local.shape[1])
    gate_full = w_full[:, :cols]
    up_full = w_full[:, cols : 2 * cols]
    down_full = w_full[:, 2 * cols :]
    row_count = rows_all.shape[0]
    share_count = row_count // arrived.shape[0]
    tok_rows = rows_all[:, :d_model]
    cot_rows = rows_all[:, d_model : 2 * d_model]
    gate_rows = rows_all[:, 2 * d_model : 2 * d_model + 1].astype(jnp.float32)
    pre_gate = jnp.dot(tok_rows, gate_full, preferred_element_type=jnp.float32)
    pre_up = jnp.dot(tok_rows, up_full, preferred_element_type=jnp.float32)
    back_proj = jnp.dot(cot_rows, down_full, preferred_element_type=jnp.float32)
    sigmoid_gate = jax.nn.sigmoid(pre_gate)
    activated = pre_gate * sigmoid_gate
    hidden = activated * pre_up
    gate_part = jnp.sum(back_proj * hidden, axis=1)
    scaled_hidden = (gate_rows * hidden).astype(jnp.bfloat16)
    d_hidden = gate_rows * back_proj
    d_pre_gate = (
        d_hidden * pre_up * sigmoid_gate * (1.0 + pre_gate * (1.0 - sigmoid_gate))
    ).astype(jnp.bfloat16)
    d_pre_up = (d_hidden * activated).astype(jnp.bfloat16)
    core_count = lax.axis_size("core")

    def core_major(rows):
        blocks = rows.reshape(row_count // (core_count * arrived.shape[0]), core_count, -1)
        return jnp.swapaxes(blocks, 0, 1).reshape(rows.shape)

    input_part = jnp.dot(core_major(d_pre_gate), gate_full.T, preferred_element_type=jnp.float32)
    input_part = input_part + jnp.dot(
        core_major(d_pre_up), up_full.T, preferred_element_type=jnp.float32
    )
    tokens_total = tok_count * pipe_size * expert_size
    grad_scale = 1.0 / math.sqrt(micro_count * tokens_total * top_count / EXPERTS)
    contract = (((0,), (0,)), ((), ()))
    part_gate = lax.dot_general(tok_rows, d_pre_gate, contract, preferred_element_type=jnp.float32)
    part_up = lax.dot_general(tok_rows, d_pre_up, contract, preferred_element_type=jnp.float32)
    part_down = lax.dot_general(
        cot_rows, scaled_hidden, contract, preferred_element_type=jnp.float32
    )
    me_share = lax.axis_index("ey") * lax.axis_size("core") + lax.axis_index("core")
    gate_high = gate_part.astype(jnp.bfloat16)
    gate_low = (gate_part - gate_high.astype(jnp.float32)).astype(jnp.bfloat16)
    lane = lax.broadcasted_iota(jnp.int32, (1, lanes), 1)
    gate_columns = jnp.where(lane == 2 * me_share, gate_high[:, None], 0).astype(jnp.bfloat16)
    gate_columns = jnp.where(lane == 2 * me_share + 1, gate_low[:, None], gate_columns)
    input_shares = jnp.concatenate(
        [input_part.astype(jnp.bfloat16), core_major(gate_columns)], axis=1
    )
    input_pair = pair_sum(input_shares.reshape(core_count, row_count // core_count, -1))
    input_mine = lax.psum_scatter(input_pair, "ey", scatter_dimension=0, tiled=True)
    summed = ring_sum(
        (jnp.concatenate([part_gate, part_up, part_down], 1) * grad_scale).astype(jnp.bfloat16),
        input_pair,
    ).astype(jnp.float32)
    hidden_width = gate_full.shape[1]
    dw_gate = summed[:, :hidden_width].astype(jnp.bfloat16)
    dw_up = summed[:, hidden_width : 2 * hidden_width].astype(jnp.bfloat16)
    dw_down_t = summed[:, 2 * hidden_width :].astype(jnp.bfloat16)
    back = exchange(input_mine.reshape(EXPERTS, block_rows, input_mine.shape[1]), 3)
    back = jnp.transpose(back.reshape(EXPERTS, micro_count, capacity, back.shape[2]), (1, 0, 2, 3))
    back = back.reshape(micro_count, slot_total, back.shape[3])
    slot_input = back[:, :, :d_model].astype(jnp.float32)
    gate_split = back[:, :, d_model : d_model + 2 * share_count].astype(jnp.float32)
    gate_per_slot = jnp.sum(gate_split, axis=2)
    d_tokens = jnp.einsum(
        "msc,msd->mcd", token_table, slot_input, precision=highest_precision
    ).astype(jnp.bfloat16)
    gate_weight_gradient = jnp.einsum(
        "kxw,kx->kw", routing_table, gate_per_slot, precision=highest_precision
    ).reshape(micro_count, tok_count, top_count)
    return (d_tokens, gate_weight_gradient, dw_gate, dw_up, dw_down_t)


def solution(mesh):
    pipe_size, expert_size = mesh.devices.shape
    split = Mesh(
        np.asarray(mesh.devices).reshape(pipe_size, EXPERTS, expert_size // EXPERTS // 2, 2),
        TOKEN_AXES,
    )
    token_spec = P(None, TOKEN_AXES, None)
    weight_spec = P("pipe", ("ex", "ey", "core"))
    return jax.shard_map(
        on_device,
        mesh=split,
        in_specs=(token_spec,) * 4 + (weight_spec,) * 3,
        out_specs=(token_spec, token_spec) + (weight_spec,) * 3,
        check_vma=False,
    )
```
